512 devices in a mesh: section: 2 (over x_lo), dom: 32 (over z, core), slab: 8 (over x_hi, y).
Axes of the slice: x: 4 (x_hi: 2, x_lo: 2; x = x_hi * 2 + x_lo), y: 4, z: 16, core: 2. Of those that a mesh axis runs over, the one named last changes fastest.
Arguments:
- residual: float32 [8, 1048576], P(None, ('section', 'dom', 'slab')), may hold values from -6 to 6
- coupling_tiles: float32 [8, 128, 128], replicated, may hold values from -0.1875 to 0.1875
- inverse_tiles: float32 [8, 128, 128], replicated, may hold values from -0.5 to 0.5
- diag_kind: int32 [8192], P(('section', 'dom', 'slab')), may hold values from 0 to 7
- diag_coeff: float32 [8192], P(('section', 'dom', 'slab')), may hold values from 0.5 to 4
- tile_cols: int32 [8, 8192], P(None, ('section', 'dom', 'slab')), may hold values from 0 to 19, as said below
- tile_kinds: int32 [8, 8192], P(None, ('section', 'dom', 'slab')), may hold values from 0 to 7
- tile_coeff: float32 [8, 8192], P(None, ('section', 'dom', 'slab')), may hold values from 0.25 to 2
- halo_rows: int32 [1024], P(('section', 'dom', 'slab')), may hold values from 0 to 15, as said below
- tile_owner: int32 [8192, 1], P(('section', 'dom', 'slab')), may hold values from 0 to 63; in each aligned block of 16 rows (0 to 15, 16 to 31, ...) at most 2 rows name the same one
- node_slot: int32 [8192], P(('section', 'dom', 'slab')), may hold values from 0 to 1
- edge_nodes: int32 [2, 1048576], P(None, ('section', 'dom', 'slab')), may hold values from 0 to 127, as said below
- tangents: float32 [3, 1048576], P(None, ('section', 'dom', 'slab')), may hold values from -5 to 5
- grad_blocks: float32 [1024, 128, 128], P(('section', 'dom', 'slab')), may hold values from -0.09375 to 0.09375
- vec_blocks: float32 [1024, 128, 128], P(('section', 'dom', 'slab')), may hold values from -0.1875 to 0.1875
Outputs:
- preconditioned: float32 [8, 1048576], P(None, ('section', 'dom', 'slab'))
The draws below stay inside these ranges and needn't reach their ends.
Inputs may be any that keep to these rules, and one draw needn't show every extreme that they name: `tile_cols`: within each device's 16 tiles (local number t): row 0 names 16 + h and row 1 names 18 + h, each h < 2 named exactly 16 // 2 times in each of these rows; rows 2 to 7 name a local tile other than t. `halo_rows`: each device's 2 entries are distinct local tile numbers. `edge_nodes`: an edge's two ends differ. `tile_owner`: among the 16 tiles of one device no owner is named more than 2 times, and 2 is reached.
All inputs are finite; a program needn't handle non-finite values.
Results may differ from the reference program's by a relative error of at most 0.0001.
Values sent between devices are 32-bit elements; how exact they have to be, the bound alone decides.
No kernel may reach another device: no remote copies, remote signals or barrier semaphores. Data moves between devices by JAX's collectives and lax.ppermute only.
A program may use at most 64 MiB of HBM per device.

```python
import math
import jax
import jax.numpy as jnp
import numpy as np
from jax import lax

B = 128
K = 8
ET = 16
NB = 8
NK = 8
HT = 2
NT_DEV = 2
OWNERS = 64
CAP = 2
EDGE_TILES = 8192
EDGES = 1048576
HALO_TILES = 1024
NODE_TILES = 1024
N_SECTION = 2
N_DOM = 32
N_SLAB = 8


def draw_tile_cols(key, part):
    block_count = EDGE_TILES // ET
    local_index = jnp.arange(ET, dtype=jnp.int32)

    def one_block(block_key):
        from_lower = jax.random.permutation(jax.random.fold_in(block_key, 1), ET) % HT + ET
        from_upper = jax.random.permutation(jax.random.fold_in(block_key, 2), ET) % HT + ET + HT
        offsets = jax.random.randint(jax.random.fold_in(block_key, 3), (NB - 2, ET), 1, ET)
        others = (local_index[None, :] + offsets) % ET
        return jnp.concatenate([from_lower[None, :], from_upper[None, :], others], axis=0).astype(jnp.int32)
    block_keys = jax.random.split(jax.random.fold_in(key, 11), block_count)
    stacked = jax.vmap(one_block)(block_keys)
    return jnp.transpose(stacked, (1, 0, 2)).reshape(NB, EDGE_TILES).astype(jnp.int32)


def draw_halo_rows(key, part):
    block_count = HALO_TILES // HT

    def one_block(block_key):
        return jax.random.permutation(block_key, ET)[:HT]
    block_keys = jax.random.split(jax.random.fold_in(key, 21), block_count)
    return jax.vmap(one_block)(block_keys).reshape(HALO_TILES).astype(jnp.int32)


def draw_edge_nodes(key, part):
    first_end = jax.random.randint(jax.random.fold_in(key, 31), (EDGES,), 0, B)
    stride = jax.random.randint(jax.random.fold_in(key, 32), (EDGES,), 1, B)
    return jnp.stack([first_end, (first_end + stride) % B]).astype(jnp.int32)


def plant(result, key, smallest, high):
    shape = result.shape
    spot = [jax.random.randint(jax.random.fold_in(key, axis), (), 0, shape[axis]) for axis in range(len(shape))]
    result = result.at[tuple(spot)].set(smallest)
    longest = shape.index(max(shape))
    spot[longest] = (spot[longest] + 1) % shape[longest]
    return result.at[tuple(spot)].set(high)


def levels(own_key, shape, cuts, low, high):
    def one(dim, shards_of):
        steps = jax.random.uniform(jax.random.fold_in(jax.random.fold_in(own_key, 6), dim), (shards_of,), jnp.float32, low / len(cuts), high / len(cuts))
        return jnp.repeat(jnp.exp(steps), shape[dim] // shards_of).reshape((-1,) + (1,) * (len(shape) - dim - 1))

    level = one(*cuts[0])
    for cut in cuts[1:]:
        level = level * one(*cut)
    return level


def assign_block(rng, own, number, rows, amount, top, most, lean):
    ranking = jax.random.permutation(rng, amount)
    crowded, ordinary = portions_of(amount, rows * top, most, lean, True), portions_of(amount, rows * top, most, lean, False)
    places = jnp.arange(amount)

    def named(sizes, turn):
        used = int((sizes > 0).sum())
        fixed = max(1, used // 4)
        shifted = fixed + (places - fixed + turn * (used - fixed)) % max(1, amount - fixed)
        return jnp.zeros((amount,), jnp.int32).at[ranking[jnp.where(places < fixed, places, shifted)]].set(jnp.asarray(sizes, jnp.int32))

    sizes = jnp.where(number % 4 == 0, named(crowded, number // 4), named(ordinary, number - number // 4 - 1))
    mixed = jax.random.permutation(jax.random.fold_in(own, 3), amount)
    source_of, receiver = mixed[0:amount // 2 * 2:2], mixed[1:amount // 2 * 2:2]
    margin = jnp.minimum(sizes[source_of] - 1, most - sizes[receiver]) // 2
    margin = jnp.where((source_of == ranking[0]) | (receiver == ranking[0]) | (sizes[receiver] == 0), 0, jnp.maximum(margin, 0))
    shifted = jax.random.randint(jax.random.fold_in(own, 4), (amount // 2,), 0, 1 << 20) % (margin + 1)
    sizes = sizes.at[source_of].add(-shifted).at[receiver].add(shifted)
    items = jnp.searchsorted(jnp.cumsum(sizes), jnp.arange(rows * top), side="right").astype(jnp.int32)
    table = items.reshape(top, rows).T
    table = table[jax.random.permutation(jax.random.fold_in(own, 1), rows)]
    turn = jax.random.randint(jax.random.fold_in(own, 2), (rows, 1), 0, top)
    return jnp.take_along_axis(table, (jnp.arange(top)[None, :] + turn) % top, axis=1)


def portions_of(count, total, limit, skew, full):
    loads = [(1 << 20) // math.isqrt(standing ** skew) + 1 for standing in range(1, count + 1)]
    largest = limit if full else min(limit, max(-(-total // count), total * loads[0] // sum(loads)))
    least = 1 if total - largest >= count - 1 else 0
    holding, rest = [largest] + [least] * (count - 1), total - largest - least * (count - 1)
    while rest > 0:
        candidates = [i for i in range(1, count) if holding[i] < largest] or [i for i in range(1, count) if holding[i] < limit]
        pool, remaining = sum([loads[i] for i in candidates]), rest
        for i in candidates:
            addition = min(limit - holding[i], max(1, remaining * loads[i] // pool), rest)
            holding[i] = holding[i] + addition
            rest = rest - addition
    return np.array(holding)


def normal_values(key, dims, spread, limit, cuts=(), held_as=jnp.bfloat16):
    entries = jax.random.normal(key, dims, jnp.float32) * spread
    if len(cuts) > 0:
        entries = levels(key, dims, cuts, -0.22, 0.18) * entries
    return jnp.clip(entries, min=-limit, max=limit).astype(held_as)


def setup_inputs(seed: int = 0) -> dict:
    key_of = jax.random.split(jax.random.key(seed), 16)
    residual = normal_values(key_of[0], (K, EDGES), 1.0, 6.0, ((1, 512),), jnp.float32)
    coupling_tiles = normal_values(key_of[1], (NK, B, B), (B * (NB + 1)) ** -0.5, 0.1875, (), jnp.float32)
    inverse_tiles = normal_values(key_of[2], (NK, B, B), B ** -0.5, 0.5, (), jnp.float32)
    diag_kind = plant(jax.random.randint(key_of[3], (EDGE_TILES,), 0, NK), jax.random.fold_in(key_of[3], 1), 0, NK - 1).astype(jnp.int32)
    diag_coeff = jnp.clip(jnp.exp(math.log(4.0) - 2.0794415 * jax.random.uniform(key_of[4], (EDGE_TILES,), jnp.float32) ** levels(key_of[4], (EDGE_TILES,), ((0, 512),), -0.2, 0.2)), 0.5, 4.0)
    tile_cols = draw_tile_cols(jax.random.fold_in(key_of[15], 71), 0)
    tile_kinds = plant(jax.random.randint(key_of[6], (NB, EDGE_TILES), 0, NK), jax.random.fold_in(key_of[6], 1), 0, NK - 1).astype(jnp.int32)
    tile_coeff = jnp.clip(jnp.exp(math.log(2.0) - 2.0794415 * jax.random.uniform(key_of[7], (NB, EDGE_TILES), jnp.float32) ** levels(key_of[7], (NB, EDGE_TILES), ((1, 512),), -0.2, 0.2)), 0.25, 2.0)
    halo_rows = draw_halo_rows(jax.random.fold_in(key_of[15], 71), 0)
    tile_owner_keys = jax.random.split(jax.random.fold_in(key_of[9], 1), EDGE_TILES // ET)
    tile_owner_turns = jax.random.permutation(jax.random.fold_in(key_of[9], 3), EDGE_TILES // ET)
    tile_owner = jax.vmap(lambda own, number: assign_block(jax.random.fold_in(key_of[9], 2), own, number, ET, OWNERS, 1, CAP, 2))(tile_owner_keys, tile_owner_turns).reshape((EDGE_TILES, 1))
    node_slot = plant(jax.random.randint(key_of[10], (EDGE_TILES,), 0, NT_DEV), jax.random.fold_in(key_of[10], 1), 0, NT_DEV - 1).astype(jnp.int32)
    edge_nodes = draw_edge_nodes(jax.random.fold_in(key_of[15], 71), 0)
    tangents = normal_values(key_of[12], (3, EDGES), 1.0, 5.0, ((1, 512),), jnp.float32)
    grad_blocks = normal_values(key_of[13], (NODE_TILES, B, B), (32 * B) ** -0.5, 0.09375, ((0, 512),), jnp.float32)
    vec_blocks = normal_values(key_of[14], (NODE_TILES, B, B), (8 * B) ** -0.5, 0.1875, ((0, 512),), jnp.float32)
    return {"residual": residual, "coupling_tiles": coupling_tiles, "inverse_tiles": inverse_tiles, "diag_kind": diag_kind, "diag_coeff": diag_coeff, "tile_cols": tile_cols, "tile_kinds": tile_kinds, "tile_coeff": tile_coeff, "halo_rows": halo_rows, "tile_owner": tile_owner, "node_slot": node_slot, "edge_nodes": edge_nodes, "tangents": tangents, "grad_blocks": grad_blocks, "vec_blocks": vec_blocks}


HIGHEST = lax.Precision.HIGHEST
DAMPING = 0.7


def tile_apply(matrices, inputs):
    return jnp.einsum('stij,kstj->ksti', matrices, inputs, precision=HIGHEST)


def pick_tiles(source, columns):
    index = jnp.broadcast_to(columns[None, :, :, None], (source.shape[0], columns.shape[0], columns.shape[1], source.shape[3]))
    return jnp.take_along_axis(source, index, axis=2)


def reference(residual, coupling_tiles, inverse_tiles, diag_kind, diag_coeff, tile_cols, tile_kinds, tile_coeff, halo_rows, tile_owner, node_slot, edge_nodes, tangents, grad_blocks, vec_blocks):
    groups = N_SECTION * N_DOM
    slab_count = N_SLAB
    blocked = residual.reshape(K, groups, slab_count, ET, B).transpose(1, 0, 2, 3, 4)
    kind_diag = diag_kind.reshape(groups, slab_count, ET)
    coeff_diag = diag_coeff.reshape(groups, slab_count, ET)
    columns = tile_cols.reshape(NB, groups, slab_count, ET).transpose(1, 0, 2, 3)
    kinds_off = tile_kinds.reshape(NB, groups, slab_count, ET).transpose(1, 0, 2, 3)
    coeff_off = tile_coeff.reshape(NB, groups, slab_count, ET).transpose(1, 0, 2, 3)
    rim_rows = halo_rows.reshape(groups, slab_count, HT)

    def smooth(pieces):
        edge_rows, kind_here, coeff_here, cols_here, kinds_here, coeffs_here, rims_here = pieces
        inverses = inverse_tiles[kind_here]
        scales = coeff_here[None, :, :, None]
        smoothed_once = tile_apply(inverses, edge_rows) / scales
        rim_values = pick_tiles(smoothed_once, rims_here)
        empty_rim = jnp.zeros((K, 1, HT, B), jnp.float32)
        from_lower = jnp.concatenate([empty_rim, rim_values[:, :-1]], axis=1)
        from_upper = jnp.concatenate([rim_values[:, 1:], empty_rim], axis=1)
        source = jnp.concatenate([smoothed_once, from_lower, from_upper], axis=2)
        applied = tile_apply(coupling_tiles[kind_here], smoothed_once) * scales
        for column in range(NB):
            picked = pick_tiles(source, cols_here[column])
            applied = applied + tile_apply(coupling_tiles[kinds_here[column]], picked) * coeffs_here[column][None, :, :, None]
        return smoothed_once + DAMPING * (tile_apply(inverses, edge_rows - applied) / scales)

    smoothed = lax.map(smooth, (blocked, kind_diag, coeff_diag, columns, kinds_off, coeff_off, rim_rows))
    smoothed = smoothed.transpose(1, 0, 2, 3, 4).reshape(K, EDGES)

    tile_index = jnp.arange(EDGE_TILES, dtype=jnp.int32)
    node_tile = (tile_owner[:, 0] * slab_count + (tile_index // ET) % slab_count) * NT_DEV + node_slot
    node_base = jnp.repeat(node_tile * B, B)
    end_first = (node_base + edge_nodes[0]).astype(jnp.int32)
    end_second = (node_base + edge_nodes[1]).astype(jnp.int32)
    node_count = NODE_TILES * B
    by_edge = residual.T
    correction = jnp.zeros((EDGES, K), jnp.float32)
    for channel in range(4):
        if channel == 0:
            weight_first = -jnp.ones((EDGES, 1), jnp.float32)
            weight_second = jnp.ones((EDGES, 1), jnp.float32)
            blocks = grad_blocks
        else:
            weight_first = 0.5 * tangents[channel - 1][:, None]
            weight_second = weight_first
            blocks = vec_blocks
        gathered = jax.ops.segment_sum(by_edge * weight_first, end_first, node_count) + jax.ops.segment_sum(by_edge * weight_second, end_second, node_count)
        solved = jnp.einsum('pij,pjk->pik', blocks, gathered.reshape(NODE_TILES, B, K), precision=HIGHEST).reshape(node_count, K)
        correction = correction + weight_first * solved[end_first] + weight_second * solved[end_second]
    return smoothed + correction.T
```

```python
import functools

import jax
import jax.numpy as jnp
from jax import lax
from jax.experimental import pallas as pl
from jax.experimental.pallas import tpu as pltpu
from jax.sharding import Mesh, PartitionSpec as P

DAMPING = 0.7
CORES = 2
F32 = jnp.float32
BF16 = jnp.bfloat16
SMEM = pltpu.SMEM
VMEM = pltpu.VMEM

vmem_spec = pl.BlockSpec(memory_space=VMEM)
smem_spec = pl.BlockSpec(memory_space=SMEM)
any_spec = pl.BlockSpec(memory_space=pl.ANY)


def split(x):
    high = x.astype(BF16)
    low = (x - high.astype(F32)).astype(BF16)
    return high, low


def dot_nt(a, b):
    return lax.dot_general(a, b, (((1,), (1,)), ((), ())), preferred_element_type=F32)


def product_nt(parts, matrix):
    count = parts.shape[0] // 2
    high, low = split(matrix)
    both = dot_nt(parts, high)
    return both[:count] + both[count:] + dot_nt(parts[:count], low)


def stacked(rows):
    high, low = split(rows)
    return jnp.concatenate([high, low], axis=0)


def pack_kernel(owner, slot, residual, tangents, ends, out):
    tiles, width = out.shape[0], out.shape[2]
    lanes = lax.broadcasted_iota(jnp.int32, (1, width), 1)
    row = jnp.zeros((1, width), jnp.int32)
    for t in range(tiles):
        row = jnp.where(lanes == t, owner[t] * 2 + slot[t], row)
    for t in range(tiles):
        part = slice(t * width, (t + 1) * width)
        out[t, 0:8, :] = residual[:, part]
        out[t, 8:11, :] = tangents[:, part]
        out[t, 11:13, :] = ends[:, part].astype(F32)
        out[t, 13:14, :] = row.astype(F32)


def pack(owner, slot, residual, tangents, ends):
    tiles = owner.shape[0]
    width = residual.shape[1] // tiles
    return pl.pallas_call(
        pack_kernel,
        out_shape=jax.ShapeDtypeStruct((tiles, 16, width), F32),
        in_specs=[smem_spec, smem_spec, vmem_spec, vmem_spec, vmem_spec],
        out_specs=vmem_spec,
        name="pack",
    )(owner, slot, residual, tangents, ends)


def sums_kernel(
    where, own, first, second, third, sums, chosen, buf, meta, sems, msems, *, sections_stride, tiles, group
):
    sources = (own, first, second, third)
    copies = []
    for q, src in enumerate(sources):
        copies.append(
            pltpu.make_async_copy(src.at[0, pl.ds(8, 8), :], meta.at[q], msems.at[q])
        )
        copies[-1].start()
    data = []
    for q, src in enumerate(sources):
        data.append(pltpu.make_async_copy(src, buf.at[pl.ds(q * tiles, tiles)], sems.at[q]))
        data[-1].start()
    trash = sums.shape[0] - 1
    sums[...] = jnp.zeros_like(sums)
    for copy in copies:
        copy.wait()
    my_section, my_core = where[0], where[1]

    count = jnp.int32(0)
    for q in range(4):
        for t in range(tiles):
            dst = meta[q, 5, t].astype(jnp.int32)
            owner = dst // 2
            mine = (owner // sections_stride == my_section) & (owner % CORES == my_core)
            local = ((owner % sections_stride) // CORES) * 2 + dst % 2
            chosen[0, count + 1] = q * tiles + t
            chosen[1, count + 1] = local
            count = jnp.where(mine, count + 1, count)
    chosen[0, 0] = count
    for extra in range(group):
        chosen[0, count + 1 + extra] = 0
        chosen[1, count + 1 + extra] = trash
    for copy in data:
        copy.wait()
    width = buf.shape[2]
    nodes = lax.broadcasted_iota(jnp.int32, (width, width), 0).astype(F32)

    def step(i, carry):
        for j in range(group):
            at = i * group + j + 1
            tile, local = chosen[0, at], chosen[1, at]
            rows = buf[tile, 0:8, :]
            halves = 0.5 * buf[tile, 8:11, :]
            at_a = (nodes == buf[tile, 11:12, :]).astype(F32)
            at_b = (nodes == buf[tile, 12:13, :]).astype(F32)
            plus = (at_a + at_b).astype(BF16)
            minus = (at_b - at_a).astype(BF16)
            vec = jnp.concatenate([halves[c : c + 1] * rows for c in range(3)], axis=0)
            total_vec = dot_nt(stacked(vec), plus)
            total_grad = dot_nt(stacked(rows), minus)
            sums[local, 0:8, :] += total_grad[:8] + total_grad[8:]
            sums[local, 8:32, :] += total_vec[:24] + total_vec[24:]
        return carry

    lax.fori_loop(0, (count + group - 1) // group, step, 0)


def node_sums(where, payloads, places, sections_stride):
    tiles, _, width = payloads[0].shape
    group = 4
    return pl.pallas_call(
        functools.partial(
            sums_kernel, sections_stride=sections_stride, tiles=tiles, group=group
        ),
        out_shape=(
            jax.ShapeDtypeStruct((places + 1, 32, width), F32),
            jax.ShapeDtypeStruct((2, 4 * tiles + 1 + group), jnp.int32),
        ),
        in_specs=[smem_spec] + [any_spec] * 4,
        out_specs=(vmem_spec, smem_spec),
        scratch_shapes=[
            VMEM((4 * tiles, 16, width), F32),
            SMEM((4, 8, width), F32),
            pltpu.SemaphoreType.DMA((4,)),
            pltpu.SemaphoreType.DMA((4,)),
        ],
        name="node_sums",
    )(where, *payloads)


def solve_kernel(arrived, grad, vec, out):
    count = arrived.shape[0]
    for n in range(grad.shape[0]):
        rows = arrived[0, n]
        for z in range(1, count):
            rows = rows + arrived[z, n]
        out[n, 0:8, :] = product_nt(stacked(rows[:8]), grad[n])
        out[n, 8:32, :] = product_nt(stacked(rows[8:]), vec[n])


def solve(arrived, grad, vec):
    return pl.pallas_call(
        solve_kernel,
        out_shape=jax.ShapeDtypeStruct(arrived.shape[1:], F32),
        in_specs=[vmem_spec] * 3,
        out_specs=vmem_spec,
        name="solve",
    )(arrived, grad, vec)


def back_kernel(chosen, own, first, second, third, values, out, buf, sems, *, tiles):
    data = []
    for q, src in enumerate((own, first, second, third)):
        data.append(
            pltpu.make_async_copy(
                src.at[:, pl.ds(8, 8), :], buf.at[pl.ds(q * tiles, tiles)], sems.at[q]
            )
        )
        data[-1].start()
    out[...] = jnp.zeros_like(out)
    for copy in data:
        copy.wait()
    width = buf.shape[2]

    def pick(rows, index):
        return jnp.take_along_axis(rows, index, axis=1)

    def step(i, carry):
        tile, local = chosen[0, i + 1], chosen[1, i + 1]
        index_a = jnp.broadcast_to(buf[tile, 3:4, :].astype(jnp.int32), (8, width))
        index_b = jnp.broadcast_to(buf[tile, 4:5, :].astype(jnp.int32), (8, width))
        grad = values[local, 0:8, :]
        total = pick(grad, index_b) - pick(grad, index_a)
        for c in range(3):
            rows = values[local, 8 + 8 * c : 16 + 8 * c, :]
            half = 0.5 * buf[tile, c : c + 1, :]
            total = total + half * (pick(rows, index_a) + pick(rows, index_b))
        out[tile] = total
        return carry

    lax.fori_loop(0, chosen[0, 0], step, 0)


def back(chosen, payloads, values):
    tiles, _, width = payloads[0].shape
    return pl.pallas_call(
        functools.partial(back_kernel, tiles=tiles),
        out_shape=jax.ShapeDtypeStruct((4 * tiles, 8, width), F32),
        in_specs=[smem_spec] + [any_spec] * 4 + [vmem_spec],
        out_specs=vmem_spec,
        scratch_shapes=[VMEM((4 * tiles, 8, width), F32), pltpu.SemaphoreType.DMA((4,))],
        name="back",
    )(chosen, *payloads, values)


def by_tile(ref, tiles, width):
    return jnp.concatenate([ref[:, t * width : (t + 1) * width] for t in range(tiles)], axis=0)


def smooth_kernel(kind, coeff, halo, residual, inverse, out, rim, work):
    tiles, _, width = out.shape
    parts = stacked(by_tile(residual, tiles, width))
    for k in range(inverse.shape[0]):
        work[k] = product_nt(parts, inverse[k]).reshape(tiles, 8, width)
    for t in range(tiles):
        out[t] = work[kind[t], t] / coeff[t]
    for h in range(rim.shape[0]):
        rim[h] = out[halo[h]]


def smooth(kind, coeff, halo, residual, inverse):
    tiles = kind.shape[0]
    kinds, width, _ = inverse.shape
    return pl.pallas_call(
        smooth_kernel,
        out_shape=(
            jax.ShapeDtypeStruct((tiles, 8, width), F32),
            jax.ShapeDtypeStruct((halo.shape[0], 8, width), F32),
        ),
        in_specs=[smem_spec] * 3 + [vmem_spec] * 2,
        out_specs=(vmem_spec, vmem_spec),
        scratch_shapes=[VMEM((kinds, tiles, 8, width), F32)],
        name="smooth_once",
    )(kind, coeff, halo, residual, inverse)


def again_kernel(
    kind, coeff, cols, kinds, coeffs, smoothed, low, high, residual, coupling, inverse, out, work, rest
):
    tiles, _, width = smoothed.shape
    sources = jnp.concatenate(
        [
            smoothed[...].reshape(tiles * 8, width),
            low[...].reshape(low.shape[0] * 8, width),
            high[...].reshape(high.shape[0] * 8, width),
        ],
        axis=0,
    )
    parts = stacked(sources)
    count = sources.shape[0] // 8
    for k in range(coupling.shape[0]):
        work[k] = product_nt(parts, coupling[k]).reshape(count, 8, width)
    for t in range(tiles):
        total = coeff[t] * work[kind[t], t]
        for m in range(cols.shape[0]):
            total = total + coeffs[m, t] * work[kinds[m, t], cols[m, t]]
        rest[t] = residual[:, t * width : (t + 1) * width] - total
    parts = stacked(rest[...].reshape(tiles * 8, width))
    for k in range(inverse.shape[0]):
        work[k, 0:tiles] = product_nt(parts, inverse[k]).reshape(tiles, 8, width)
    for t in range(tiles):
        out[t] = smoothed[t] + DAMPING * (work[kind[t], t] / coeff[t])


def smooth_again(kind, coeff, cols, kinds, coeffs, smoothed, low, high, residual, coupling, inverse):
    tiles, _, width = smoothed.shape
    count = tiles + low.shape[0] + high.shape[0]
    return pl.pallas_call(
        again_kernel,
        out_shape=jax.ShapeDtypeStruct((tiles, 8, width), F32),
        in_specs=[smem_spec] * 5 + [vmem_spec] * 6,
        out_specs=vmem_spec,
        scratch_shapes=[
            VMEM((coupling.shape[0], count, 8, width), F32),
            VMEM((tiles, 8, width), F32),
        ],
        name="smooth_again",
    )(kind, coeff, cols, kinds, coeffs, smoothed, low, high, residual, coupling, inverse)


def finish_kernel(smoothed, own, first, second, third, out):
    tiles, _, width = smoothed.shape
    for t in range(tiles):
        out[:, t * width : (t + 1) * width] = smoothed[t] + (
            (own[t] + first[t]) + (second[t] + third[t])
        )


def finish(smoothed, pieces):
    tiles, cases, width = smoothed.shape
    return pl.pallas_call(
        finish_kernel,
        out_shape=jax.ShapeDtypeStruct((cases, tiles * width), F32),
        in_specs=[vmem_spec] * 5,
        out_specs=vmem_spec,
        name="finish",
    )(smoothed, *pieces)


def swap(x, which):
    return lax.ppermute(x, ("section", "core"), [(i, i ^ which) for i in range(4)])


def body(
    residual,
    coupling_tiles,
    inverse_tiles,
    diag_kind,
    diag_coeff,
    tile_cols,
    tile_kinds,
    tile_coeff,
    halo_rows,
    tile_owner,
    node_slot,
    edge_nodes,
    tangents,
    grad_blocks,
    vec_blocks,
):
    heights = lax.axis_size("z")
    node_tiles = grad_blocks.shape[0]
    tiles = diag_kind.shape[0]
    width = coupling_tiles.shape[1]
    where = jnp.stack([lax.axis_index("section"), lax.axis_index("core")]).astype(jnp.int32)
    own = pack(tile_owner[:, 0], node_slot, residual, tangents, edge_nodes)
    payloads = [own] + [swap(own, which) for which in (1, 2, 3)]

    smoothed, rim = smooth(diag_kind, diag_coeff, halo_rows, residual, inverse_tiles)
    slabs = lax.axis_size("slab")
    low = lax.ppermute(rim, "slab", [(i, i + 1) for i in range(slabs - 1)])
    high = lax.ppermute(rim, "slab", [(i + 1, i) for i in range(slabs - 1)])

    sums, chosen = node_sums(where, payloads, heights * node_tiles, heights * CORES)
    sums = sums[: heights * node_tiles].reshape(heights, node_tiles * 32, width)
    arrived = lax.all_to_all(sums, "z", split_axis=0, concat_axis=0, tiled=True)

    smoothed_twice = smooth_again(
        diag_kind, diag_coeff, tile_cols, tile_kinds, tile_coeff,
        smoothed, low, high, residual, coupling_tiles, inverse_tiles,
    )

    solved = solve(arrived.reshape(heights, node_tiles, 32, width), grad_blocks, vec_blocks)
    values = lax.all_gather(solved, "z", tiled=True)
    corrections = back(chosen, payloads, values).reshape(4, tiles, 8, width)
    pieces = [corrections[0]] + [swap(corrections[which], which) for which in (1, 2, 3)]
    return finish(smoothed_twice, pieces)


def solution(mesh):
    names = ("section", "z", "core", "slab")
    sections, doms, slabs = (mesh.shape[name] for name in ("section", "dom", "slab"))
    inner = Mesh(mesh.devices.reshape(sections, doms // CORES, CORES, slabs), names)
    rows, cols = P(names), P(None, names)
    placed = (
        cols, P(), P(), rows, rows, cols, cols, cols, rows, rows, rows, cols, cols, rows, rows,
    )
    return jax.shard_map(
        body, mesh=inner, in_specs=placed, out_specs=cols, check_vma=False
    )
```

```python
import functools

import jax
import jax.numpy as jnp
from jax import lax
from jax.experimental import pallas as pl
from jax.experimental.pallas import tpu as pltpu
from jax.sharding import Mesh, PartitionSpec as P

DAMPING = 0.7
CORES = 2
NEAR = 1
F32 = jnp.float32
BF16 = jnp.bfloat16
SMEM = pltpu.SMEM
VMEM = pltpu.VMEM

vmem_spec = pl.BlockSpec(memory_space=VMEM)
smem_spec = pl.BlockSpec(memory_space=SMEM)
any_spec = pl.BlockSpec(memory_space=pl.ANY)


def split(x):
    high = x.astype(BF16)
    low = (x - high.astype(F32)).astype(BF16)
    return high, low


def dot_nt(a, b):
    return lax.dot_general(a, b, (((1,), (1,)), ((), ())), preferred_element_type=F32)


def product_nt(parts, matrix):
    count = parts.shape[0] // 2
    high, low = split(matrix)
    both = dot_nt(parts, high)
    return both[:count] + both[count:] + dot_nt(parts[:count], low)


def stacked(rows):
    high, low = split(rows)
    return jnp.concatenate([high, low], axis=0)


def pack_kernel(owner, slot, residual, tangents, ends, out):
    tiles, width = out.shape[0], out.shape[2]
    lanes = lax.broadcasted_iota(jnp.int32, (1, width), 1)
    row = jnp.zeros((1, width), jnp.int32)
    for t in range(tiles):
        row = jnp.where(lanes == t, owner[t] * 2 + slot[t], row)
    for t in range(tiles):
        part = slice(t * width, (t + 1) * width)
        out[t, 0:8, :] = residual[:, part]
        out[t, 8:11, :] = tangents[:, part]
        out[t, 11:13, :] = ends[:, part].astype(F32)
        out[t, 13:14, :] = row.astype(F32)


def pack(owner, slot, residual, tangents, ends):
    tiles = owner.shape[0]
    width = residual.shape[1] // tiles
    return pl.pallas_call(
        pack_kernel,
        out_shape=jax.ShapeDtypeStruct((tiles, 16, width), F32),
        in_specs=[smem_spec, smem_spec, vmem_spec, vmem_spec, vmem_spec],
        out_specs=vmem_spec,
        name="pack",
    )(owner, slot, residual, tangents, ends)


def sums_kernel(where, gathered, sums, chosen, buf, meta, sems, *, doms, stride, team, tiles, group):
    width = buf.shape[2]
    total = team * tiles
    copies = [
        pltpu.make_async_copy(gathered.at[q * tiles, pl.ds(8, 8), :], meta.at[q], sems.at[q])
        for q in range(team)
    ]
    for copy in copies:
        copy.start()
    data = pltpu.make_async_copy(gathered, buf.at[pl.ds(0, total)], sems.at[team])
    data.start()
    sums[...] = jnp.zeros_like(sums)
    buf[total] = jnp.zeros(buf.shape[1:], F32)
    for copy in copies:
        copy.wait()
    mine = where[0]

    count = jnp.int32(0)
    for q in range(team):
        for t in range(tiles):
            dst = meta[q, 5, t].astype(jnp.int32)
            owner, slot = dst // 2, dst % 2
            section, dom = owner // doms, owner % doms
            z, core = dom // CORES, dom % CORES
            cls = (section * stride + z % stride) * CORES + core
            chosen[0, count + 1] = q * tiles + t
            chosen[1, count + 1] = (z // stride) * 2 + slot
            count = jnp.where(cls == mine, count + 1, count)
    chosen[0, 0] = count
    for extra in range(group):
        chosen[0, count + 1 + extra] = total
        chosen[1, count + 1 + extra] = 0
    data.wait()
    nodes = lax.broadcasted_iota(jnp.int32, (width, width), 0).astype(F32)

    def step(i, carry):
        for j in range(group):
            at = i * group + j + 1
            tile, local = chosen[0, at], chosen[1, at]
            rows = buf[tile, 0:8, :]
            halves = 0.5 * buf[tile, 8:11, :]
            at_a = (nodes == buf[tile, 11:12, :]).astype(F32)
            at_b = (nodes == buf[tile, 12:13, :]).astype(F32)
            plus = (at_a + at_b).astype(BF16)
            minus = (at_b - at_a).astype(BF16)
            vec = jnp.concatenate([halves[c : c + 1] * rows for c in range(3)], axis=0)
            total_vec = dot_nt(stacked(vec), plus)
            total_grad = dot_nt(stacked(rows), minus)
            sums[local, 0:8, :] += total_grad[:8] + total_grad[8:]
            sums[local, 8:32, :] += total_vec[:24] + total_vec[24:]
        return carry

    lax.fori_loop(0, (count + group - 1) // group, step, 0)


def node_sums(where, gathered, team, places, doms, stride):
    total, _, width = gathered.shape
    group = 4
    return pl.pallas_call(
        functools.partial(
            sums_kernel, doms=doms, stride=stride, team=team, tiles=total // team, group=group
        ),
        out_shape=(
            jax.ShapeDtypeStruct((places, 32, width), F32),
            jax.ShapeDtypeStruct((2, total + 1 + group), jnp.int32),
        ),
        in_specs=[smem_spec, any_spec],
        out_specs=(vmem_spec, smem_spec),
        scratch_shapes=[
            VMEM((total + 1, 16, width), F32),
            SMEM((team, 8, width), F32),
            pltpu.SemaphoreType.DMA((team + 1,)),
        ],
        name="node_sums",
    )(where, gathered)


def solve_kernel(arrived, grad, vec, out):
    count = arrived.shape[0]
    for n in range(grad.shape[0]):
        rows = arrived[0, n]
        for z in range(1, count):
            rows = rows + arrived[z, n]
        out[n, 0:8, :] = product_nt(stacked(rows[:8]), grad[n])
        out[n, 8:32, :] = product_nt(stacked(rows[8:]), vec[n])


def solve(arrived, grad, vec):
    return pl.pallas_call(
        solve_kernel,
        out_shape=jax.ShapeDtypeStruct(arrived.shape[1:], F32),
        in_specs=[vmem_spec] * 3,
        out_specs=vmem_spec,
        name="solve",
    )(arrived, grad, vec)


def back_kernel(chosen, gathered, values, out, buf, sem):
    data = pltpu.make_async_copy(gathered.at[:, pl.ds(8, 8), :], buf, sem)
    data.start()
    out[...] = jnp.zeros_like(out)
    data.wait()
    width = buf.shape[2]

    def pick(rows, index):
        return jnp.take_along_axis(rows, index, axis=1)

    def step(i, carry):
        tile, local = chosen[0, i + 1], chosen[1, i + 1]
        index_a = jnp.broadcast_to(buf[tile, 3:4, :].astype(jnp.int32), (8, width))
        index_b = jnp.broadcast_to(buf[tile, 4:5, :].astype(jnp.int32), (8, width))
        grad = values[local, 0:8, :]
        total = pick(grad, index_b) - pick(grad, index_a)
        for c in range(3):
            rows = values[local, 8 + 8 * c : 16 + 8 * c, :]
            half = 0.5 * buf[tile, c : c + 1, :]
            total = total + half * (pick(rows, index_a) + pick(rows, index_b))
        out[tile] = total
        return carry

    lax.fori_loop(0, chosen[0, 0], step, 0)


def back(chosen, gathered, values):
    total, _, width = gathered.shape
    return pl.pallas_call(
        back_kernel,
        out_shape=jax.ShapeDtypeStruct((total, 8, width), F32),
        in_specs=[smem_spec, any_spec, vmem_spec],
        out_specs=vmem_spec,
        scratch_shapes=[VMEM((total, 8, width), F32), pltpu.SemaphoreType.DMA(())],
        name="back",
    )(chosen, gathered, values)


def by_tile(ref, tiles, width):
    return jnp.concatenate([ref[:, t * width : (t + 1) * width] for t in range(tiles)], axis=0)


def smooth_kernel(kind, coeff, halo, residual, inverse, out, rim, work):
    tiles, _, width = out.shape
    parts = stacked(by_tile(residual, tiles, width))
    for k in range(inverse.shape[0]):
        work[k] = product_nt(parts, inverse[k]).reshape(tiles, 8, width)
    for t in range(tiles):
        out[t] = work[kind[t], t] / coeff[t]
    for h in range(rim.shape[0]):
        rim[h] = out[halo[h]]


def smooth(kind, coeff, halo, residual, inverse):
    tiles = kind.shape[0]
    kinds, width, _ = inverse.shape
    return pl.pallas_call(
        smooth_kernel,
        out_shape=(
            jax.ShapeDtypeStruct((tiles, 8, width), F32),
            jax.ShapeDtypeStruct((halo.shape[0], 8, width), F32),
        ),
        in_specs=[smem_spec] * 3 + [vmem_spec] * 2,
        out_specs=(vmem_spec, vmem_spec),
        scratch_shapes=[VMEM((kinds, tiles, 8, width), F32)],
        name="smooth_once",
    )(kind, coeff, halo, residual, inverse)


def again_kernel(
    kind, coeff, cols, kinds, coeffs, smoothed, low, high, residual, coupling, inverse, out, work, rest
):
    tiles, _, width = smoothed.shape
    sources = jnp.concatenate(
        [
            smoothed[...].reshape(tiles * 8, width),
            low[...].reshape(low.shape[0] * 8, width),
            high[...].reshape(high.shape[0] * 8, width),
        ],
        axis=0,
    )
    parts = stacked(sources)
    count = sources.shape[0] // 8
    for k in range(coupling.shape[0]):
        work[k] = product_nt(parts, coupling[k]).reshape(count, 8, width)
    for t in range(tiles):
        total = coeff[t] * work[kind[t], t]
        for m in range(cols.shape[0]):
            total = total + coeffs[m, t] * work[kinds[m, t], cols[m, t]]
        rest[t] = residual[:, t * width : (t + 1) * width] - total
    parts = stacked(rest[...].reshape(tiles * 8, width))
    for k in range(inverse.shape[0]):
        work[k, 0:tiles] = product_nt(parts, inverse[k]).reshape(tiles, 8, width)
    for t in range(tiles):
        out[t] = smoothed[t] + DAMPING * (work[kind[t], t] / coeff[t])


def smooth_again(kind, coeff, cols, kinds, coeffs, smoothed, low, high, residual, coupling, inverse):
    tiles, _, width = smoothed.shape
    count = tiles + low.shape[0] + high.shape[0]
    return pl.pallas_call(
        again_kernel,
        out_shape=jax.ShapeDtypeStruct((tiles, 8, width), F32),
        in_specs=[smem_spec] * 5 + [vmem_spec] * 6,
        out_specs=vmem_spec,
        scratch_shapes=[
            VMEM((coupling.shape[0], count, 8, width), F32),
            VMEM((tiles, 8, width), F32),
        ],
        name="smooth_again",
    )(kind, coeff, cols, kinds, coeffs, smoothed, low, high, residual, coupling, inverse)


def finish_kernel(smoothed, pieces, out):
    tiles, _, width = smoothed.shape
    for t in range(tiles):
        rows = pieces[0, t]
        for q in range(1, pieces.shape[0]):
            rows = rows + pieces[q, t]
        out[:, t * width : (t + 1) * width] = smoothed[t] + rows


def finish(smoothed, pieces):
    tiles, cases, width = smoothed.shape
    return pl.pallas_call(
        finish_kernel,
        out_shape=jax.ShapeDtypeStruct((cases, tiles * width), F32),
        in_specs=[vmem_spec] * 2,
        out_specs=vmem_spec,
        name="finish",
    )(smoothed, pieces)


TEAM = ("section", "near", "core")


def body(
    residual,
    coupling_tiles,
    inverse_tiles,
    diag_kind,
    diag_coeff,
    tile_cols,
    tile_kinds,
    tile_coeff,
    halo_rows,
    tile_owner,
    node_slot,
    edge_nodes,
    tangents,
    grad_blocks,
    vec_blocks,
):
    heights, stride, team = lax.axis_size("far"), lax.axis_size("near"), lax.axis_size(TEAM)
    node_tiles = grad_blocks.shape[0]
    tiles = diag_kind.shape[0]
    width = coupling_tiles.shape[1]
    where = lax.axis_index(TEAM).astype(jnp.int32).reshape(1)
    own = pack(tile_owner[:, 0], node_slot, residual, tangents, edge_nodes)
    gathered = lax.all_gather(own, TEAM, tiled=True)

    smoothed, rim = smooth(diag_kind, diag_coeff, halo_rows, residual, inverse_tiles)
    slabs = lax.axis_size("slab")
    low = lax.ppermute(rim, "slab", [(i, i + 1) for i in range(slabs - 1)])
    high = lax.ppermute(rim, "slab", [(i + 1, i) for i in range(slabs - 1)])

    doms = heights * stride * CORES
    sums, chosen = node_sums(where, gathered, team, heights * node_tiles, doms, stride)
    sums = sums.reshape(heights, node_tiles * 32, width)
    arrived = lax.all_to_all(sums, "far", split_axis=0, concat_axis=0, tiled=True)

    smoothed_twice = smooth_again(
        diag_kind, diag_coeff, tile_cols, tile_kinds, tile_coeff,
        smoothed, low, high, residual, coupling_tiles, inverse_tiles,
    )
    arrived, smoothed_twice = lax.optimization_barrier((arrived, smoothed_twice))

    solved = solve(arrived.reshape(heights, node_tiles, 32, width), grad_blocks, vec_blocks)
    values = lax.all_gather(solved, "far", tiled=True)
    corrections = back(chosen, gathered, values).reshape(team, tiles, 8, width)
    pieces = lax.all_to_all(corrections, TEAM, split_axis=0, concat_axis=0, tiled=True)
    return finish(smoothed_twice, pieces)


def solution(mesh):
    names = ("section", "far", "near", "core", "slab")
    sections, doms, slabs = (mesh.shape[name] for name in ("section", "dom", "slab"))
    shape = (sections, doms // CORES // NEAR, NEAR, CORES, slabs)
    inner = Mesh(mesh.devices.reshape(shape), names)
    rows, cols = P(names), P(None, names)
    placed = (
        cols, P(), P(), rows, rows, cols, cols, cols, rows, rows, rows, cols, cols, rows, rows,
    )
    return jax.shard_map(
        body, mesh=inner, in_specs=placed, out_specs=cols, check_vma=False
    )
```

```python
import functools

import jax
import jax.numpy as jnp
from jax import lax
from jax.experimental import pallas as pl
from jax.experimental.pallas import tpu as pltpu
from jax.sharding import Mesh, PartitionSpec as P

DAMPING = 0.7
CORES = 2
NEAR = 2
F32 = jnp.float32
BF16 = jnp.bfloat16
SMEM = pltpu.SMEM
VMEM = pltpu.VMEM

vmem_spec = pl.BlockSpec(memory_space=VMEM)
smem_spec = pl.BlockSpec(memory_space=SMEM)
any_spec = pl.BlockSpec(memory_space=pl.ANY)


def split(x):
    high = x.astype(BF16)
    low = (x - high.astype(F32)).astype(BF16)
    return high, low


def dot_nt(a, b):
    return lax.dot_general(a, b, (((1,), (1,)), ((), ())), preferred_element_type=F32)


def product_nt(parts, matrix):
    count = parts.shape[0] // 2
    high, low = split(matrix)
    both = dot_nt(parts, high)
    return both[:count] + both[count:] + dot_nt(parts[:count], low)


def stacked(rows):
    high, low = split(rows)
    return jnp.concatenate([high, low], axis=0)


def pack_kernel(owner, slot, residual, tangents, ends, out):
    tiles, width = out.shape[0], out.shape[2]
    lanes = lax.broadcasted_iota(jnp.int32, (1, width), 1)
    row = jnp.zeros((1, width), jnp.int32)
    for t in range(tiles):
        row = jnp.where(lanes == t, owner[t] * 2 + slot[t], row)
    for t in range(tiles):
        part = slice(t * width, (t + 1) * width)
        out[t, 0:8, :] = residual[:, part]
        out[t, 8:11, :] = tangents[:, part]
        out[t, 11:13, :] = ends[:, part].astype(F32)
        out[t, 13:14, :] = row.astype(F32)


def pack(owner, slot, residual, tangents, ends):
    tiles = owner.shape[0]
    width = residual.shape[1] // tiles
    return pl.pallas_call(
        pack_kernel,
        out_shape=jax.ShapeDtypeStruct((tiles, 16, width), F32),
        in_specs=[smem_spec, smem_spec, vmem_spec, vmem_spec, vmem_spec],
        out_specs=vmem_spec,
        name="pack",
    )(owner, slot, residual, tangents, ends)


def sums_kernel(where, gathered, sums, chosen, buf, meta, sems, *, doms, stride, team, tiles, group):
    width = buf.shape[2]
    total = team * tiles
    copies = [
        pltpu.make_async_copy(gathered.at[q * tiles, pl.ds(8, 8), :], meta.at[q], sems.at[q])
        for q in range(team)
    ]
    for copy in copies:
        copy.start()
    data = pltpu.make_async_copy(gathered, buf.at[pl.ds(0, total)], sems.at[team])
    data.start()
    sums[...] = jnp.zeros_like(sums)
    buf[total] = jnp.zeros(buf.shape[1:], F32)
    for copy in copies:
        copy.wait()
    mine = where[0]

    count = jnp.int32(0)
    for q in range(team):
        for t in range(tiles):
            dst = meta[q, 5, t].astype(jnp.int32)
            owner, slot = dst // 2, dst % 2
            section, dom = owner // doms, owner % doms
            z, core = dom // CORES, dom % CORES
            cls = (section * stride + z % stride) * CORES + core
            chosen[0, count + 1] = q * tiles + t
            chosen[1, count + 1] = (z // stride) * 2 + slot
            count = jnp.where(cls == mine, count + 1, count)
    chosen[0, 0] = count
    for extra in range(group):
        chosen[0, count + 1 + extra] = total
        chosen[1, count + 1 + extra] = 0
    data.wait()
    nodes = lax.broadcasted_iota(jnp.int32, (width, width), 0).astype(F32)

    def step(i, carry):
        for j in range(group):
            at = i * group + j + 1
            tile, local = chosen[0, at], chosen[1, at]
            rows = buf[tile, 0:8, :]
            halves = 0.5 * buf[tile, 8:11, :]
            at_a = (nodes == buf[tile, 11:12, :]).astype(F32)
            at_b = (nodes == buf[tile, 12:13, :]).astype(F32)
            plus = (at_a + at_b).astype(BF16)
            minus = (at_b - at_a).astype(BF16)
            vec = jnp.concatenate([halves[c : c + 1] * rows for c in range(3)], axis=0)
            total_vec = dot_nt(stacked(vec), plus)
            total_grad = dot_nt(stacked(rows), minus)
            sums[local, 0:8, :] += total_grad[:8] + total_grad[8:]
            sums[local, 8:32, :] += total_vec[:24] + total_vec[24:]
        return carry

    lax.fori_loop(0, (count + group - 1) // group, step, 0)


def node_sums(where, gathered, team, places, doms, stride):
    total, _, width = gathered.shape
    group = 4
    return pl.pallas_call(
        functools.partial(
            sums_kernel, doms=doms, stride=stride, team=team, tiles=total // team, group=group
        ),
        out_shape=(
            jax.ShapeDtypeStruct((places, 32, width), F32),
            jax.ShapeDtypeStruct((2, total + 1 + group), jnp.int32),
        ),
        in_specs=[smem_spec, any_spec],
        out_specs=(vmem_spec, smem_spec),
        scratch_shapes=[
            VMEM((total + 1, 16, width), F32),
            SMEM((team, 8, width), F32),
            pltpu.SemaphoreType.DMA((team + 1,)),
        ],
        name="node_sums",
    )(where, gathered)


def solve_kernel(arrived, grad, vec, out):
    count = arrived.shape[0]
    for n in range(grad.shape[0]):
        rows = arrived[0, n]
        for z in range(1, count):
            rows = rows + arrived[z, n]
        out[n, 0:8, :] = product_nt(stacked(rows[:8]), grad[n])
        out[n, 8:32, :] = product_nt(stacked(rows[8:]), vec[n])


def solve(arrived, grad, vec):
    return pl.pallas_call(
        solve_kernel,
        out_shape=jax.ShapeDtypeStruct(arrived.shape[1:], F32),
        in_specs=[vmem_spec] * 3,
        out_specs=vmem_spec,
        name="solve",
    )(arrived, grad, vec)


def back_kernel(chosen, gathered, values, out, buf, sem):
    data = pltpu.make_async_copy(gathered.at[:, pl.ds(8, 8), :], buf, sem)
    data.start()
    out[...] = jnp.zeros_like(out)
    data.wait()
    width = buf.shape[2]

    def pick(rows, index):
        return jnp.take_along_axis(rows, index, axis=1)

    def step(i, carry):
        tile, local = chosen[0, i + 1], chosen[1, i + 1]
        index_a = jnp.broadcast_to(buf[tile, 3:4, :].astype(jnp.int32), (8, width))
        index_b = jnp.broadcast_to(buf[tile, 4:5, :].astype(jnp.int32), (8, width))
        grad = values[local, 0:8, :]
        total = pick(grad, index_b) - pick(grad, index_a)
        for c in range(3):
            rows = values[local, 8 + 8 * c : 16 + 8 * c, :]
            half = 0.5 * buf[tile, c : c + 1, :]
            total = total + half * (pick(rows, index_a) + pick(rows, index_b))
        out[tile] = total
        return carry

    lax.fori_loop(0, chosen[0, 0], step, 0)


def back(chosen, gathered, values):
    total, _, width = gathered.shape
    return pl.pallas_call(
        back_kernel,
        out_shape=jax.ShapeDtypeStruct((total, 8, width), F32),
        in_specs=[smem_spec, any_spec, vmem_spec],
        out_specs=vmem_spec,
        scratch_shapes=[VMEM((total, 8, width), F32), pltpu.SemaphoreType.DMA(())],
        name="back",
    )(chosen, gathered, values)


def by_tile(ref, tiles, width):
    return jnp.concatenate([ref[:, t * width : (t + 1) * width] for t in range(tiles)], axis=0)


def smooth_kernel(kind, coeff, halo, residual, inverse, out, rim, work):
    tiles, _, width = out.shape
    parts = stacked(by_tile(residual, tiles, width))
    for k in range(inverse.shape[0]):
        work[k] = product_nt(parts, inverse[k]).reshape(tiles, 8, width)
    for t in range(tiles):
        out[t] = work[kind[t], t] / coeff[t]
    for h in range(rim.shape[0]):
        rim[h] = out[halo[h]]


def smooth(kind, coeff, halo, residual, inverse):
    tiles = kind.shape[0]
    kinds, width, _ = inverse.shape
    return pl.pallas_call(
        smooth_kernel,
        out_shape=(
            jax.ShapeDtypeStruct((tiles, 8, width), F32),
            jax.ShapeDtypeStruct((halo.shape[0], 8, width), F32),
        ),
        in_specs=[smem_spec] * 3 + [vmem_spec] * 2,
        out_specs=(vmem_spec, vmem_spec),
        scratch_shapes=[VMEM((kinds, tiles, 8, width), F32)],
        name="smooth_once",
    )(kind, coeff, halo, residual, inverse)


def again_kernel(
    kind, coeff, cols, kinds, coeffs, smoothed, low, high, residual, coupling, inverse, out, work, rest
):
    tiles, _, width = smoothed.shape
    sources = jnp.concatenate(
        [
            smoothed[...].reshape(tiles * 8, width),
            low[...].reshape(low.shape[0] * 8, width),
            high[...].reshape(high.shape[0] * 8, width),
        ],
        axis=0,
    )
    parts = stacked(sources)
    count = sources.shape[0] // 8
    for k in range(coupling.shape[0]):
        work[k] = product_nt(parts, coupling[k]).reshape(count, 8, width)
    for t in range(tiles):
        total = coeff[t] * work[kind[t], t]
        for m in range(cols.shape[0]):
            total = total + coeffs[m, t] * work[kinds[m, t], cols[m, t]]
        rest[t] = residual[:, t * width : (t + 1) * width] - total
    parts = stacked(rest[...].reshape(tiles * 8, width))
    for k in range(inverse.shape[0]):
        work[k, 0:tiles] = product_nt(parts, inverse[k]).reshape(tiles, 8, width)
    for t in range(tiles):
        out[t] = smoothed[t] + DAMPING * (work[kind[t], t] / coeff[t])


def smooth_again(kind, coeff, cols, kinds, coeffs, smoothed, low, high, residual, coupling, inverse):
    tiles, _, width = smoothed.shape
    count = tiles + low.shape[0] + high.shape[0]
    return pl.pallas_call(
        again_kernel,
        out_shape=jax.ShapeDtypeStruct((tiles, 8, width), F32),
        in_specs=[smem_spec] * 5 + [vmem_spec] * 6,
        out_specs=vmem_spec,
        scratch_shapes=[
            VMEM((coupling.shape[0], count, 8, width), F32),
            VMEM((tiles, 8, width), F32),
        ],
        name="smooth_again",
    )(kind, coeff, cols, kinds, coeffs, smoothed, low, high, residual, coupling, inverse)


def finish_kernel(smoothed, pieces, out):
    tiles, _, width = smoothed.shape
    for t in range(tiles):
        rows = pieces[0, t]
        for q in range(1, pieces.shape[0]):
            rows = rows + pieces[q, t]
        out[:, t * width : (t + 1) * width] = smoothed[t] + rows


def finish(smoothed, pieces):
    tiles, cases, width = smoothed.shape
    return pl.pallas_call(
        finish_kernel,
        out_shape=jax.ShapeDtypeStruct((cases, tiles * width), F32),
        in_specs=[vmem_spec] * 2,
        out_specs=vmem_spec,
        name="finish",
    )(smoothed, pieces)


TEAM = ("section", "near", "core")


def body(
    residual,
    coupling_tiles,
    inverse_tiles,
    diag_kind,
    diag_coeff,
    tile_cols,
    tile_kinds,
    tile_coeff,
    halo_rows,
    tile_owner,
    node_slot,
    edge_nodes,
    tangents,
    grad_blocks,
    vec_blocks,
):
    heights, stride, team = lax.axis_size("far"), lax.axis_size("near"), lax.axis_size(TEAM)
    node_tiles = grad_blocks.shape[0]
    tiles = diag_kind.shape[0]
    width = coupling_tiles.shape[1]
    where = lax.axis_index(TEAM).astype(jnp.int32).reshape(1)
    own = pack(tile_owner[:, 0], node_slot, residual, tangents, edge_nodes)
    gathered = lax.all_gather(own, TEAM, tiled=True)

    smoothed, rim = smooth(diag_kind, diag_coeff, halo_rows, residual, inverse_tiles)
    slabs = lax.axis_size("slab")
    low = lax.ppermute(rim, "slab", [(i, i + 1) for i in range(slabs - 1)])
    high = lax.ppermute(rim, "slab", [(i + 1, i) for i in range(slabs - 1)])

    doms = heights * stride * CORES
    sums, chosen = node_sums(where, gathered, team, heights * node_tiles, doms, stride)
    sums = sums.reshape(heights, node_tiles * 32, width)
    arrived = lax.all_to_all(sums, "far", split_axis=0, concat_axis=0, tiled=True)

    smoothed_twice = smooth_again(
        diag_kind, diag_coeff, tile_cols, tile_kinds, tile_coeff,
        smoothed, low, high, residual, coupling_tiles, inverse_tiles,
    )
    arrived, smoothed_twice = lax.optimization_barrier((arrived, smoothed_twice))

    solved = solve(arrived.reshape(heights, node_tiles, 32, width), grad_blocks, vec_blocks)
    values = lax.all_gather(solved, "far", tiled=True)
    corrections = back(chosen, gathered, values).reshape(team, tiles, 8, width)
    pieces = lax.all_to_all(corrections, TEAM, split_axis=0, concat_axis=0, tiled=True)
    return finish(smoothed_twice, pieces)


def solution(mesh):
    names = ("section", "far", "near", "core", "slab")
    sections, doms, slabs = (mesh.shape[name] for name in ("section", "dom", "slab"))
    shape = (sections, doms // CORES // NEAR, NEAR, CORES, slabs)
    inner = Mesh(mesh.devices.reshape(shape), names)
    rows, cols = P(names), P(None, names)
    placed = (
        cols, P(), P(), rows, rows, cols, cols, cols, rows, rows, rows, cols, cols, rows, rows,
    )
    return jax.shard_map(
        body, mesh=inner, in_specs=placed, out_specs=cols, check_vma=False
    )
```

```python
import functools

import jax
import jax.numpy as jnp
from jax import lax
from jax.experimental import pallas as pl
from jax.experimental.pallas import tpu as pltpu
from jax.sharding import Mesh, PartitionSpec as P

DAMPING = 0.7
CORES = 2
NEAR = 1
F32 = jnp.float32
BF16 = jnp.bfloat16
SMEM = pltpu.SMEM
VMEM = pltpu.VMEM

vmem_spec = pl.BlockSpec(memory_space=VMEM)
smem_spec = pl.BlockSpec(memory_space=SMEM)
any_spec = pl.BlockSpec(memory_space=pl.ANY)


def held(shape):
    return pltpu.VMEM(shape, F32)


def hold(x):
    return pltpu.with_memory_space_constraint(x, VMEM)


def split(x):
    high = x.astype(BF16)
    low = (x - high.astype(F32)).astype(BF16)
    return high, low


def dot_nt(a, b):
    return lax.dot_general(a, b, (((1,), (1,)), ((), ())), preferred_element_type=F32)


def product_nt(parts, matrix):
    count = parts.shape[0] // 2
    high, low = split(matrix)
    both = dot_nt(parts, high)
    return both[:count] + both[count:] + dot_nt(parts[:count], low)


def stacked(rows):
    high, low = split(rows)
    return jnp.concatenate([high, low], axis=0)


def pack_kernel(owner, slot, residual, tangents, ends, out):
    tiles, width = out.shape[0], out.shape[2]
    lanes = lax.broadcasted_iota(jnp.int32, (1, width), 1)
    row = jnp.zeros((1, width), jnp.int32)
    for t in range(tiles):
        row = jnp.where(lanes == t, owner[t] * 2 + slot[t], row)
    for t in range(tiles):
        part = slice(t * width, (t + 1) * width)
        out[t, 0:8, :] = residual[:, part]
        out[t, 8:11, :] = tangents[:, part]
        out[t, 11:13, :] = ends[:, part].astype(F32)
        out[t, 13:14, :] = row.astype(F32)


def pack(owner, slot, residual, tangents, ends):
    tiles = owner.shape[0]
    width = residual.shape[1] // tiles
    return pl.pallas_call(
        pack_kernel,
        out_shape=held((tiles, 16, width)),
        in_specs=[smem_spec, smem_spec, vmem_spec, vmem_spec, vmem_spec],
        out_specs=vmem_spec,
        name="pack",
    )(owner, slot, residual, tangents, ends)


def sums_kernel(where, gathered, sums, chosen, meta, sems, *, doms, stride, team, tiles, group):
    width = gathered.shape[2]
    copies = [
        pltpu.make_async_copy(gathered.at[q * tiles, pl.ds(8, 8), :], meta.at[q], sems.at[q])
        for q in range(team)
    ]
    for copy in copies:
        copy.start()
    sums[...] = jnp.zeros_like(sums)
    for copy in copies:
        copy.wait()
    mine = where[0]

    count = jnp.int32(0)
    for q in range(team):
        for t in range(tiles):
            dst = meta[q, 5, t].astype(jnp.int32)
            owner, slot = dst // 2, dst % 2
            section, dom = owner // doms, owner % doms
            z, core = dom // CORES, dom % CORES
            cls = (section * stride + z % stride) * CORES + core
            chosen[0, count + 1] = q * tiles + t
            chosen[1, count + 1] = (z // stride) * 2 + slot
            count = jnp.where(cls == mine, count + 1, count)
    chosen[0, 0] = count
    for extra in range(group):
        chosen[0, count + 1 + extra] = 0
        chosen[1, count + 1 + extra] = 0
    nodes = lax.broadcasted_iota(jnp.int32, (width, width), 0).astype(F32)

    def step(i, carry):
        for j in range(group):
            at = i * group + j + 1
            tile, local = chosen[0, at], chosen[1, at]
            rows = gathered[tile, 0:8, :] * jnp.where(at <= count, 1.0, 0.0)
            halves = 0.5 * gathered[tile, 8:11, :]
            at_a = (nodes == gathered[tile, 11:12, :]).astype(F32)
            at_b = (nodes == gathered[tile, 12:13, :]).astype(F32)
            plus = (at_a + at_b).astype(BF16)
            minus = (at_b - at_a).astype(BF16)
            vec = jnp.concatenate([halves[c : c + 1] * rows for c in range(3)], axis=0)
            total_vec = dot_nt(stacked(vec), plus)
            total_grad = dot_nt(stacked(rows), minus)
            sums[local, 0:8, :] += total_grad[:8] + total_grad[8:]
            sums[local, 8:32, :] += total_vec[:24] + total_vec[24:]
        return carry

    lax.fori_loop(0, (count + group - 1) // group, step, 0)


def node_sums(where, gathered, team, places, doms, stride):
    total, _, width = gathered.shape
    group = 4
    return pl.pallas_call(
        functools.partial(
            sums_kernel, doms=doms, stride=stride, team=team, tiles=total // team, group=group
        ),
        out_shape=(
            held((places, 32, width)),
            jax.ShapeDtypeStruct((2, total + 1 + group), jnp.int32),
        ),
        in_specs=[smem_spec, vmem_spec],
        out_specs=(vmem_spec, smem_spec),
        scratch_shapes=[
            SMEM((team, 8, width), F32),
            pltpu.SemaphoreType.DMA((team,)),
        ],
        name="node_sums",
    )(where, hold(gathered))


def solve_kernel(arrived, grad, vec, out):
    count = arrived.shape[0]
    for n in range(grad.shape[0]):
        rows = arrived[0, n]
        for z in range(1, count):
            rows = rows + arrived[z, n]
        out[n, 0:8, :] = product_nt(stacked(rows[:8]), grad[n])
        out[n, 8:32, :] = product_nt(stacked(rows[8:]), vec[n])


def solve(arrived, grad, vec):
    return pl.pallas_call(
        solve_kernel,
        out_shape=held(arrived.shape[1:]),
        in_specs=[vmem_spec] * 3,
        out_specs=vmem_spec,
        name="solve",
    )(hold(arrived), hold(grad), hold(vec))


def back_kernel(chosen, gathered, values, out):
    out[...] = jnp.zeros_like(out)
    width = gathered.shape[2]

    def pick(rows, index):
        return jnp.take_along_axis(rows, index, axis=1)

    def step(i, carry):
        tile, local = chosen[0, i + 1], chosen[1, i + 1]
        index_a = jnp.broadcast_to(gathered[tile, 11:12, :].astype(jnp.int32), (8, width))
        index_b = jnp.broadcast_to(gathered[tile, 12:13, :].astype(jnp.int32), (8, width))
        grad = values[local, 0:8, :]
        total = pick(grad, index_b) - pick(grad, index_a)
        for c in range(3):
            rows = values[local, 8 + 8 * c : 16 + 8 * c, :]
            half = 0.5 * gathered[tile, 8 + c : 9 + c, :]
            total = total + half * (pick(rows, index_a) + pick(rows, index_b))
        out[tile] = total
        return carry

    lax.fori_loop(0, chosen[0, 0], step, 0)


def back(chosen, gathered, values):
    total, _, width = gathered.shape
    return pl.pallas_call(
        back_kernel,
        out_shape=held((total, 8, width)),
        in_specs=[smem_spec, vmem_spec, vmem_spec],
        out_specs=vmem_spec,
        name="back",
    )(chosen, hold(gathered), hold(values))


def by_tile(ref, tiles, width):
    return jnp.concatenate([ref[:, t * width : (t + 1) * width] for t in range(tiles)], axis=0)


def smooth_kernel(kind, coeff, halo, residual, inverse, out, rim, work):
    tiles, _, width = out.shape
    parts = stacked(by_tile(residual, tiles, width))
    for k in range(inverse.shape[0]):
        work[k] = product_nt(parts, inverse[k]).reshape(tiles, 8, width)
    for t in range(tiles):
        out[t] = work[kind[t], t] / coeff[t]
    for h in range(rim.shape[0]):
        rim[h] = out[halo[h]]


def smooth(kind, coeff, halo, residual, inverse):
    tiles = kind.shape[0]
    kinds, width, _ = inverse.shape
    return pl.pallas_call(
        smooth_kernel,
        out_shape=(
            held((tiles, 8, width)),
            held((halo.shape[0], 8, width)),
        ),
        in_specs=[smem_spec] * 3 + [vmem_spec] * 2,
        out_specs=(vmem_spec, vmem_spec),
        scratch_shapes=[VMEM((kinds, tiles, 8, width), F32)],
        name="smooth_once",
    )(kind, coeff, halo, hold(residual), hold(inverse))


def again_kernel(
    kind, coeff, cols, kinds, coeffs, smoothed, low, high, residual, coupling, inverse, out, work, rest
):
    tiles, _, width = smoothed.shape
    sources = jnp.concatenate(
        [
            smoothed[...].reshape(tiles * 8, width),
            low[...].reshape(low.shape[0] * 8, width),
            high[...].reshape(high.shape[0] * 8, width),
        ],
        axis=0,
    )
    parts = stacked(sources)
    count = sources.shape[0] // 8
    for k in range(coupling.shape[0]):
        work[k] = product_nt(parts, coupling[k]).reshape(count, 8, width)
    for t in range(tiles):
        total = coeff[t] * work[kind[t], t]
        for m in range(cols.shape[0]):
            total = total + coeffs[m, t] * work[kinds[m, t], cols[m, t]]
        rest[t] = residual[:, t * width : (t + 1) * width] - total
    parts = stacked(rest[...].reshape(tiles * 8, width))
    for k in range(inverse.shape[0]):
        work[k, 0:tiles] = product_nt(parts, inverse[k]).reshape(tiles, 8, width)
    for t in range(tiles):
        out[t] = smoothed[t] + DAMPING * (work[kind[t], t] / coeff[t])


def smooth_again(kind, coeff, cols, kinds, coeffs, smoothed, low, high, residual, coupling, inverse):
    tiles, _, width = smoothed.shape
    count = tiles + low.shape[0] + high.shape[0]
    return pl.pallas_call(
        again_kernel,
        out_shape=held((tiles, 8, width)),
        in_specs=[smem_spec] * 5 + [vmem_spec] * 6,
        out_specs=vmem_spec,
        scratch_shapes=[
            VMEM((coupling.shape[0], count, 8, width), F32),
            VMEM((tiles, 8, width), F32),
        ],
        name="smooth_again",
    )(
        kind, coeff, cols, kinds, coeffs,
        hold(smoothed), hold(low), hold(high), hold(residual), hold(coupling), hold(inverse),
    )


def finish_kernel(smoothed, pieces, out):
    tiles, _, width = smoothed.shape
    for t in range(tiles):
        rows = pieces[0, t]
        for q in range(1, pieces.shape[0]):
            rows = rows + pieces[q, t]
        out[:, t * width : (t + 1) * width] = smoothed[t] + rows


def finish(smoothed, pieces):
    tiles, cases, width = smoothed.shape
    return pl.pallas_call(
        finish_kernel,
        out_shape=jax.ShapeDtypeStruct((cases, tiles * width), F32),
        in_specs=[vmem_spec] * 2,
        out_specs=vmem_spec,
        name="finish",
    )(hold(smoothed), hold(pieces))


TEAM = ("section", "near", "core")


def body(
    residual,
    coupling_tiles,
    inverse_tiles,
    diag_kind,
    diag_coeff,
    tile_cols,
    tile_kinds,
    tile_coeff,
    halo_rows,
    tile_owner,
    node_slot,
    edge_nodes,
    tangents,
    grad_blocks,
    vec_blocks,
):
    heights, stride, team = lax.axis_size("far"), lax.axis_size("near"), lax.axis_size(TEAM)
    node_tiles = grad_blocks.shape[0]
    tiles = diag_kind.shape[0]
    width = coupling_tiles.shape[1]
    where = lax.axis_index(TEAM).astype(jnp.int32).reshape(1)
    own = pack(tile_owner[:, 0], node_slot, residual, tangents, edge_nodes)
    gathered = lax.all_gather(own, TEAM, tiled=True)

    smoothed, rim = smooth(diag_kind, diag_coeff, halo_rows, residual, inverse_tiles)
    slabs = lax.axis_size("slab")
    low = lax.ppermute(rim, "slab", [(i, i + 1) for i in range(slabs - 1)])
    high = lax.ppermute(rim, "slab", [(i + 1, i) for i in range(slabs - 1)])

    doms = heights * stride * CORES
    sums, chosen = node_sums(where, gathered, team, heights * node_tiles, doms, stride)
    sums = sums.reshape(heights, node_tiles * 32, width)
    arrived = lax.all_to_all(sums, "far", split_axis=0, concat_axis=0, tiled=True)

    smoothed_twice = smooth_again(
        diag_kind, diag_coeff, tile_cols, tile_kinds, tile_coeff,
        smoothed, low, high, residual, coupling_tiles, inverse_tiles,
    )
    arrived, smoothed_twice = lax.optimization_barrier((arrived, smoothed_twice))

    solved = solve(arrived.reshape(heights, node_tiles, 32, width), grad_blocks, vec_blocks)
    values = lax.all_gather(solved, "far", tiled=True)
    corrections = back(chosen, gathered, values).reshape(team, tiles, 8, width)
    pieces = lax.all_to_all(corrections, TEAM, split_axis=0, concat_axis=0, tiled=True)
    return finish(smoothed_twice, pieces)


def solution(mesh):
    names = ("section", "far", "near", "core", "slab")
    sections, doms, slabs = (mesh.shape[name] for name in ("section", "dom", "slab"))
    shape = (sections, doms // CORES // NEAR, NEAR, CORES, slabs)
    inner = Mesh(mesh.devices.reshape(shape), names)
    rows, cols = P(names), P(None, names)
    placed = (
        cols, P(), P(), rows, rows, cols, cols, cols, rows, rows, rows, cols, cols, rows, rows,
    )
    return jax.shard_map(
        body, mesh=inner, in_specs=placed, out_specs=cols, check_vma=False
    )
```

```python
import functools

import jax
import jax.numpy as jnp
from jax import lax
from jax.experimental import pallas as pl
from jax.experimental.pallas import tpu as pltpu
from jax.sharding import Mesh, PartitionSpec as P

DAMPING = 0.7
CORES = 2
NEAR = 1
GROUP = 8
F32 = jnp.float32
BF16 = jnp.bfloat16
SMEM = pltpu.SMEM
VMEM = pltpu.VMEM

vmem_spec = pl.BlockSpec(memory_space=VMEM)
smem_spec = pl.BlockSpec(memory_space=SMEM)
any_spec = pl.BlockSpec(memory_space=pl.ANY)


def held(shape):
    return pltpu.VMEM(shape, F32)


def hold(x):
    return pltpu.with_memory_space_constraint(x, VMEM)


def split(x):
    high = x.astype(BF16)
    low = (x - high.astype(F32)).astype(BF16)
    return high, low


def dot_nt(a, b):
    return lax.dot_general(a, b, (((1,), (1,)), ((), ())), preferred_element_type=F32)


def product_nt(parts, matrix):
    count = parts.shape[0] // 2
    high, low = split(matrix)
    both = dot_nt(parts, high)
    return both[:count] + both[count:] + dot_nt(parts[:count], low)


def stacked(rows):
    high, low = split(rows)
    return jnp.concatenate([high, low], axis=0)


def parts_of(x, size):
    if size & (size - 1) == 0:
        return lax.shift_right_logical(x, jnp.int32(size.bit_length() - 1)), x & (size - 1)
    return x // size, x % size


def pack_kernel(owner, slot, residual, tangents, ends, out, *, doms, stride):
    tiles, width = out.shape[0], out.shape[2]
    lanes = lax.broadcasted_iota(jnp.int32, (1, width), 1)
    owners = jnp.zeros((1, width), jnp.int32)
    slots = jnp.zeros((1, width), jnp.int32)
    for t in range(tiles):
        owners = jnp.where(lanes == t, owner[t], owners)
        slots = jnp.where(lanes == t, slot[t], slots)
    section, dom = parts_of(owners, doms)
    z, core = parts_of(dom, CORES)
    far, near = parts_of(z, stride)
    for t in range(tiles):
        part = slice(t * width, (t + 1) * width)
        out[t, 0:8, :] = residual[:, part]
        out[t, 8:11, :] = tangents[:, part]
        out[t, 11:13, :] = ends[:, part].astype(F32)
    out[0, 13:14, :] = ((section * stride + near) * CORES + core).astype(F32)
    out[0, 14:15, :] = (far * 2 + slots).astype(F32)


def pack(owner, slot, residual, tangents, ends, doms, stride):
    tiles = owner.shape[0]
    width = residual.shape[1] // tiles
    return pl.pallas_call(
        functools.partial(pack_kernel, doms=doms, stride=stride),
        out_shape=held((tiles, 16, width)),
        in_specs=[smem_spec, smem_spec, vmem_spec, vmem_spec, vmem_spec],
        out_specs=vmem_spec,
        name="pack",
    )(owner, slot, residual, tangents, ends)


def sums_kernel(where, gathered, sums, chosen, meta, sems, *, team, tiles, group):
    width = gathered.shape[2]
    copies = [
        pltpu.make_async_copy(gathered.at[q * tiles, pl.ds(8, 8), :], meta.at[q], sems.at[q])
        for q in range(team)
    ]
    for copy in copies:
        copy.start()
    sums[...] = jnp.zeros_like(sums)
    for copy in copies:
        copy.wait()
    mine = where[0].astype(F32)

    count = jnp.int32(0)
    for q in range(team):
        for t in range(tiles):
            chosen[0, count + 1] = q * tiles + t
            chosen[1, count + 1] = meta[q, 6, t].astype(jnp.int32)
            count = count + (meta[q, 5, t] == mine).astype(jnp.int32)
    chosen[0, 0] = count
    last, place = chosen[0, count], chosen[1, count]
    for extra in range(group):
        chosen[0, count + 1 + extra] = last
        chosen[1, count + 1 + extra] = place
    nodes = lax.broadcasted_iota(jnp.int32, (width, width), 0).astype(F32)

    def step(i, carry):
        for j in range(group):
            at = i * group + j + 1
            tile, local = chosen[0, at], chosen[1, at]
            rows = gathered[tile, 0:8, :] * jnp.where(at <= count, 1.0, 0.0)
            halves = 0.5 * gathered[tile, 8:11, :]
            at_a = (nodes == gathered[tile, 11:12, :]).astype(F32)
            at_b = (nodes == gathered[tile, 12:13, :]).astype(F32)
            plus = (at_a + at_b).astype(BF16)
            minus = (at_b - at_a).astype(BF16)
            vec = jnp.concatenate([halves[c : c + 1] * rows for c in range(3)], axis=0)
            total_vec = dot_nt(stacked(vec), plus)
            total_grad = dot_nt(stacked(rows), minus)
            sums[local, 0:8, :] += total_grad[:8] + total_grad[8:]
            sums[local, 8:32, :] += total_vec[:24] + total_vec[24:]
        return carry

    lax.fori_loop(0, (count + group - 1) // group, step, 0)


def node_sums(where, gathered, team, places):
    total, _, width = gathered.shape
    return pl.pallas_call(
        functools.partial(sums_kernel, team=team, tiles=total // team, group=GROUP),
        out_shape=(
            held((places, 32, width)),
            jax.ShapeDtypeStruct((2, total + 1 + GROUP), jnp.int32),
        ),
        in_specs=[smem_spec, vmem_spec],
        out_specs=(vmem_spec, smem_spec),
        scratch_shapes=[
            SMEM((team, 8, width), F32),
            pltpu.SemaphoreType.DMA((team,)),
        ],
        name="node_sums",
    )(where, hold(gathered))


def solve_kernel(arrived, grad, vec, out):
    count = arrived.shape[0]
    for n in range(grad.shape[0]):
        rows = arrived[0, n]
        for z in range(1, count):
            rows = rows + arrived[z, n]
        out[n, 0:8, :] = product_nt(stacked(rows[:8]), grad[n])
        out[n, 8:32, :] = product_nt(stacked(rows[8:]), vec[n])


def solve(arrived, grad, vec):
    return pl.pallas_call(
        solve_kernel,
        out_shape=held(arrived.shape[1:]),
        in_specs=[vmem_spec] * 3,
        out_specs=vmem_spec,
        name="solve",
    )(hold(arrived), hold(grad), hold(vec))


def back_kernel(chosen, gathered, values, out):
    out[...] = jnp.zeros_like(out)
    width = gathered.shape[2]

    def pick(rows, index):
        return jnp.take_along_axis(rows, index, axis=1)

    def step(i, carry):
        for j in range(GROUP):
            at = i * GROUP + j + 1
            tile, local = chosen[0, at], chosen[1, at]
            index_a = jnp.broadcast_to(gathered[tile, 11:12, :].astype(jnp.int32), (8, width))
            index_b = jnp.broadcast_to(gathered[tile, 12:13, :].astype(jnp.int32), (8, width))
            grad = values[local, 0:8, :]
            total = pick(grad, index_b) - pick(grad, index_a)
            for c in range(3):
                rows = values[local, 8 + 8 * c : 16 + 8 * c, :]
                half = 0.5 * gathered[tile, 8 + c : 9 + c, :]
                total = total + half * (pick(rows, index_a) + pick(rows, index_b))
            out[tile] = total
        return carry

    lax.fori_loop(0, (chosen[0, 0] + GROUP - 1) // GROUP, step, 0)


def back(chosen, gathered, values):
    total, _, width = gathered.shape
    return pl.pallas_call(
        back_kernel,
        out_shape=held((total, 8, width)),
        in_specs=[smem_spec, vmem_spec, vmem_spec],
        out_specs=vmem_spec,
        name="back",
    )(chosen, hold(gathered), hold(values))


def by_tile(ref, tiles, width):
    return jnp.concatenate([ref[:, t * width : (t + 1) * width] for t in range(tiles)], axis=0)


def smooth_kernel(kind, coeff, halo, residual, inverse, out, rim, work):
    tiles, _, width = out.shape
    parts = stacked(by_tile(residual, tiles, width))
    for k in range(inverse.shape[0]):
        work[k] = product_nt(parts, inverse[k]).reshape(tiles, 8, width)
    for t in range(tiles):
        out[t] = work[kind[t], t] / coeff[t]
    for h in range(rim.shape[0]):
        rim[h] = out[halo[h]]


def smooth(kind, coeff, halo, residual, inverse):
    tiles = kind.shape[0]
    kinds, width, _ = inverse.shape
    return pl.pallas_call(
        smooth_kernel,
        out_shape=(
            held((tiles, 8, width)),
            held((halo.shape[0], 8, width)),
        ),
        in_specs=[smem_spec] * 3 + [vmem_spec] * 2,
        out_specs=(vmem_spec, vmem_spec),
        scratch_shapes=[VMEM((kinds, tiles, 8, width), F32)],
        name="smooth_once",
    )(kind, coeff, halo, hold(residual), hold(inverse))


def again_kernel(
    kind, coeff, cols, kinds, coeffs, smoothed, low, high, residual, coupling, inverse, out, work, rest
):
    tiles, _, width = smoothed.shape
    sources = jnp.concatenate(
        [
            smoothed[...].reshape(tiles * 8, width),
            low[...].reshape(low.shape[0] * 8, width),
            high[...].reshape(high.shape[0] * 8, width),
        ],
        axis=0,
    )
    parts = stacked(sources)
    count = sources.shape[0] // 8
    for k in range(coupling.shape[0]):
        work[k] = product_nt(parts, coupling[k]).reshape(count, 8, width)
    for t in range(tiles):
        total = coeff[t] * work[kind[t], t]
        for m in range(cols.shape[0]):
            total = total + coeffs[m, t] * work[kinds[m, t], cols[m, t]]
        rest[t] = residual[:, t * width : (t + 1) * width] - total
    parts = stacked(rest[...].reshape(tiles * 8, width))
    for k in range(inverse.shape[0]):
        work[k, 0:tiles] = product_nt(parts, inverse[k]).reshape(tiles, 8, width)
    for t in range(tiles):
        out[t] = smoothed[t] + DAMPING * (work[kind[t], t] / coeff[t])


def smooth_again(kind, coeff, cols, kinds, coeffs, smoothed, low, high, residual, coupling, inverse):
    tiles, _, width = smoothed.shape
    count = tiles + low.shape[0] + high.shape[0]
    return pl.pallas_call(
        again_kernel,
        out_shape=held((tiles, 8, width)),
        in_specs=[smem_spec] * 5 + [vmem_spec] * 6,
        out_specs=vmem_spec,
        scratch_shapes=[
            VMEM((coupling.shape[0], count, 8, width), F32),
            VMEM((tiles, 8, width), F32),
        ],
        name="smooth_again",
    )(
        kind, coeff, cols, kinds, coeffs,
        hold(smoothed), hold(low), hold(high), hold(residual), hold(coupling), hold(inverse),
    )


def finish_kernel(smoothed, pieces, out):
    tiles, _, width = smoothed.shape
    for t in range(tiles):
        rows = pieces[0, t]
        for q in range(1, pieces.shape[0]):
            rows = rows + pieces[q, t]
        out[:, t * width : (t + 1) * width] = smoothed[t] + rows


def finish(smoothed, pieces):
    tiles, cases, width = smoothed.shape
    return pl.pallas_call(
        finish_kernel,
        out_shape=jax.ShapeDtypeStruct((cases, tiles * width), F32),
        in_specs=[vmem_spec] * 2,
        out_specs=vmem_spec,
        name="finish",
    )(hold(smoothed), hold(pieces))


TEAM = ("section", "near", "core")


def body(
    residual,
    coupling_tiles,
    inverse_tiles,
    diag_kind,
    diag_coeff,
    tile_cols,
    tile_kinds,
    tile_coeff,
    halo_rows,
    tile_owner,
    node_slot,
    edge_nodes,
    tangents,
    grad_blocks,
    vec_blocks,
):
    heights, stride, team = lax.axis_size("far"), lax.axis_size("near"), lax.axis_size(TEAM)
    node_tiles = grad_blocks.shape[0]
    tiles = diag_kind.shape[0]
    width = coupling_tiles.shape[1]
    where = lax.axis_index(TEAM).astype(jnp.int32).reshape(1)
    doms = heights * stride * CORES
    own = pack(tile_owner[:, 0], node_slot, residual, tangents, edge_nodes, doms, stride)
    gathered = lax.all_gather(own, TEAM, tiled=True)

    smoothed, rim = smooth(diag_kind, diag_coeff, halo_rows, residual, inverse_tiles)
    slabs = lax.axis_size("slab")
    low = lax.ppermute(rim, "slab", [(i, i + 1) for i in range(slabs - 1)])
    high = lax.ppermute(rim, "slab", [(i + 1, i) for i in range(slabs - 1)])

    sums, chosen = node_sums(where, gathered, team, heights * node_tiles)
    sums = sums.reshape(heights, node_tiles * 32, width)
    arrived = lax.all_to_all(sums, "far", split_axis=0, concat_axis=0, tiled=True)

    smoothed_twice = smooth_again(
        diag_kind, diag_coeff, tile_cols, tile_kinds, tile_coeff,
        smoothed, low, high, residual, coupling_tiles, inverse_tiles,
    )
    arrived, smoothed_twice = lax.optimization_barrier((arrived, smoothed_twice))

    solved = solve(arrived.reshape(heights, node_tiles, 32, width), grad_blocks, vec_blocks)
    values = lax.all_gather(solved, "far", tiled=True)
    corrections = back(chosen, gathered, values).reshape(team, tiles, 8, width)
    pieces = lax.all_to_all(corrections, TEAM, split_axis=0, concat_axis=0, tiled=True)
    return finish(smoothed_twice, pieces)


def solution(mesh):
    names = ("section", "far", "near", "core", "slab")
    sections, doms, slabs = (mesh.shape[name] for name in ("section", "dom", "slab"))
    shape = (sections, doms // CORES // NEAR, NEAR, CORES, slabs)
    inner = Mesh(mesh.devices.reshape(shape), names)
    rows, cols = P(names), P(None, names)
    placed = (
        cols, P(), P(), rows, rows, cols, cols, cols, rows, rows, rows, cols, cols, rows, rows,
    )
    return jax.shard_map(
        body, mesh=inner, in_specs=placed, out_specs=cols, check_vma=False
    )
```

```python
import functools

import jax
import jax.numpy as jnp
from jax import lax
from jax.experimental import pallas as pl
from jax.experimental.pallas import tpu as pltpu
from jax.sharding import Mesh, PartitionSpec as P

DAMPING = 0.7
CORES = 2
NEAR = 1
GROUP = 8
F32 = jnp.float32
BF16 = jnp.bfloat16
SMEM = pltpu.SMEM
VMEM = pltpu.VMEM

vmem_spec = pl.BlockSpec(memory_space=VMEM)
smem_spec = pl.BlockSpec(memory_space=SMEM)
any_spec = pl.BlockSpec(memory_space=pl.ANY)


def held(shape):
    return pltpu.VMEM(shape, F32)


def hold(x):
    return pltpu.with_memory_space_constraint(x, VMEM)


def split(x):
    high = x.astype(BF16)
    low = (x - high.astype(F32)).astype(BF16)
    return high, low


def dot_nt(a, b):
    return lax.dot_general(a, b, (((1,), (1,)), ((), ())), preferred_element_type=F32)


def product_nt(parts, matrix):
    count = parts.shape[0] // 2
    high, low = split(matrix)
    both = dot_nt(parts, high)
    return both[:count] + both[count:] + dot_nt(parts[:count], low)


def stacked(rows):
    high, low = split(rows)
    return jnp.concatenate([high, low], axis=0)


def parts_of(x, size):
    if size & (size - 1) == 0:
        return lax.shift_right_logical(x, jnp.int32(size.bit_length() - 1)), x & (size - 1)
    return x // size, x % size


FIELDS = 5


def pack_kernel(owner, slot, residual, tangents, ends, out, *, doms, stride):
    tiles = owner.shape[0]
    width = residual.shape[1] // tiles
    lanes = lax.broadcasted_iota(jnp.int32, (1, width), 1)
    owners = jnp.zeros((1, width), jnp.int32)
    slots = jnp.zeros((1, width), jnp.int32)
    for t in range(tiles):
        owners = jnp.where(lanes == t, owner[t], owners)
        slots = jnp.where(lanes == t, slot[t], slots)
    section, dom = parts_of(owners, doms)
    z, core = parts_of(dom, CORES)
    far, near = parts_of(z, stride)
    out[:, 0 : tiles * width] = residual[...]
    for t in range(tiles):
        part = slice(t * width, (t + 1) * width)
        for f in range(FIELDS):
            row = tangents[f : f + 1, part] if f < 3 else ends[f - 3 : f - 2, part].astype(F32)
            at = (tiles + (t // 8) * FIELDS + f) * width
            out[t % 8 : t % 8 + 1, at : at + width] = row
    at = (tiles + tiles // 8 * FIELDS) * width
    out[:, at : at + width] = jnp.zeros((8, width), F32)
    out[0:1, at : at + width] = ((section * stride + near) * CORES + core).astype(F32)
    out[1:2, at : at + width] = (far * 2 + slots).astype(F32)


def pack(owner, slot, residual, tangents, ends, doms, stride):
    tiles = owner.shape[0]
    width = residual.shape[1] // tiles
    return pl.pallas_call(
        functools.partial(pack_kernel, doms=doms, stride=stride),
        out_shape=held((8, (tiles + tiles // 8 * FIELDS + 1) * width)),
        in_specs=[smem_spec, smem_spec, vmem_spec, vmem_spec, vmem_spec],
        out_specs=vmem_spec,
        name="pack",
    )(owner, slot, residual, tangents, ends)


def tile_reader(gathered, tile, tiles, width):
    device, t = parts_of(tile, tiles)
    block, row = parts_of(t, 8)
    base = tiles + block * FIELDS

    def lanes(at):
        return pl.ds(pl.multiple_of(at * width, width), width)

    return (
        lambda: gathered[device, :, lanes(t)],
        lambda f: pltpu.roll(gathered[device, :, lanes(base + f)], 8 - row, 0)[0:1],
    )


def sums_kernel(where, gathered, sums, chosen, *, tiles, width, group):
    sums[...] = jnp.zeros_like(sums)
    mine = where[0].astype(F32)
    count = jnp.int32(0)
    for q in range(gathered.shape[0]):
        last_block = gathered[q, :, gathered.shape[2] - width :]
        codes = jnp.where(last_block[0:1] == mine, last_block[1:2], -1.0).astype(jnp.int32)
        for t in range(tiles):
            code = codes[0, t]
            chosen[0, count + 1] = q * tiles + t
            chosen[1, count + 1] = code
            count = count + (code >= 0).astype(jnp.int32)
    chosen[0, 0] = count
    last, place = chosen[0, count], chosen[1, count]
    for extra in range(group):
        chosen[0, count + 1 + extra] = last
        chosen[1, count + 1 + extra] = place
    nodes = lax.broadcasted_iota(jnp.int32, (width, width), 0).astype(F32)

    def step(i, carry):
        for j in range(group):
            at = i * group + j + 1
            tile, local = chosen[0, at], chosen[1, at]
            residual, field = tile_reader(gathered, tile, tiles, width)
            rows = residual() * jnp.where(at <= count, 1.0, 0.0)
            at_a = (nodes == field(3)).astype(F32)
            at_b = (nodes == field(4)).astype(F32)
            plus = (at_a + at_b).astype(BF16)
            minus = (at_b - at_a).astype(BF16)
            vec = jnp.concatenate([(0.5 * field(c)) * rows for c in range(3)], axis=0)
            total_vec = dot_nt(stacked(vec), plus)
            total_grad = dot_nt(stacked(rows), minus)
            sums[local, 0:8, :] += total_grad[:8] + total_grad[8:]
            sums[local, 8:32, :] += total_vec[:24] + total_vec[24:]
        return carry

    lax.fori_loop(0, (count + group - 1) // group, step, 0)


def node_sums(where, gathered, tiles, width, places):
    total = gathered.shape[0] * tiles
    return pl.pallas_call(
        functools.partial(sums_kernel, tiles=tiles, width=width, group=GROUP),
        out_shape=(
            held((places, 32, width)),
            jax.ShapeDtypeStruct((2, total + 1 + GROUP), jnp.int32),
        ),
        in_specs=[smem_spec, vmem_spec],
        out_specs=(vmem_spec, smem_spec),
        name="node_sums",
    )(where, hold(gathered))


def solve_kernel(arrived, grad, vec, out):
    count = arrived.shape[0]
    for n in range(grad.shape[0]):
        rows = arrived[0, n]
        for z in range(1, count):
            rows = rows + arrived[z, n]
        out[n, 0:8, :] = product_nt(stacked(rows[:8]), grad[n])
        out[n, 8:32, :] = product_nt(stacked(rows[8:]), vec[n])


def solve(arrived, grad, vec):
    return pl.pallas_call(
        solve_kernel,
        out_shape=held(arrived.shape[1:]),
        in_specs=[vmem_spec] * 3,
        out_specs=vmem_spec,
        name="solve",
    )(hold(arrived), hold(grad), hold(vec))


def back_kernel(chosen, gathered, values, out):
    out[...] = jnp.zeros_like(out)
    total, _, width = out.shape

    def pick(rows, index):
        return jnp.take_along_axis(rows, index, axis=1)

    def step(i, carry):
        for j in range(GROUP):
            at = i * GROUP + j + 1
            tile, local = chosen[0, at], chosen[1, at]
            _, field = tile_reader(gathered, tile, total // gathered.shape[0], width)
            index_a = jnp.broadcast_to(field(3).astype(jnp.int32), (8, width))
            index_b = jnp.broadcast_to(field(4).astype(jnp.int32), (8, width))
            grad = values[local, 0:8, :]
            found = pick(grad, index_b) - pick(grad, index_a)
            for c in range(3):
                rows = values[local, 8 + 8 * c : 16 + 8 * c, :]
                half = 0.5 * field(c)
                found = found + half * (pick(rows, index_a) + pick(rows, index_b))
            out[tile] = found
        return carry

    lax.fori_loop(0, (chosen[0, 0] + GROUP - 1) // GROUP, step, 0)


def back(chosen, gathered, values, tiles):
    width = values.shape[2]
    return pl.pallas_call(
        back_kernel,
        out_shape=held((gathered.shape[0] * tiles, 8, width)),
        in_specs=[smem_spec, vmem_spec, vmem_spec],
        out_specs=vmem_spec,
        name="back",
    )(chosen, hold(gathered), hold(values))


def by_tile(ref, tiles, width):
    return jnp.concatenate([ref[:, t * width : (t + 1) * width] for t in range(tiles)], axis=0)


def smooth_kernel(kind, coeff, halo, residual, inverse, out, rim, work):
    tiles, _, width = out.shape
    parts = stacked(by_tile(residual, tiles, width))
    for k in range(inverse.shape[0]):
        work[k] = product_nt(parts, inverse[k]).reshape(tiles, 8, width)
    for t in range(tiles):
        out[t] = work[kind[t], t] / coeff[t]
    for h in range(rim.shape[0]):
        rim[h] = out[halo[h]]


def smooth(kind, coeff, halo, residual, inverse):
    tiles = kind.shape[0]
    kinds, width, _ = inverse.shape
    return pl.pallas_call(
        smooth_kernel,
        out_shape=(
            held((tiles, 8, width)),
            held((halo.shape[0], 8, width)),
        ),
        in_specs=[smem_spec] * 3 + [vmem_spec] * 2,
        out_specs=(vmem_spec, vmem_spec),
        scratch_shapes=[VMEM((kinds, tiles, 8, width), F32)],
        name="smooth_once",
    )(kind, coeff, halo, hold(residual), hold(inverse))


def again_kernel(
    kind, coeff, cols, kinds, coeffs, smoothed, low, high, residual, coupling, inverse, out, work, rest
):
    tiles, _, width = smoothed.shape
    sources = jnp.concatenate(
        [
            smoothed[...].reshape(tiles * 8, width),
            low[...].reshape(low.shape[0] * 8, width),
            high[...].reshape(high.shape[0] * 8, width),
        ],
        axis=0,
    )
    parts = stacked(sources)
    count = sources.shape[0] // 8
    for k in range(coupling.shape[0]):
        work[k] = product_nt(parts, coupling[k]).reshape(count, 8, width)
    for t in range(tiles):
        total = coeff[t] * work[kind[t], t]
        for m in range(cols.shape[0]):
            total = total + coeffs[m, t] * work[kinds[m, t], cols[m, t]]
        rest[t] = residual[:, t * width : (t + 1) * width] - total
    parts = stacked(rest[...].reshape(tiles * 8, width))
    for k in range(inverse.shape[0]):
        work[k, 0:tiles] = product_nt(parts, inverse[k]).reshape(tiles, 8, width)
    for t in range(tiles):
        out[t] = smoothed[t] + DAMPING * (work[kind[t], t] / coeff[t])


def smooth_again(kind, coeff, cols, kinds, coeffs, smoothed, low, high, residual, coupling, inverse):
    tiles, _, width = smoothed.shape
    count = tiles + low.shape[0] + high.shape[0]
    return pl.pallas_call(
        again_kernel,
        out_shape=held((tiles, 8, width)),
        in_specs=[smem_spec] * 5 + [vmem_spec] * 6,
        out_specs=vmem_spec,
        scratch_shapes=[
            VMEM((coupling.shape[0], count, 8, width), F32),
            VMEM((tiles, 8, width), F32),
        ],
        name="smooth_again",
    )(
        kind, coeff, cols, kinds, coeffs,
        hold(smoothed), hold(low), hold(high), hold(residual), hold(coupling), hold(inverse),
    )


def finish_kernel(smoothed, pieces, out):
    tiles, _, width = smoothed.shape
    for t in range(tiles):
        rows = pieces[0, t]
        for q in range(1, pieces.shape[0]):
            rows = rows + pieces[q, t]
        out[:, t * width : (t + 1) * width] = smoothed[t] + rows


def finish(smoothed, pieces):
    tiles, cases, width = smoothed.shape
    return pl.pallas_call(
        finish_kernel,
        out_shape=jax.ShapeDtypeStruct((cases, tiles * width), F32),
        in_specs=[vmem_spec] * 2,
        out_specs=vmem_spec,
        name="finish",
    )(hold(smoothed), hold(pieces))


TEAM = ("section", "near", "core")


def body(
    residual,
    coupling_tiles,
    inverse_tiles,
    diag_kind,
    diag_coeff,
    tile_cols,
    tile_kinds,
    tile_coeff,
    halo_rows,
    tile_owner,
    node_slot,
    edge_nodes,
    tangents,
    grad_blocks,
    vec_blocks,
):
    heights, stride, team = lax.axis_size("far"), lax.axis_size("near"), lax.axis_size(TEAM)
    node_tiles = grad_blocks.shape[0]
    tiles = diag_kind.shape[0]
    width = coupling_tiles.shape[1]
    where = lax.axis_index(TEAM).astype(jnp.int32).reshape(1)
    doms = heights * stride * CORES
    own = pack(tile_owner[:, 0], node_slot, residual, tangents, edge_nodes, doms, stride)
    gathered = lax.all_gather(own, TEAM)

    smoothed, rim = smooth(diag_kind, diag_coeff, halo_rows, residual, inverse_tiles)
    slabs = lax.axis_size("slab")
    low = lax.ppermute(rim, "slab", [(i, i + 1) for i in range(slabs - 1)])
    high = lax.ppermute(rim, "slab", [(i + 1, i) for i in range(slabs - 1)])

    sums, chosen = node_sums(where, gathered, tiles, width, heights * node_tiles)
    sums = sums.reshape(heights, node_tiles * 32, width)
    arrived = lax.all_to_all(sums, "far", split_axis=0, concat_axis=0, tiled=True)

    smoothed_twice = smooth_again(
        diag_kind, diag_coeff, tile_cols, tile_kinds, tile_coeff,
        smoothed, low, high, residual, coupling_tiles, inverse_tiles,
    )
    arrived, smoothed_twice = lax.optimization_barrier((arrived, smoothed_twice))

    solved = solve(arrived.reshape(heights, node_tiles, 32, width), grad_blocks, vec_blocks)
    values = lax.all_gather(solved, "far", tiled=True)
    corrections = back(chosen, gathered, values, tiles).reshape(team, tiles, 8, width)
    pieces = lax.all_to_all(corrections, TEAM, split_axis=0, concat_axis=0, tiled=True)
    return finish(smoothed_twice, pieces)


def solution(mesh):
    names = ("section", "far", "near", "core", "slab")
    sections, doms, slabs = (mesh.shape[name] for name in ("section", "dom", "slab"))
    shape = (sections, doms // CORES // NEAR, NEAR, CORES, slabs)
    inner = Mesh(mesh.devices.reshape(shape), names)
    rows, cols = P(names), P(None, names)
    placed = (
        cols, P(), P(), rows, rows, cols, cols, cols, rows, rows, rows, cols, cols, rows, rows,
    )
    return jax.shard_map(
        body, mesh=inner, in_specs=placed, out_specs=cols, check_vma=False
    )
```

```python
import functools

import jax
import jax.numpy as jnp
from jax import lax
from jax.experimental import pallas as pl
from jax.experimental.pallas import tpu as pltpu
from jax.sharding import Mesh, PartitionSpec as P

DAMPING = 0.7
CORES = 2
NEAR = 2
GROUP = 8
F32 = jnp.float32
BF16 = jnp.bfloat16
SMEM = pltpu.SMEM
VMEM = pltpu.VMEM

vmem_spec = pl.BlockSpec(memory_space=VMEM)
smem_spec = pl.BlockSpec(memory_space=SMEM)
any_spec = pl.BlockSpec(memory_space=pl.ANY)


def held(shape):
    return pltpu.VMEM(shape, F32)


def hold(x):
    return pltpu.with_memory_space_constraint(x, VMEM)


def split(x):
    high = x.astype(BF16)
    low = (x - high.astype(F32)).astype(BF16)
    return high, low


def dot_nt(a, b):
    return lax.dot_general(a, b, (((1,), (1,)), ((), ())), preferred_element_type=F32)


def product_nt(parts, matrix):
    count = parts.shape[0] // 2
    high, low = split(matrix)
    both = dot_nt(parts, high)
    return both[:count] + both[count:] + dot_nt(parts[:count], low)


def stacked(rows):
    high, low = split(rows)
    return jnp.concatenate([high, low], axis=0)


def parts_of(x, size):
    if size & (size - 1) == 0:
        return lax.shift_right_logical(x, jnp.int32(size.bit_length() - 1)), x & (size - 1)
    return x // size, x % size


FIELDS = 5


def pack_kernel(owner, slot, residual, tangents, ends, out, *, doms):
    tiles = owner.shape[0]
    width = residual.shape[1] // tiles
    lanes = lax.broadcasted_iota(jnp.int32, (1, width), 1)
    owners = jnp.zeros((1, width), jnp.int32)
    slots = jnp.zeros((1, width), jnp.int32)
    for t in range(tiles):
        owners = jnp.where(lanes == t, owner[t], owners)
        slots = jnp.where(lanes == t, slot[t], slots)
    section, dom = parts_of(owners, doms)
    z, core = parts_of(dom, CORES)
    out[:, 0 : tiles * width] = residual[...]
    for t in range(tiles):
        part = slice(t * width, (t + 1) * width)
        for f in range(FIELDS):
            row = tangents[f : f + 1, part] if f < 3 else ends[f - 3 : f - 2, part].astype(F32)
            at = (tiles + (t // 8) * FIELDS + f) * width
            out[t % 8 : t % 8 + 1, at : at + width] = row
    at = (tiles + tiles // 8 * FIELDS) * width
    out[:, at : at + width] = jnp.zeros((8, width), F32)
    out[0:1, at : at + width] = (section * CORES + core).astype(F32)
    out[1:2, at : at + width] = (z * 2 + slots).astype(F32)


def pack(owner, slot, residual, tangents, ends, doms):
    tiles = owner.shape[0]
    width = residual.shape[1] // tiles
    return pl.pallas_call(
        functools.partial(pack_kernel, doms=doms),
        out_shape=held((8, (tiles + tiles // 8 * FIELDS + 1) * width)),
        in_specs=[smem_spec, smem_spec, vmem_spec, vmem_spec, vmem_spec],
        out_specs=vmem_spec,
        name="pack",
    )(owner, slot, residual, tangents, ends)


def tile_reader(gathered, tile, tiles, width):
    device, t = parts_of(tile, tiles)
    block, row = parts_of(t, 8)
    base = tiles + block * FIELDS

    def lanes(at):
        return pl.ds(pl.multiple_of(at * width, width), width)

    return (
        lambda: gathered[device, :, lanes(t)],
        lambda f: pltpu.roll(gathered[device, :, lanes(base + f)], 8 - row, 0)[0:1],
    )


def choose(chosen, gathered, tiles, width, rule):
    count = jnp.int32(0)
    for q in range(gathered.shape[0]):
        block = gathered[q, :, gathered.shape[2] - width :]
        codes = rule(block[0:1], block[1:2].astype(jnp.int32))
        for t in range(tiles):
            code = codes[0, t]
            chosen[0, count + 1] = q * tiles + t
            chosen[1, count + 1] = code
            count = count + (code >= 0).astype(jnp.int32)
    chosen[0, 0] = count
    last, place = chosen[0, count], chosen[1, count]
    for extra in range(GROUP):
        chosen[0, count + 1 + extra] = last
        chosen[1, count + 1 + extra] = place
    return count


def sums_kernel(where, own, other, sums, chosen_own, chosen_other, *, tiles, width):
    sums[...] = jnp.zeros_like(sums)
    mine, near = where[0].astype(F32), where[1]

    def rule(classes, places):
        fits = (classes == mine) & (((places >> 1) & (NEAR - 1)) == near)
        return jnp.where(fits, (places >> NEAR) * 2 + (places & 1), -1)

    nodes = lax.broadcasted_iota(jnp.int32, (width, width), 0).astype(F32)
    counts = [
        choose(chosen, gathered, tiles, width, rule)
        for chosen, gathered in ((chosen_own, own), (chosen_other, other))
    ]
    for count, chosen, gathered in zip(counts, (chosen_own, chosen_other), (own, other)):

        def step(i, carry, count=count, chosen=chosen, gathered=gathered):
            for j in range(GROUP):
                at = i * GROUP + j + 1
                tile, local = chosen[0, at], chosen[1, at]
                residual, field = tile_reader(gathered, tile, tiles, width)
                rows = residual() * jnp.where(at <= count, 1.0, 0.0)
                at_a = (nodes == field(3)).astype(F32)
                at_b = (nodes == field(4)).astype(F32)
                plus = (at_a + at_b).astype(BF16)
                minus = (at_b - at_a).astype(BF16)
                vec = jnp.concatenate([(0.5 * field(c)) * rows for c in range(3)], axis=0)
                total_vec = dot_nt(stacked(vec), plus)
                total_grad = dot_nt(stacked(rows), minus)
                sums[local, 0:8, :] += total_grad[:8] + total_grad[8:]
                sums[local, 8:32, :] += total_vec[:24] + total_vec[24:]
            return carry

        lax.fori_loop(0, (count + GROUP - 1) // GROUP, step, 0)


def list_shape(gathered, tiles):
    return (2, gathered.shape[0] * tiles + 1 + GROUP)


def node_sums(where, own, other, tiles, width, places):
    return pl.pallas_call(
        functools.partial(sums_kernel, tiles=tiles, width=width),
        out_shape=held((places, 32, width)),
        in_specs=[smem_spec, vmem_spec, vmem_spec],
        out_specs=vmem_spec,
        scratch_shapes=[SMEM(list_shape(own, tiles), jnp.int32) for _ in range(2)],
        name="node_sums",
    )(where, hold(own), hold(other))


def list_kernel(where, gathered, chosen, *, tiles, width):
    mine = where[0].astype(F32)
    choose(
        chosen, gathered, tiles, width, lambda classes, places: jnp.where(classes == mine, places, -1)
    )


def class_list(where, gathered, tiles, width):
    return pl.pallas_call(
        functools.partial(list_kernel, tiles=tiles, width=width),
        out_shape=jax.ShapeDtypeStruct(list_shape(gathered, tiles), jnp.int32),
        in_specs=[smem_spec, vmem_spec],
        out_specs=smem_spec,
        name="class_list",
    )(where, hold(gathered))


def solve_kernel(arrived, grad, vec, out):
    count = arrived.shape[0]
    for n in range(grad.shape[0]):
        rows = arrived[0, n]
        for z in range(1, count):
            rows = rows + arrived[z, n]
        out[n, 0:8, :] = product_nt(stacked(rows[:8]), grad[n])
        out[n, 8:32, :] = product_nt(stacked(rows[8:]), vec[n])


def solve(arrived, grad, vec):
    return pl.pallas_call(
        solve_kernel,
        out_shape=held(arrived.shape[1:]),
        in_specs=[vmem_spec] * 3,
        out_specs=vmem_spec,
        name="solve",
    )(hold(arrived), hold(grad), hold(vec))


def back_kernel(chosen, gathered, values, out):
    out[...] = jnp.zeros_like(out)
    total, _, width = out.shape

    def pick(rows, index):
        return jnp.take_along_axis(rows, index, axis=1)

    def step(i, carry):
        for j in range(GROUP):
            at = i * GROUP + j + 1
            tile, local = chosen[0, at], chosen[1, at]
            _, field = tile_reader(gathered, tile, total // gathered.shape[0], width)
            index_a = jnp.broadcast_to(field(3).astype(jnp.int32), (8, width))
            index_b = jnp.broadcast_to(field(4).astype(jnp.int32), (8, width))
            grad = values[local, 0:8, :]
            found = pick(grad, index_b) - pick(grad, index_a)
            for c in range(3):
                rows = values[local, 8 + 8 * c : 16 + 8 * c, :]
                half = 0.5 * field(c)
                found = found + half * (pick(rows, index_a) + pick(rows, index_b))
            out[tile] = found
        return carry

    lax.fori_loop(0, (chosen[0, 0] + GROUP - 1) // GROUP, step, 0)


def back(chosen, gathered, values, tiles):
    width = values.shape[2]
    return pl.pallas_call(
        back_kernel,
        out_shape=held((gathered.shape[0] * tiles, 8, width)),
        in_specs=[smem_spec, vmem_spec, vmem_spec],
        out_specs=vmem_spec,
        name="back",
    )(chosen, hold(gathered), hold(values))


def by_tile(ref, tiles, width):
    return jnp.concatenate([ref[:, t * width : (t + 1) * width] for t in range(tiles)], axis=0)


def smooth_kernel(kind, coeff, halo, residual, inverse, out, rim, work):
    tiles, _, width = out.shape
    parts = stacked(by_tile(residual, tiles, width))
    for k in range(inverse.shape[0]):
        work[k] = product_nt(parts, inverse[k]).reshape(tiles, 8, width)
    for t in range(tiles):
        out[t] = work[kind[t], t] / coeff[t]
    for h in range(rim.shape[0]):
        rim[h] = out[halo[h]]


def smooth(kind, coeff, halo, residual, inverse):
    tiles = kind.shape[0]
    kinds, width, _ = inverse.shape
    return pl.pallas_call(
        smooth_kernel,
        out_shape=(
            held((tiles, 8, width)),
            held((halo.shape[0], 8, width)),
        ),
        in_specs=[smem_spec] * 3 + [vmem_spec] * 2,
        out_specs=(vmem_spec, vmem_spec),
        scratch_shapes=[VMEM((kinds, tiles, 8, width), F32)],
        name="smooth_once",
    )(kind, coeff, halo, hold(residual), hold(inverse))


def again_kernel(
    kind, coeff, cols, kinds, coeffs, smoothed, low, high, residual, coupling, inverse, out, work, rest
):
    tiles, _, width = smoothed.shape
    sources = jnp.concatenate(
        [
            smoothed[...].reshape(tiles * 8, width),
            low[...].reshape(low.shape[0] * 8, width),
            high[...].reshape(high.shape[0] * 8, width),
        ],
        axis=0,
    )
    parts = stacked(sources)
    count = sources.shape[0] // 8
    for k in range(coupling.shape[0]):
        work[k] = product_nt(parts, coupling[k]).reshape(count, 8, width)
    for t in range(tiles):
        total = coeff[t] * work[kind[t], t]
        for m in range(cols.shape[0]):
            total = total + coeffs[m, t] * work[kinds[m, t], cols[m, t]]
        rest[t] = residual[:, t * width : (t + 1) * width] - total
    parts = stacked(rest[...].reshape(tiles * 8, width))
    for k in range(inverse.shape[0]):
        work[k, 0:tiles] = product_nt(parts, inverse[k]).reshape(tiles, 8, width)
    for t in range(tiles):
        out[t] = smoothed[t] + DAMPING * (work[kind[t], t] / coeff[t])


def smooth_again(kind, coeff, cols, kinds, coeffs, smoothed, low, high, residual, coupling, inverse):
    tiles, _, width = smoothed.shape
    count = tiles + low.shape[0] + high.shape[0]
    return pl.pallas_call(
        again_kernel,
        out_shape=held((tiles, 8, width)),
        in_specs=[smem_spec] * 5 + [vmem_spec] * 6,
        out_specs=vmem_spec,
        scratch_shapes=[
            VMEM((coupling.shape[0], count, 8, width), F32),
            VMEM((tiles, 8, width), F32),
        ],
        name="smooth_again",
    )(
        kind, coeff, cols, kinds, coeffs,
        hold(smoothed), hold(low), hold(high), hold(residual), hold(coupling), hold(inverse),
    )


def finish_kernel(smoothed, pieces, out):
    tiles, _, width = smoothed.shape
    for t in range(tiles):
        rows = pieces[0, t]
        for q in range(1, pieces.shape[0]):
            rows = rows + pieces[q, t]
        out[:, t * width : (t + 1) * width] = smoothed[t] + rows


def finish(smoothed, pieces):
    tiles, cases, width = smoothed.shape
    return pl.pallas_call(
        finish_kernel,
        out_shape=jax.ShapeDtypeStruct((cases, tiles * width), F32),
        in_specs=[vmem_spec] * 2,
        out_specs=vmem_spec,
        name="finish",
    )(hold(smoothed), hold(pieces))


TEAM = ("section", "core")
HEIGHT = ("far", "near")


def body(
    residual,
    coupling_tiles,
    inverse_tiles,
    diag_kind,
    diag_coeff,
    tile_cols,
    tile_kinds,
    tile_coeff,
    halo_rows,
    tile_owner,
    node_slot,
    edge_nodes,
    tangents,
    grad_blocks,
    vec_blocks,
):
    far, team = lax.axis_size("far"), lax.axis_size(TEAM)
    node_tiles = grad_blocks.shape[0]
    tiles = diag_kind.shape[0]
    width = coupling_tiles.shape[1]
    where = jnp.stack([lax.axis_index(TEAM), lax.axis_index("near")]).astype(jnp.int32)
    own = pack(tile_owner[:, 0], node_slot, residual, tangents, edge_nodes, far * NEAR * CORES)
    other = lax.ppermute(own, "near", [(0, 1), (1, 0)])
    gathered = lax.all_gather(own, TEAM)
    gathered_other = lax.all_gather(other, TEAM)

    smoothed, rim = smooth(diag_kind, diag_coeff, halo_rows, residual, inverse_tiles)
    slabs = lax.axis_size("slab")
    low = lax.ppermute(rim, "slab", [(i, i + 1) for i in range(slabs - 1)])
    high = lax.ppermute(rim, "slab", [(i + 1, i) for i in range(slabs - 1)])

    sums = node_sums(where, gathered, gathered_other, tiles, width, far * node_tiles)
    sums = sums.reshape(far, node_tiles * 32, width)
    arrived = lax.all_to_all(sums, "far", split_axis=0, concat_axis=0, tiled=True)

    chosen = class_list(where, gathered, tiles, width)
    smoothed_twice = smooth_again(
        diag_kind, diag_coeff, tile_cols, tile_kinds, tile_coeff,
        smoothed, low, high, residual, coupling_tiles, inverse_tiles,
    )
    arrived, smoothed_twice, chosen = lax.optimization_barrier((arrived, smoothed_twice, chosen))

    solved = solve(arrived.reshape(far, node_tiles, 32, width), grad_blocks, vec_blocks)
    values = lax.all_gather(solved, HEIGHT, tiled=True)
    corrections = back(chosen, gathered, values, tiles).reshape(team, tiles, 8, width)
    pieces = lax.all_to_all(corrections, TEAM, split_axis=0, concat_axis=0, tiled=True)
    return finish(smoothed_twice, pieces)


def solution(mesh):
    names = ("section", "far", "near", "core", "slab")
    sections, doms, slabs = (mesh.shape[name] for name in ("section", "dom", "slab"))
    shape = (sections, doms // CORES // NEAR, NEAR, CORES, slabs)
    inner = Mesh(mesh.devices.reshape(shape), names)
    rows, cols = P(names), P(None, names)
    placed = (
        cols, P(), P(), rows, rows, cols, cols, cols, rows, rows, rows, cols, cols, rows, rows,
    )
    return jax.shard_map(
        body, mesh=inner, in_specs=placed, out_specs=cols, check_vma=False
    )
```

```python
import functools

import jax
import jax.numpy as jnp
from jax import lax
from jax.experimental import pallas as pl
from jax.experimental.pallas import tpu as pltpu
from jax.sharding import Mesh, PartitionSpec as P

DAMPING = 0.7
CORES = 2
NEAR = 2
GROUP = 8
F32 = jnp.float32
BF16 = jnp.bfloat16
SMEM = pltpu.SMEM
VMEM = pltpu.VMEM

vmem_spec = pl.BlockSpec(memory_space=VMEM)
smem_spec = pl.BlockSpec(memory_space=SMEM)
any_spec = pl.BlockSpec(memory_space=pl.ANY)


def held(shape):
    return pltpu.VMEM(shape, F32)


def hold(x):
    return pltpu.with_memory_space_constraint(x, VMEM)


def split(x):
    high = x.astype(BF16)
    low = (x - high.astype(F32)).astype(BF16)
    return high, low


def dot_nt(a, b):
    return lax.dot_general(a, b, (((1,), (1,)), ((), ())), preferred_element_type=F32)


def product_nt(parts, matrix):
    count = parts.shape[0] // 2
    high, low = split(matrix)
    both = dot_nt(parts, high)
    return both[:count] + both[count:] + dot_nt(parts[:count], low)


def stacked(rows):
    high, low = split(rows)
    return jnp.concatenate([high, low], axis=0)


def parts_of(x, size):
    if size & (size - 1) == 0:
        return lax.shift_right_logical(x, jnp.int32(size.bit_length() - 1)), x & (size - 1)
    return x // size, x % size


FIELDS = 5


def pack_kernel(owner, slot, residual, tangents, ends, out, *, doms):
    tiles = owner.shape[0]
    width = residual.shape[1] // tiles
    lanes = lax.broadcasted_iota(jnp.int32, (1, width), 1)
    owners = jnp.zeros((1, width), jnp.int32)
    slots = jnp.zeros((1, width), jnp.int32)
    for t in range(tiles):
        owners = jnp.where(lanes == t, owner[t], owners)
        slots = jnp.where(lanes == t, slot[t], slots)
    section, dom = parts_of(owners, doms)
    z, core = parts_of(dom, CORES)
    out[:, 0 : tiles * width] = residual[...]
    for t in range(tiles):
        part = slice(t * width, (t + 1) * width)
        for f in range(FIELDS):
            row = tangents[f : f + 1, part] if f < 3 else ends[f - 3 : f - 2, part].astype(F32)
            at = (tiles + (t // 8) * FIELDS + f) * width
            out[t % 8 : t % 8 + 1, at : at + width] = row
    at = (tiles + tiles // 8 * FIELDS) * width
    out[:, at : at + width] = jnp.zeros((8, width), F32)
    out[0:1, at : at + width] = (section * CORES + core).astype(F32)
    out[1:2, at : at + width] = (z * 2 + slots).astype(F32)


def pack(owner, slot, residual, tangents, ends, doms):
    tiles = owner.shape[0]
    width = residual.shape[1] // tiles
    return pl.pallas_call(
        functools.partial(pack_kernel, doms=doms),
        out_shape=held((8, (tiles + tiles // 8 * FIELDS + 1) * width)),
        in_specs=[smem_spec, smem_spec, vmem_spec, vmem_spec, vmem_spec],
        out_specs=vmem_spec,
        name="pack",
    )(owner, slot, residual, tangents, ends)


def tile_reader(gathered, tile, tiles, width):
    device, t = parts_of(tile, tiles)
    block, row = parts_of(t, 8)
    base = tiles + block * FIELDS

    def lanes(at):
        return pl.ds(pl.multiple_of(at * width, width), width)

    return (
        lambda: gathered[device, :, lanes(t)],
        lambda f: pltpu.roll(gathered[device, :, lanes(base + f)], 8 - row, 0)[0:1],
    )


def choose(chosen, gathered, tiles, width, rule):
    count = jnp.int32(0)
    for q in range(gathered.shape[0]):
        block = gathered[q, :, gathered.shape[2] - width :]
        codes = rule(block[0:1], block[1:2].astype(jnp.int32))
        for t in range(tiles):
            code = codes[0, t]
            chosen[0, count + 1] = q * tiles + t
            chosen[1, count + 1] = code
            count = count + (code >= 0).astype(jnp.int32)
    chosen[0, 0] = count
    last, place = chosen[0, count], chosen[1, count]
    for extra in range(GROUP):
        chosen[0, count + 1 + extra] = last
        chosen[1, count + 1 + extra] = place
    return count


def sums_kernel(cls, parity, own, other, sums, chosen_own, chosen_other, *, tiles, width):
    sums[...] = jnp.zeros_like(sums)
    mine, near = cls[0].astype(F32), parity[0]

    def rule(classes, places):
        fits = (classes == mine) & (((places >> 1) & (NEAR - 1)) == near)
        return jnp.where(fits, (places >> NEAR) * 2 + (places & 1), -1)

    nodes = lax.broadcasted_iota(jnp.int32, (width, width), 0).astype(F32)
    counts = [
        choose(chosen, gathered, tiles, width, rule)
        for chosen, gathered in ((chosen_own, own), (chosen_other, other))
    ]
    for count, chosen, gathered in zip(counts, (chosen_own, chosen_other), (own, other)):

        def step(i, carry, count=count, chosen=chosen, gathered=gathered):
            for j in range(GROUP):
                at = i * GROUP + j + 1
                tile, local = chosen[0, at], chosen[1, at]
                residual, field = tile_reader(gathered, tile, tiles, width)
                rows = residual() * jnp.where(at <= count, 1.0, 0.0)
                at_a = (nodes == field(3)).astype(F32)
                at_b = (nodes == field(4)).astype(F32)
                plus = (at_a + at_b).astype(BF16)
                minus = (at_b - at_a).astype(BF16)
                vec = jnp.concatenate([(0.5 * field(c)) * rows for c in range(3)], axis=0)
                total_vec = dot_nt(stacked(vec), plus)
                total_grad = dot_nt(stacked(rows), minus)
                sums[local, 0:8, :] += total_grad[:8] + total_grad[8:]
                sums[local, 8:32, :] += total_vec[:24] + total_vec[24:]
            return carry

        lax.fori_loop(0, (count + GROUP - 1) // GROUP, step, 0)


def list_shape(gathered, tiles):
    return (2, gathered.shape[0] * tiles + 1 + GROUP)


def node_sums(cls, parity, own, other, tiles, width, places):
    return pl.pallas_call(
        functools.partial(sums_kernel, tiles=tiles, width=width),
        out_shape=held((places, 32, width)),
        in_specs=[smem_spec, smem_spec, vmem_spec, vmem_spec],
        out_specs=vmem_spec,
        scratch_shapes=[SMEM(list_shape(own, tiles), jnp.int32) for _ in range(2)],
        name="node_sums",
    )(cls, parity, hold(own), hold(other))


def solve_kernel(arrived, grad, vec, out):
    count = arrived.shape[0]
    for n in range(grad.shape[0]):
        rows = arrived[0, n]
        for z in range(1, count):
            rows = rows + arrived[z, n]
        out[n, 0:8, :] = product_nt(stacked(rows[:8]), grad[n])
        out[n, 8:32, :] = product_nt(stacked(rows[8:]), vec[n])


def solve(arrived, grad, vec):
    return pl.pallas_call(
        solve_kernel,
        out_shape=held(arrived.shape[1:]),
        in_specs=[vmem_spec] * 3,
        out_specs=vmem_spec,
        name="solve",
    )(hold(arrived), hold(grad), hold(vec))


def back_kernel(chosen, gathered, values, out):
    out[...] = jnp.zeros_like(out)
    total, _, width = out.shape

    def pick(rows, index):
        return jnp.take_along_axis(rows, index, axis=1)

    def step(i, carry):
        for j in range(GROUP):
            at = i * GROUP + j + 1
            tile, local = chosen[0, at], chosen[1, at]
            _, field = tile_reader(gathered, tile, total // gathered.shape[0], width)
            index_a = jnp.broadcast_to(field(3).astype(jnp.int32), (8, width))
            index_b = jnp.broadcast_to(field(4).astype(jnp.int32), (8, width))
            grad = values[local, 0:8, :]
            found = pick(grad, index_b) - pick(grad, index_a)
            for c in range(3):
                rows = values[local, 8 + 8 * c : 16 + 8 * c, :]
                half = 0.5 * field(c)
                found = found + half * (pick(rows, index_a) + pick(rows, index_b))
            out[tile] = found
        return carry

    lax.fori_loop(0, (chosen[0, 0] + GROUP - 1) // GROUP, step, 0)


def back(chosen, gathered, values, tiles):
    width = values.shape[2]
    return pl.pallas_call(
        back_kernel,
        out_shape=held((gathered.shape[0] * tiles, 8, width)),
        in_specs=[smem_spec, vmem_spec, vmem_spec],
        out_specs=vmem_spec,
        name="back",
    )(chosen, hold(gathered), hold(values))


def by_tile(ref, tiles, width):
    return jnp.concatenate([ref[:, t * width : (t + 1) * width] for t in range(tiles)], axis=0)


def smooth_kernel(kind, coeff, halo, residual, inverse, out, rim, work):
    tiles, _, width = out.shape
    parts = stacked(by_tile(residual, tiles, width))
    for k in range(inverse.shape[0]):
        work[k] = product_nt(parts, inverse[k]).reshape(tiles, 8, width)
    for t in range(tiles):
        out[t] = work[kind[t], t] / coeff[t]
    for h in range(rim.shape[0]):
        rim[h] = out[halo[h]]


def smooth(kind, coeff, halo, residual, inverse):
    tiles = kind.shape[0]
    kinds, width, _ = inverse.shape
    return pl.pallas_call(
        smooth_kernel,
        out_shape=(
            held((tiles, 8, width)),
            held((halo.shape[0], 8, width)),
        ),
        in_specs=[smem_spec] * 3 + [vmem_spec] * 2,
        out_specs=(vmem_spec, vmem_spec),
        scratch_shapes=[VMEM((kinds, tiles, 8, width), F32)],
        name="smooth_once",
    )(kind, coeff, halo, hold(residual), hold(inverse))


def again_kernel(
    kind, coeff, cols, kinds, coeffs, cls, smoothed, low, high, residual, coupling, inverse, gathered,
    out, chosen, work, rest,
):
    tiles, _, width = smoothed.shape
    mine = cls[0].astype(F32)
    choose(
        chosen, gathered, tiles, width, lambda classes, places: jnp.where(classes == mine, places, -1)
    )
    sources = jnp.concatenate(
        [
            smoothed[...].reshape(tiles * 8, width),
            low[...].reshape(low.shape[0] * 8, width),
            high[...].reshape(high.shape[0] * 8, width),
        ],
        axis=0,
    )
    parts = stacked(sources)
    count = sources.shape[0] // 8
    for k in range(coupling.shape[0]):
        work[k] = product_nt(parts, coupling[k]).reshape(count, 8, width)
    for t in range(tiles):
        total = coeff[t] * work[kind[t], t]
        for m in range(cols.shape[0]):
            total = total + coeffs[m, t] * work[kinds[m, t], cols[m, t]]
        rest[t] = residual[:, t * width : (t + 1) * width] - total
    parts = stacked(rest[...].reshape(tiles * 8, width))
    for k in range(inverse.shape[0]):
        work[k, 0:tiles] = product_nt(parts, inverse[k]).reshape(tiles, 8, width)
    for t in range(tiles):
        out[t] = smoothed[t] + DAMPING * (work[kind[t], t] / coeff[t])


def smooth_again(
    kind, coeff, cols, kinds, coeffs, smoothed, low, high, residual, coupling, inverse, cls, gathered
):
    tiles, _, width = smoothed.shape
    count = tiles + low.shape[0] + high.shape[0]
    return pl.pallas_call(
        again_kernel,
        out_shape=(
            held((tiles, 8, width)),
            jax.ShapeDtypeStruct(list_shape(gathered, tiles), jnp.int32),
        ),
        in_specs=[smem_spec] * 6 + [vmem_spec] * 7,
        out_specs=(vmem_spec, smem_spec),
        scratch_shapes=[
            VMEM((coupling.shape[0], count, 8, width), F32),
            VMEM((tiles, 8, width), F32),
        ],
        name="smooth_again",
    )(
        kind, coeff, cols, kinds, coeffs, cls,
        hold(smoothed), hold(low), hold(high), hold(residual), hold(coupling), hold(inverse),
        hold(gathered),
    )


def finish_kernel(smoothed, pieces, out):
    tiles, _, width = smoothed.shape
    for t in range(tiles):
        rows = pieces[0, t]
        for q in range(1, pieces.shape[0]):
            rows = rows + pieces[q, t]
        out[:, t * width : (t + 1) * width] = smoothed[t] + rows


def finish(smoothed, pieces):
    tiles, cases, width = smoothed.shape
    return pl.pallas_call(
        finish_kernel,
        out_shape=jax.ShapeDtypeStruct((cases, tiles * width), F32),
        in_specs=[vmem_spec] * 2,
        out_specs=vmem_spec,
        name="finish",
    )(hold(smoothed), hold(pieces))


TEAM = ("section", "core")
HEIGHT = ("far", "near")


def body(
    residual,
    coupling_tiles,
    inverse_tiles,
    diag_kind,
    diag_coeff,
    tile_cols,
    tile_kinds,
    tile_coeff,
    halo_rows,
    tile_owner,
    node_slot,
    edge_nodes,
    tangents,
    grad_blocks,
    vec_blocks,
):
    far, team = lax.axis_size("far"), lax.axis_size(TEAM)
    node_tiles = grad_blocks.shape[0]
    tiles = diag_kind.shape[0]
    width = coupling_tiles.shape[1]
    cls = lax.axis_index(TEAM).astype(jnp.int32).reshape(1)
    parity = lax.axis_index("near").astype(jnp.int32).reshape(1)
    own = pack(tile_owner[:, 0], node_slot, residual, tangents, edge_nodes, far * NEAR * CORES)
    other = lax.ppermute(own, "near", [(0, 1), (1, 0)])
    gathered = lax.all_gather(own, TEAM)
    gathered_other = lax.all_gather(other, TEAM)

    smoothed, rim = smooth(diag_kind, diag_coeff, halo_rows, residual, inverse_tiles)
    slabs = lax.axis_size("slab")
    low = lax.ppermute(rim, "slab", [(i, i + 1) for i in range(slabs - 1)])
    high = lax.ppermute(rim, "slab", [(i + 1, i) for i in range(slabs - 1)])

    sums = node_sums(cls, parity, gathered, gathered_other, tiles, width, far * node_tiles)
    sums = sums.reshape(far, node_tiles * 32, width)
    arrived = lax.all_to_all(sums, "far", split_axis=0, concat_axis=0, tiled=True)

    smoothed_twice, chosen = smooth_again(
        diag_kind, diag_coeff, tile_cols, tile_kinds, tile_coeff,
        smoothed, low, high, residual, coupling_tiles, inverse_tiles, cls, gathered,
    )
    arrived, smoothed_twice, chosen = lax.optimization_barrier((arrived, smoothed_twice, chosen))

    solved = solve(arrived.reshape(far, node_tiles, 32, width), grad_blocks, vec_blocks)
    values = lax.all_gather(solved, HEIGHT, tiled=True)
    corrections = back(chosen, gathered, values, tiles).reshape(team, tiles, 8, width)
    pieces = lax.all_to_all(corrections, TEAM, split_axis=0, concat_axis=0, tiled=True)
    return finish(smoothed_twice, pieces)


def solution(mesh):
    names = ("section", "far", "near", "core", "slab")
    sections, doms, slabs = (mesh.shape[name] for name in ("section", "dom", "slab"))
    shape = (sections, doms // CORES // NEAR, NEAR, CORES, slabs)
    inner = Mesh(mesh.devices.reshape(shape), names)
    rows, cols = P(names), P(None, names)
    placed = (
        cols, P(), P(), rows, rows, cols, cols, cols, rows, rows, rows, cols, cols, rows, rows,
    )
    return jax.shard_map(
        body, mesh=inner, in_specs=placed, out_specs=cols, check_vma=False
    )
```

```python
import functools

import jax
import jax.numpy as jnp
from jax import lax
from jax.experimental import pallas as pl
from jax.experimental.pallas import tpu as pltpu
from jax.sharding import Mesh, PartitionSpec as P

DAMPING = 0.7
CORES = 2
NEAR = 2
GROUP = 8
F32 = jnp.float32
BF16 = jnp.bfloat16
SMEM = pltpu.SMEM
VMEM = pltpu.VMEM

vmem_spec = pl.BlockSpec(memory_space=VMEM)
smem_spec = pl.BlockSpec(memory_space=SMEM)
any_spec = pl.BlockSpec(memory_space=pl.ANY)


def held(shape):
    return pltpu.VMEM(shape, F32)


def hold(x):
    return pltpu.with_memory_space_constraint(x, VMEM)


def split(x):
    high = x.astype(BF16)
    low = (x - high.astype(F32)).astype(BF16)
    return high, low


def dot_nt(a, b):
    return lax.dot_general(a, b, (((1,), (1,)), ((), ())), preferred_element_type=F32)


def product_nt(parts, matrix):
    count = parts.shape[0] // 2
    high, low = split(matrix)
    both = dot_nt(parts, high)
    return both[:count] + both[count:] + dot_nt(parts[:count], low)


def stacked(rows):
    high, low = split(rows)
    return jnp.concatenate([high, low], axis=0)


def parts_of(x, size):
    if size & (size - 1) == 0:
        return lax.shift_right_logical(x, jnp.int32(size.bit_length() - 1)), x & (size - 1)
    return x // size, x % size


FIELDS = 5


def pack_kernel(owner, slot, residual, tangents, ends, out, *, doms):
    tiles = owner.shape[0]
    width = residual.shape[1] // tiles
    lanes = lax.broadcasted_iota(jnp.int32, (1, width), 1)
    owners = jnp.zeros((1, width), jnp.int32)
    slots = jnp.zeros((1, width), jnp.int32)
    for t in range(tiles):
        owners = jnp.where(lanes == t, owner[t], owners)
        slots = jnp.where(lanes == t, slot[t], slots)
    section, dom = parts_of(owners, doms)
    z, core = parts_of(dom, CORES)
    out[:, 0 : tiles * width] = residual[...]
    for t in range(tiles):
        part = slice(t * width, (t + 1) * width)
        for f in range(FIELDS):
            row = tangents[f : f + 1, part] if f < 3 else ends[f - 3 : f - 2, part].astype(F32)
            at = (tiles + (t // 8) * FIELDS + f) * width
            out[t % 8 : t % 8 + 1, at : at + width] = row
    at = (tiles + tiles // 8 * FIELDS) * width
    out[:, at : at + width] = jnp.zeros((8, width), F32)
    out[0:1, at : at + width] = (section * CORES + core).astype(F32)
    out[1:2, at : at + width] = (z * 2 + slots).astype(F32)


def pack(owner, slot, residual, tangents, ends, doms):
    tiles = owner.shape[0]
    width = residual.shape[1] // tiles
    return pl.pallas_call(
        functools.partial(pack_kernel, doms=doms),
        out_shape=held((8, (tiles + tiles // 8 * FIELDS + 1) * width)),
        in_specs=[smem_spec, smem_spec, vmem_spec, vmem_spec, vmem_spec],
        out_specs=vmem_spec,
        name="pack",
    )(owner, slot, residual, tangents, ends)


def tile_reader(gathered, tile, tiles, width):
    device, t = parts_of(tile, tiles)
    block, row = parts_of(t, 8)
    base = tiles + block * FIELDS

    def lanes(at):
        return pl.ds(pl.multiple_of(at * width, width), width)

    return (
        lambda: gathered[device, :, lanes(t)],
        lambda f: pltpu.roll(gathered[device, :, lanes(base + f)], 8 - row, 0)[0:1],
    )


def choose(chosen, gathered, tiles, width, rule):
    count = jnp.int32(0)
    for q in range(gathered.shape[0]):
        block = gathered[q, :, gathered.shape[2] - width :]
        codes = rule(block[0:1], block[1:2].astype(jnp.int32))
        for t in range(tiles):
            code = codes[0, t]
            chosen[0, count + 1] = q * tiles + t
            chosen[1, count + 1] = code
            count = count + (code >= 0).astype(jnp.int32)
    chosen[0, 0] = count
    last, place = chosen[0, count], chosen[1, count]
    for extra in range(GROUP):
        chosen[0, count + 1 + extra] = last
        chosen[1, count + 1 + extra] = place
    return count


def sums_kernel(cls, parity, own, other, sums, chosen_own, chosen_other, *, tiles, width):
    sums[...] = jnp.zeros_like(sums)
    mine, near = cls[0].astype(F32), parity[0]

    def rule(classes, places):
        fits = (classes == mine) & (((places >> 1) & (NEAR - 1)) == near)
        return jnp.where(fits, (places >> NEAR) * 2 + (places & 1), -1)

    nodes = lax.broadcasted_iota(jnp.int32, (width, width), 0).astype(F32)
    counts = [
        choose(chosen, gathered, tiles, width, rule)
        for chosen, gathered in ((chosen_own, own), (chosen_other, other))
    ]
    for count, chosen, gathered in zip(counts, (chosen_own, chosen_other), (own, other)):

        def step(i, carry, count=count, chosen=chosen, gathered=gathered):
            for j in range(GROUP):
                at = i * GROUP + j + 1
                tile, local = chosen[0, at], chosen[1, at]
                residual, field = tile_reader(gathered, tile, tiles, width)
                rows = residual() * jnp.where(at <= count, 1.0, 0.0)
                at_a = (nodes == field(3)).astype(F32)
                at_b = (nodes == field(4)).astype(F32)
                plus = (at_a + at_b).astype(BF16)
                minus = (at_b - at_a).astype(BF16)
                vec = jnp.concatenate([(0.5 * field(c)) * rows for c in range(3)], axis=0)
                total_vec = dot_nt(stacked(vec), plus)
                total_grad = dot_nt(stacked(rows), minus)
                sums[local, 0:8, :] += total_grad[:8] + total_grad[8:]
                sums[local, 8:32, :] += total_vec[:24] + total_vec[24:]
            return carry

        lax.fori_loop(0, (count + GROUP - 1) // GROUP, step, 0)


def list_shape(gathered, tiles):
    return (2, gathered.shape[0] * tiles + 1 + GROUP)


def node_sums(cls, parity, own, other, tiles, width, places):
    return pl.pallas_call(
        functools.partial(sums_kernel, tiles=tiles, width=width),
        out_shape=held((places, 32, width)),
        in_specs=[smem_spec, smem_spec, vmem_spec, vmem_spec],
        out_specs=vmem_spec,
        scratch_shapes=[SMEM(list_shape(own, tiles), jnp.int32) for _ in range(2)],
        name="node_sums",
    )(cls, parity, hold(own), hold(other))


def list_kernel(cls, gathered, chosen, *, tiles, width):
    mine = cls[0].astype(F32)
    choose(
        chosen, gathered, tiles, width, lambda classes, places: jnp.where(classes == mine, places, -1)
    )


def class_list(cls, gathered, tiles, width):
    return pl.pallas_call(
        functools.partial(list_kernel, tiles=tiles, width=width),
        out_shape=jax.ShapeDtypeStruct(list_shape(gathered, tiles), jnp.int32),
        in_specs=[smem_spec, vmem_spec],
        out_specs=smem_spec,
        name="class_list",
    )(cls, hold(gathered))


def solve_kernel(arrived, grad, vec, out):
    count = arrived.shape[0]
    for n in range(grad.shape[0]):
        rows = arrived[0, n]
        for z in range(1, count):
            rows = rows + arrived[z, n]
        out[n, 0:8, :] = product_nt(stacked(rows[:8]), grad[n])
        out[n, 8:32, :] = product_nt(stacked(rows[8:]), vec[n])


def solve(arrived, grad, vec):
    return pl.pallas_call(
        solve_kernel,
        out_shape=held(arrived.shape[1:]),
        in_specs=[vmem_spec] * 3,
        out_specs=vmem_spec,
        name="solve",
    )(hold(arrived), hold(grad), hold(vec))


def back_kernel(chosen, gathered, values, out):
    out[...] = jnp.zeros_like(out)
    total, _, width = out.shape

    def pick(rows, index):
        return jnp.take_along_axis(rows, index, axis=1)

    def step(i, carry):
        for j in range(GROUP):
            at = i * GROUP + j + 1
            tile, local = chosen[0, at], chosen[1, at]
            _, field = tile_reader(gathered, tile, total // gathered.shape[0], width)
            index_a = jnp.broadcast_to(field(3).astype(jnp.int32), (8, width))
            index_b = jnp.broadcast_to(field(4).astype(jnp.int32), (8, width))
            grad = values[local, 0:8, :]
            found = pick(grad, index_b) - pick(grad, index_a)
            for c in range(3):
                rows = values[local, 8 + 8 * c : 16 + 8 * c, :]
                half = 0.5 * field(c)
                found = found + half * (pick(rows, index_a) + pick(rows, index_b))
            out[tile] = found
        return carry

    lax.fori_loop(0, (chosen[0, 0] + GROUP - 1) // GROUP, step, 0)


def back(chosen, gathered, values, tiles):
    width = values.shape[2]
    return pl.pallas_call(
        back_kernel,
        out_shape=held((gathered.shape[0] * tiles, 8, width)),
        in_specs=[smem_spec, vmem_spec, vmem_spec],
        out_specs=vmem_spec,
        name="back",
    )(chosen, hold(gathered), hold(values))


def by_tile(ref, tiles, width):
    return jnp.concatenate([ref[:, t * width : (t + 1) * width] for t in range(tiles)], axis=0)


def smooth_kernel(kind, coeff, halo, residual, inverse, out, rim, work):
    tiles, _, width = out.shape
    parts = stacked(by_tile(residual, tiles, width))
    for k in range(inverse.shape[0]):
        work[k] = product_nt(parts, inverse[k]).reshape(tiles, 8, width)
    for t in range(tiles):
        out[t] = work[kind[t], t] / coeff[t]
    for h in range(rim.shape[0]):
        rim[h] = out[halo[h]]


def smooth(kind, coeff, halo, residual, inverse):
    tiles = kind.shape[0]
    kinds, width, _ = inverse.shape
    return pl.pallas_call(
        smooth_kernel,
        out_shape=(
            held((tiles, 8, width)),
            held((halo.shape[0], 8, width)),
        ),
        in_specs=[smem_spec] * 3 + [vmem_spec] * 2,
        out_specs=(vmem_spec, vmem_spec),
        scratch_shapes=[VMEM((kinds, tiles, 8, width), F32)],
        name="smooth_once",
    )(kind, coeff, halo, hold(residual), hold(inverse))


def again_kernel(
    kind, coeff, cols, kinds, coeffs, smoothed, low, high, residual, coupling, inverse, out, work, rest
):
    tiles, _, width = smoothed.shape
    sources = jnp.concatenate(
        [
            smoothed[...].reshape(tiles * 8, width),
            low[...].reshape(low.shape[0] * 8, width),
            high[...].reshape(high.shape[0] * 8, width),
        ],
        axis=0,
    )
    parts = stacked(sources)
    count = sources.shape[0] // 8
    for k in range(coupling.shape[0]):
        work[k] = product_nt(parts, coupling[k]).reshape(count, 8, width)
    for t in range(tiles):
        total = coeff[t] * work[kind[t], t]
        for m in range(cols.shape[0]):
            total = total + coeffs[m, t] * work[kinds[m, t], cols[m, t]]
        rest[t] = residual[:, t * width : (t + 1) * width] - total
    parts = stacked(rest[...].reshape(tiles * 8, width))
    for k in range(inverse.shape[0]):
        work[k, 0:tiles] = product_nt(parts, inverse[k]).reshape(tiles, 8, width)
    for t in range(tiles):
        out[t] = smoothed[t] + DAMPING * (work[kind[t], t] / coeff[t])


def smooth_again(kind, coeff, cols, kinds, coeffs, smoothed, low, high, residual, coupling, inverse):
    tiles, _, width = smoothed.shape
    count = tiles + low.shape[0] + high.shape[0]
    return pl.pallas_call(
        again_kernel,
        out_shape=held((tiles, 8, width)),
        in_specs=[smem_spec] * 5 + [vmem_spec] * 6,
        out_specs=vmem_spec,
        scratch_shapes=[
            VMEM((coupling.shape[0], count, 8, width), F32),
            VMEM((tiles, 8, width), F32),
        ],
        name="smooth_again",
    )(
        kind, coeff, cols, kinds, coeffs,
        hold(smoothed), hold(low), hold(high), hold(residual), hold(coupling), hold(inverse),
    )


def finish_kernel(smoothed, pieces, out):
    tiles, _, width = smoothed.shape
    for t in range(tiles):
        rows = pieces[0, t]
        for q in range(1, pieces.shape[0]):
            rows = rows + pieces[q, t]
        out[:, t * width : (t + 1) * width] = smoothed[t] + rows


def finish(smoothed, pieces):
    tiles, cases, width = smoothed.shape
    return pl.pallas_call(
        finish_kernel,
        out_shape=jax.ShapeDtypeStruct((cases, tiles * width), F32),
        in_specs=[vmem_spec] * 2,
        out_specs=vmem_spec,
        name="finish",
    )(hold(smoothed), hold(pieces))


TEAM = ("section", "core")
HEIGHT = ("far", "near")


def body(
    residual,
    coupling_tiles,
    inverse_tiles,
    diag_kind,
    diag_coeff,
    tile_cols,
    tile_kinds,
    tile_coeff,
    halo_rows,
    tile_owner,
    node_slot,
    edge_nodes,
    tangents,
    grad_blocks,
    vec_blocks,
):
    far, team = lax.axis_size("far"), lax.axis_size(TEAM)
    node_tiles = grad_blocks.shape[0]
    tiles = diag_kind.shape[0]
    width = coupling_tiles.shape[1]
    cls = lax.axis_index(TEAM).astype(jnp.int32).reshape(1)
    parity = lax.axis_index("near").astype(jnp.int32).reshape(1)
    own = pack(tile_owner[:, 0], node_slot, residual, tangents, edge_nodes, far * NEAR * CORES)
    other = lax.ppermute(own, "near", [(0, 1), (1, 0)])
    gathered = lax.all_gather(own, TEAM)
    gathered_other = lax.all_gather(other, TEAM)

    smoothed, rim = smooth(diag_kind, diag_coeff, halo_rows, residual, inverse_tiles)
    slabs = lax.axis_size("slab")
    low = lax.ppermute(rim, "slab", [(i, i + 1) for i in range(slabs - 1)])
    high = lax.ppermute(rim, "slab", [(i + 1, i) for i in range(slabs - 1)])

    sums = node_sums(cls, parity, gathered, gathered_other, tiles, width, far * node_tiles)
    sums = sums.reshape(far, node_tiles * 32, width)
    arrived = lax.all_to_all(sums, "far", split_axis=0, concat_axis=0, tiled=True)

    chosen = class_list(cls, gathered, tiles, width)
    smoothed_twice = smooth_again(
        diag_kind, diag_coeff, tile_cols, tile_kinds, tile_coeff,
        smoothed, low, high, residual, coupling_tiles, inverse_tiles,
    )
    arrived, smoothed_twice, chosen = lax.optimization_barrier((arrived, smoothed_twice, chosen))

    solved = solve(arrived.reshape(far, node_tiles, 32, width), grad_blocks, vec_blocks)
    values = lax.all_gather(solved, HEIGHT, tiled=True)
    corrections = back(chosen, gathered, values, tiles).reshape(team, tiles, 8, width)
    pieces = lax.all_to_all(corrections, TEAM, split_axis=0, concat_axis=0, tiled=True)
    return finish(smoothed_twice, pieces)


def solution(mesh):
    names = ("section", "far", "near", "core", "slab")
    sections, doms, slabs = (mesh.shape[name] for name in ("section", "dom", "slab"))
    shape = (sections, doms // CORES // NEAR, NEAR, CORES, slabs)
    inner = Mesh(mesh.devices.reshape(shape), names)
    rows, cols = P(names), P(None, names)
    placed = (
        cols, P(), P(), rows, rows, cols, cols, cols, rows, rows, rows, cols, cols, rows, rows,
    )
    return jax.shard_map(
        body, mesh=inner, in_specs=placed, out_specs=cols, check_vma=False
    )
```

```python
import functools

import jax
import jax.numpy as jnp
from jax import lax
from jax.experimental import pallas as pl
from jax.experimental.pallas import tpu as pltpu
from jax.sharding import Mesh, PartitionSpec as P

DAMPING = 0.7
CORES = 2
NEAR = 2
GROUP = 8
F32 = jnp.float32
BF16 = jnp.bfloat16
SMEM = pltpu.SMEM
VMEM = pltpu.VMEM

vmem_spec = pl.BlockSpec(memory_space=VMEM)
smem_spec = pl.BlockSpec(memory_space=SMEM)
any_spec = pl.BlockSpec(memory_space=pl.ANY)


def held(shape):
    return pltpu.VMEM(shape, F32)


def hold(x):
    return pltpu.with_memory_space_constraint(x, VMEM)


def split(x):
    high = x.astype(BF16)
    low = (x - high.astype(F32)).astype(BF16)
    return high, low


def dot_nt(a, b):
    return lax.dot_general(a, b, (((1,), (1,)), ((), ())), preferred_element_type=F32)


def product_nt(parts, matrix):
    count = parts.shape[0] // 2
    high, low = split(matrix)
    both = dot_nt(parts, high)
    return both[:count] + both[count:] + dot_nt(parts[:count], low)


def stacked(rows):
    high, low = split(rows)
    return jnp.concatenate([high, low], axis=0)


def parts_of(x, size):
    if size & (size - 1) == 0:
        return lax.shift_right_logical(x, jnp.int32(size.bit_length() - 1)), x & (size - 1)
    return x // size, x % size


FIELDS = 5


def pack_kernel(owner, slot, residual, tangents, ends, out, *, doms):
    tiles = owner.shape[0]
    width = residual.shape[1] // tiles
    lanes = lax.broadcasted_iota(jnp.int32, (1, width), 1)
    owners = jnp.zeros((1, width), jnp.int32)
    slots = jnp.zeros((1, width), jnp.int32)
    for t in range(tiles):
        owners = jnp.where(lanes == t, owner[t], owners)
        slots = jnp.where(lanes == t, slot[t], slots)
    section, dom = parts_of(owners, doms)
    z, core = parts_of(dom, CORES)
    out[:, 0 : tiles * width] = residual[...]
    for t in range(tiles):
        part = slice(t * width, (t + 1) * width)
        for f in range(FIELDS):
            row = tangents[f : f + 1, part] if f < 3 else ends[f - 3 : f - 2, part].astype(F32)
            at = (tiles + (t // 8) * FIELDS + f) * width
            out[t % 8 : t % 8 + 1, at : at + width] = row
    at = (tiles + tiles // 8 * FIELDS) * width
    out[:, at : at + width] = jnp.zeros((8, width), F32)
    out[0:1, at : at + width] = (section * CORES + core).astype(F32)
    out[1:2, at : at + width] = (z * 2 + slots).astype(F32)


def pack(owner, slot, residual, tangents, ends, doms):
    tiles = owner.shape[0]
    width = residual.shape[1] // tiles
    return pl.pallas_call(
        functools.partial(pack_kernel, doms=doms),
        out_shape=held((8, (tiles + tiles // 8 * FIELDS + 1) * width)),
        in_specs=[smem_spec, smem_spec, vmem_spec, vmem_spec, vmem_spec],
        out_specs=vmem_spec,
        name="pack",
    )(owner, slot, residual, tangents, ends)


def tile_reader(gathered, tile, tiles, width):
    device, t = parts_of(tile, tiles)
    block, row = parts_of(t, 8)
    base = tiles + block * FIELDS

    def lanes(at):
        return pl.ds(pl.multiple_of(at * width, width), width)

    return (
        lambda: gathered[device, :, lanes(t)],
        lambda f: pltpu.roll(gathered[device, :, lanes(base + f)], 8 - row, 0)[0:1],
    )


def choose(chosen, gathered, tiles, width, rule):
    count = jnp.int32(0)
    for q in range(gathered.shape[0]):
        block = gathered[q, :, gathered.shape[2] - width :]
        codes = rule(block[0:1], block[1:2].astype(jnp.int32))
        for t in range(tiles):
            code = codes[0, t]
            chosen[0, count + 1] = q * tiles + t
            chosen[1, count + 1] = code
            count = count + (code >= 0).astype(jnp.int32)
    chosen[0, 0] = count
    last, place = chosen[0, count], chosen[1, count]
    for extra in range(GROUP):
        chosen[0, count + 1 + extra] = last
        chosen[1, count + 1 + extra] = place
    return count


def sums_kernel(cls, parity, own, other, sums, chosen_own, chosen_other, *, tiles, width):
    sums[...] = jnp.zeros_like(sums)
    mine, near = cls[0].astype(F32), parity[0]

    def rule(classes, places):
        fits = (classes == mine) & (((places >> 1) & (NEAR - 1)) == near)
        return jnp.where(fits, (places >> NEAR) * 2 + (places & 1), -1)

    nodes = lax.broadcasted_iota(jnp.int32, (width, width), 0).astype(F32)
    counts = [
        choose(chosen, gathered, tiles, width, rule)
        for chosen, gathered in ((chosen_own, own), (chosen_other, other))
    ]
    for count, chosen, gathered in zip(counts, (chosen_own, chosen_other), (own, other)):

        def step(i, carry, count=count, chosen=chosen, gathered=gathered):
            for j in range(GROUP):
                at = i * GROUP + j + 1
                tile, local = chosen[0, at], chosen[1, at]
                residual, field = tile_reader(gathered, tile, tiles, width)
                rows = residual() * jnp.where(at <= count, 1.0, 0.0)
                at_a = (nodes == field(3)).astype(F32)
                at_b = (nodes == field(4)).astype(F32)
                plus = (at_a + at_b).astype(BF16)
                minus = (at_b - at_a).astype(BF16)
                vec = jnp.concatenate([(0.5 * field(c)) * rows for c in range(3)], axis=0)
                total_vec = dot_nt(stacked(vec), plus)
                total_grad = dot_nt(stacked(rows), minus)
                sums[local, 0:8, :] += total_grad[:8] + total_grad[8:]
                sums[local, 8:32, :] += total_vec[:24] + total_vec[24:]
            return carry

        lax.fori_loop(0, (count + GROUP - 1) // GROUP, step, 0)


def list_shape(gathered, tiles):
    return (2, gathered.shape[0] * tiles + 1 + GROUP)


def node_sums(cls, parity, own, other, tiles, width, places):
    return pl.pallas_call(
        functools.partial(sums_kernel, tiles=tiles, width=width),
        out_shape=held((places, 32, width)),
        in_specs=[smem_spec, smem_spec, vmem_spec, vmem_spec],
        out_specs=vmem_spec,
        scratch_shapes=[SMEM(list_shape(own, tiles), jnp.int32) for _ in range(2)],
        name="node_sums",
    )(cls, parity, hold(own), hold(other))


def list_kernel(cls, gathered, chosen, *, tiles, width):
    mine = cls[0].astype(F32)
    choose(
        chosen, gathered, tiles, width, lambda classes, places: jnp.where(classes == mine, places, -1)
    )


def class_list(cls, gathered, tiles, width):
    return pl.pallas_call(
        functools.partial(list_kernel, tiles=tiles, width=width),
        out_shape=jax.ShapeDtypeStruct(list_shape(gathered, tiles), jnp.int32),
        in_specs=[smem_spec, vmem_spec],
        out_specs=smem_spec,
        name="class_list",
    )(cls, hold(gathered))


def solve_kernel(arrived, grad, vec, out):
    count = arrived.shape[0]
    for n in range(grad.shape[0]):
        rows = arrived[0, n]
        for z in range(1, count):
            rows = rows + arrived[z, n]
        out[n, 0:8, :] = product_nt(stacked(rows[:8]), grad[n])
        out[n, 8:32, :] = product_nt(stacked(rows[8:]), vec[n])


def solve(arrived, grad, vec):
    return pl.pallas_call(
        solve_kernel,
        out_shape=held(arrived.shape[1:]),
        in_specs=[vmem_spec] * 3,
        out_specs=vmem_spec,
        name="solve",
    )(hold(arrived), hold(grad), hold(vec))


def back_kernel(chosen, gathered, values, out):
    out[...] = jnp.zeros_like(out)
    total, _, width = out.shape

    def pick(rows, index):
        return jnp.take_along_axis(rows, index, axis=1)

    def step(i, carry):
        for j in range(GROUP):
            at = i * GROUP + j + 1
            tile, local = chosen[0, at], chosen[1, at]
            _, field = tile_reader(gathered, tile, total // gathered.shape[0], width)
            index_a = jnp.broadcast_to(field(3).astype(jnp.int32), (8, width))
            index_b = jnp.broadcast_to(field(4).astype(jnp.int32), (8, width))
            grad = values[local, 0:8, :]
            found = pick(grad, index_b) - pick(grad, index_a)
            for c in range(3):
                rows = values[local, 8 + 8 * c : 16 + 8 * c, :]
                half = 0.5 * field(c)
                found = found + half * (pick(rows, index_a) + pick(rows, index_b))
            out[tile] = found
        return carry

    lax.fori_loop(0, (chosen[0, 0] + GROUP - 1) // GROUP, step, 0)


def back(chosen, gathered, values, tiles):
    width = values.shape[2]
    return pl.pallas_call(
        back_kernel,
        out_shape=held((gathered.shape[0] * tiles, 8, width)),
        in_specs=[smem_spec, vmem_spec, vmem_spec],
        out_specs=vmem_spec,
        name="back",
    )(chosen, hold(gathered), hold(values))


def by_tile(ref, tiles, width):
    return jnp.concatenate([ref[:, t * width : (t + 1) * width] for t in range(tiles)], axis=0)


def smooth_kernel(kind, coeff, halo, residual, inverse, out, rim, work):
    tiles, _, width = out.shape
    parts = stacked(by_tile(residual, tiles, width))
    for k in range(inverse.shape[0]):
        work[k] = product_nt(parts, inverse[k]).reshape(tiles, 8, width)
    for t in range(tiles):
        out[t] = work[kind[t], t] / coeff[t]
    for h in range(rim.shape[0]):
        rim[h] = out[halo[h]]


def smooth(kind, coeff, halo, residual, inverse):
    tiles = kind.shape[0]
    kinds, width, _ = inverse.shape
    return pl.pallas_call(
        smooth_kernel,
        out_shape=(
            held((tiles, 8, width)),
            held((halo.shape[0], 8, width)),
        ),
        in_specs=[smem_spec] * 3 + [vmem_spec] * 2,
        out_specs=(vmem_spec, vmem_spec),
        scratch_shapes=[VMEM((kinds, tiles, 8, width), F32)],
        name="smooth_once",
    )(kind, coeff, halo, hold(residual), hold(inverse))


def again_kernel(
    kind, coeff, cols, kinds, coeffs, smoothed, low, high, residual, coupling, inverse, out, work, rest
):
    tiles, _, width = smoothed.shape
    sources = jnp.concatenate(
        [
            smoothed[...].reshape(tiles * 8, width),
            low[...].reshape(low.shape[0] * 8, width),
            high[...].reshape(high.shape[0] * 8, width),
        ],
        axis=0,
    )
    parts = stacked(sources)
    count = sources.shape[0] // 8
    for k in range(coupling.shape[0]):
        work[k] = product_nt(parts, coupling[k]).reshape(count, 8, width)
    for t in range(tiles):
        total = coeff[t] * work[kind[t], t]
        for m in range(cols.shape[0]):
            total = total + coeffs[m, t] * work[kinds[m, t], cols[m, t]]
        rest[t] = residual[:, t * width : (t + 1) * width] - total
    parts = stacked(rest[...].reshape(tiles * 8, width))
    for k in range(inverse.shape[0]):
        work[k, 0:tiles] = product_nt(parts, inverse[k]).reshape(tiles, 8, width)
    for t in range(tiles):
        out[t] = smoothed[t] + DAMPING * (work[kind[t], t] / coeff[t])


def smooth_again(kind, coeff, cols, kinds, coeffs, smoothed, low, high, residual, coupling, inverse):
    tiles, _, width = smoothed.shape
    count = tiles + low.shape[0] + high.shape[0]
    return pl.pallas_call(
        again_kernel,
        out_shape=held((tiles, 8, width)),
        in_specs=[smem_spec] * 5 + [vmem_spec] * 6,
        out_specs=vmem_spec,
        scratch_shapes=[
            VMEM((coupling.shape[0], count, 8, width), F32),
            VMEM((tiles, 8, width), F32),
        ],
        name="smooth_again",
    )(
        kind, coeff, cols, kinds, coeffs,
        hold(smoothed), hold(low), hold(high), hold(residual), hold(coupling), hold(inverse),
    )


def finish_kernel(smoothed, pieces, out):
    tiles, _, width = smoothed.shape
    for t in range(tiles):
        rows = pieces[0, t]
        for q in range(1, pieces.shape[0]):
            rows = rows + pieces[q, t]
        out[:, t * width : (t + 1) * width] = smoothed[t] + rows


def finish(smoothed, pieces):
    tiles, cases, width = smoothed.shape
    return pl.pallas_call(
        finish_kernel,
        out_shape=jax.ShapeDtypeStruct((cases, tiles * width), F32),
        in_specs=[vmem_spec] * 2,
        out_specs=vmem_spec,
        name="finish",
    )(hold(smoothed), hold(pieces))


TEAM = ("section", "core")
HEIGHT = ("far", "near")


def body(
    residual,
    coupling_tiles,
    inverse_tiles,
    diag_kind,
    diag_coeff,
    tile_cols,
    tile_kinds,
    tile_coeff,
    halo_rows,
    tile_owner,
    node_slot,
    edge_nodes,
    tangents,
    grad_blocks,
    vec_blocks,
):
    far, team = lax.axis_size("far"), lax.axis_size(TEAM)
    node_tiles = grad_blocks.shape[0]
    tiles = diag_kind.shape[0]
    width = coupling_tiles.shape[1]
    cls = lax.axis_index(TEAM).astype(jnp.int32).reshape(1)
    parity = lax.axis_index("near").astype(jnp.int32).reshape(1)
    own = pack(tile_owner[:, 0], node_slot, residual, tangents, edge_nodes, far * NEAR * CORES)
    other = lax.ppermute(own, "near", [(0, 1), (1, 0)])
    gathered = lax.all_gather(own, TEAM)
    gathered_other = lax.all_gather(other, TEAM)

    smoothed, rim = smooth(diag_kind, diag_coeff, halo_rows, residual, inverse_tiles)
    slabs = lax.axis_size("slab")
    low = lax.ppermute(rim, "slab", [(i, i + 1) for i in range(slabs - 1)])
    high = lax.ppermute(rim, "slab", [(i + 1, i) for i in range(slabs - 1)])

    sums = node_sums(cls, parity, gathered, gathered_other, tiles, width, far * node_tiles)
    sums = sums.reshape(far, node_tiles * 32, width)
    arrived = lax.all_to_all(sums, "far", split_axis=0, concat_axis=0, tiled=True)

    chosen = class_list(cls, gathered, tiles, width)
    arrived, chosen, smoothed, low, high = lax.optimization_barrier(
        (arrived, chosen, smoothed, low, high)
    )

    solved = solve(arrived.reshape(far, node_tiles, 32, width), grad_blocks, vec_blocks)
    values = lax.all_gather(solved, HEIGHT, tiled=True)
    corrections = back(chosen, gathered, values, tiles).reshape(team, tiles, 8, width)
    pieces = lax.all_to_all(corrections, TEAM, split_axis=0, concat_axis=0, tiled=True)

    low, high, values = lax.optimization_barrier((low, high, values))
    smoothed_twice = smooth_again(
        diag_kind, diag_coeff, tile_cols, tile_kinds, tile_coeff,
        smoothed, low, high, residual, coupling_tiles, inverse_tiles,
    )
    return finish(smoothed_twice, pieces)


def solution(mesh):
    names = ("section", "far", "near", "core", "slab")
    sections, doms, slabs = (mesh.shape[name] for name in ("section", "dom", "slab"))
    shape = (sections, doms // CORES // NEAR, NEAR, CORES, slabs)
    inner = Mesh(mesh.devices.reshape(shape), names)
    rows, cols = P(names), P(None, names)
    placed = (
        cols, P(), P(), rows, rows, cols, cols, cols, rows, rows, rows, cols, cols, rows, rows,
    )
    return jax.shard_map(
        body, mesh=inner, in_specs=placed, out_specs=cols, check_vma=False
    )
```

```python
import functools

import jax
import jax.numpy as jnp
from jax import lax
from jax.experimental import pallas as pl
from jax.experimental.pallas import tpu as pltpu
from jax.sharding import Mesh, PartitionSpec as P

DAMPING = 0.7
CORES = 2
NEAR = 2
GROUP = 8
F32 = jnp.float32
BF16 = jnp.bfloat16
SMEM = pltpu.SMEM
VMEM = pltpu.VMEM

vmem_spec = pl.BlockSpec(memory_space=VMEM)
smem_spec = pl.BlockSpec(memory_space=SMEM)
any_spec = pl.BlockSpec(memory_space=pl.ANY)


def held(shape):
    return pltpu.VMEM(shape, F32)


def hold(x):
    return pltpu.with_memory_space_constraint(x, VMEM)


def split(x):
    high = x.astype(BF16)
    low = (x - high.astype(F32)).astype(BF16)
    return high, low


def dot_nt(a, b):
    return lax.dot_general(a, b, (((1,), (1,)), ((), ())), preferred_element_type=F32)


def product_nt(parts, matrix):
    count = parts.shape[0] // 2
    high, low = split(matrix)
    both = dot_nt(parts, high)
    return both[:count] + both[count:] + dot_nt(parts[:count], low)


def stacked(rows):
    high, low = split(rows)
    return jnp.concatenate([high, low], axis=0)


def parts_of(x, size):
    if size & (size - 1) == 0:
        return lax.shift_right_logical(x, jnp.int32(size.bit_length() - 1)), x & (size - 1)
    return x // size, x % size


FIELDS = 5


def pack_kernel(owner, slot, residual, tangents, ends, out, *, doms):
    tiles = owner.shape[0]
    width = residual.shape[1] // tiles
    lanes = lax.broadcasted_iota(jnp.int32, (1, width), 1)
    owners = jnp.zeros((1, width), jnp.int32)
    slots = jnp.zeros((1, width), jnp.int32)
    for t in range(tiles):
        owners = jnp.where(lanes == t, owner[t], owners)
        slots = jnp.where(lanes == t, slot[t], slots)
    section, dom = parts_of(owners, doms)
    z, core = parts_of(dom, CORES)
    out[:, 0 : tiles * width] = residual[...]
    for t in range(tiles):
        part = slice(t * width, (t + 1) * width)
        for f in range(FIELDS):
            row = tangents[f : f + 1, part] if f < 3 else ends[f - 3 : f - 2, part].astype(F32)
            at = (tiles + (t // 8) * FIELDS + f) * width
            out[t % 8 : t % 8 + 1, at : at + width] = row
    at = (tiles + tiles // 8 * FIELDS) * width
    out[:, at : at + width] = jnp.zeros((8, width), F32)
    out[0:1, at : at + width] = (section * CORES + core).astype(F32)
    out[1:2, at : at + width] = (z * 2 + slots).astype(F32)


def pack(owner, slot, residual, tangents, ends, doms):
    tiles = owner.shape[0]
    width = residual.shape[1] // tiles
    return pl.pallas_call(
        functools.partial(pack_kernel, doms=doms),
        out_shape=held((8, (tiles + tiles // 8 * FIELDS + 1) * width)),
        in_specs=[smem_spec, smem_spec, vmem_spec, vmem_spec, vmem_spec],
        out_specs=vmem_spec,
        name="pack",
    )(owner, slot, residual, tangents, ends)


def tile_reader(gathered, tile, tiles, width):
    device, t = parts_of(tile, tiles)
    block, row = parts_of(t, 8)
    base = tiles + block * FIELDS

    def lanes(at):
        return pl.ds(pl.multiple_of(at * width, width), width)

    return (
        lambda: gathered[device, :, lanes(t)],
        lambda f: pltpu.roll(gathered[device, :, lanes(base + f)], 8 - row, 0)[0:1],
    )


def choose(chosen, gathered, tiles, width, rule):
    count = jnp.int32(0)
    for q in range(gathered.shape[0]):
        block = gathered[q, :, gathered.shape[2] - width :]
        codes = rule(q, block[0:1], block[1:2].astype(jnp.int32))
        for t in range(tiles):
            code = codes[0, t]
            chosen[0, count + 1] = q * tiles + t
            chosen[1, count + 1] = code
            count = count + (code >= 0).astype(jnp.int32)
    chosen[0, 0] = count
    last, place = chosen[0, count], chosen[1, count]
    for extra in range(GROUP):
        chosen[0, count + 1 + extra] = last
        chosen[1, count + 1 + extra] = place
    return count


def sums_kernel(cls, parity, gathered, sums, chosen, *, tiles, width):
    sums[...] = jnp.zeros_like(sums)
    mine, near = cls[0].astype(F32), parity[0]

    def rule(q, classes, places):
        fits = (classes == mine) & (((places >> 1) & (NEAR - 1)) == near)
        return jnp.where(fits, (places >> NEAR) * 2 + (places & 1), -1)

    nodes = lax.broadcasted_iota(jnp.int32, (width, width), 0).astype(F32)
    count = choose(chosen, gathered, tiles, width, rule)

    def step(i, carry):
        for j in range(GROUP):
            at = i * GROUP + j + 1
            tile, local = chosen[0, at], chosen[1, at]
            residual, field = tile_reader(gathered, tile, tiles, width)
            rows = residual() * jnp.where(at <= count, 1.0, 0.0)
            at_a = (nodes == field(3)).astype(F32)
            at_b = (nodes == field(4)).astype(F32)
            plus = (at_a + at_b).astype(BF16)
            minus = (at_b - at_a).astype(BF16)
            vec = jnp.concatenate([(0.5 * field(c)) * rows for c in range(3)], axis=0)
            total_vec = dot_nt(stacked(vec), plus)
            total_grad = dot_nt(stacked(rows), minus)
            sums[local, 0:8, :] += total_grad[:8] + total_grad[8:]
            sums[local, 8:32, :] += total_vec[:24] + total_vec[24:]
        return carry

    lax.fori_loop(0, (count + GROUP - 1) // GROUP, step, 0)


def list_shape(gathered, tiles):
    return (2, gathered.shape[0] * tiles + 1 + GROUP)


def node_sums(cls, parity, gathered, tiles, width, places):
    return pl.pallas_call(
        functools.partial(sums_kernel, tiles=tiles, width=width),
        out_shape=held((places, 32, width)),
        in_specs=[smem_spec, smem_spec, vmem_spec],
        out_specs=vmem_spec,
        scratch_shapes=[SMEM(list_shape(gathered, tiles), jnp.int32)],
        name="node_sums",
    )(cls, parity, hold(gathered))


def list_kernel(cls, parity, gathered, chosen, *, tiles, width):
    mine = cls[0].astype(F32)

    def rule(q, classes, places):
        beside = jnp.where(parity[0] == (q // CORES) % NEAR, mine, -1.0)
        return jnp.where(classes == beside, places, -1)

    choose(chosen, gathered, tiles, width, rule)


def class_list(cls, parity, gathered, tiles, width):
    return pl.pallas_call(
        functools.partial(list_kernel, tiles=tiles, width=width),
        out_shape=jax.ShapeDtypeStruct(list_shape(gathered, tiles), jnp.int32),
        in_specs=[smem_spec, smem_spec, vmem_spec],
        out_specs=smem_spec,
        name="class_list",
    )(cls, parity, hold(gathered))


def solve_kernel(arrived, grad, vec, out):
    count = arrived.shape[0]
    for n in range(grad.shape[0]):
        rows = arrived[0, n]
        for z in range(1, count):
            rows = rows + arrived[z, n]
        out[n, 0:8, :] = product_nt(stacked(rows[:8]), grad[n])
        out[n, 8:32, :] = product_nt(stacked(rows[8:]), vec[n])


def solve(arrived, grad, vec):
    return pl.pallas_call(
        solve_kernel,
        out_shape=held(arrived.shape[1:]),
        in_specs=[vmem_spec] * 3,
        out_specs=vmem_spec,
        name="solve",
    )(hold(arrived), hold(grad), hold(vec))


def back_kernel(chosen, gathered, values, out, *, tiles):
    out[...] = jnp.zeros_like(out)
    width = out.shape[2]

    def pick(rows, index):
        return jnp.take_along_axis(rows, index, axis=1)

    def step(i, carry):
        for j in range(GROUP):
            at = i * GROUP + j + 1
            tile, local = chosen[0, at], chosen[1, at]
            _, field = tile_reader(gathered, tile, tiles, width)
            index_a = jnp.broadcast_to(field(3).astype(jnp.int32), (8, width))
            index_b = jnp.broadcast_to(field(4).astype(jnp.int32), (8, width))
            grad = values[local, 0:8, :]
            found = pick(grad, index_b) - pick(grad, index_a)
            for c in range(3):
                rows = values[local, 8 + 8 * c : 16 + 8 * c, :]
                half = 0.5 * field(c)
                found = found + half * (pick(rows, index_a) + pick(rows, index_b))
            device, t = parts_of(tile, tiles)
            pair, core = parts_of(device, CORES)
            out[(pair // NEAR * CORES + core) * tiles + t] = found
        return carry

    lax.fori_loop(0, (chosen[0, 0] + GROUP - 1) // GROUP, step, 0)


def back(chosen, gathered, values, tiles):
    width = values.shape[2]
    return pl.pallas_call(
        functools.partial(back_kernel, tiles=tiles),
        out_shape=held((gathered.shape[0] // NEAR * tiles, 8, width)),
        in_specs=[smem_spec, vmem_spec, vmem_spec],
        out_specs=vmem_spec,
        name="back",
    )(chosen, hold(gathered), hold(values))


def by_tile(ref, tiles, width):
    return jnp.concatenate([ref[:, t * width : (t + 1) * width] for t in range(tiles)], axis=0)


def smooth_kernel(kind, coeff, halo, residual, inverse, out, rim, work):
    tiles, _, width = out.shape
    parts = stacked(by_tile(residual, tiles, width))
    for k in range(inverse.shape[0]):
        work[k] = product_nt(parts, inverse[k]).reshape(tiles, 8, width)
    for t in range(tiles):
        out[t] = work[kind[t], t] / coeff[t]
    for h in range(rim.shape[0]):
        rim[h] = out[halo[h]]


def smooth(kind, coeff, halo, residual, inverse):
    tiles = kind.shape[0]
    kinds, width, _ = inverse.shape
    return pl.pallas_call(
        smooth_kernel,
        out_shape=(
            held((tiles, 8, width)),
            held((halo.shape[0], 8, width)),
        ),
        in_specs=[smem_spec] * 3 + [vmem_spec] * 2,
        out_specs=(vmem_spec, vmem_spec),
        scratch_shapes=[VMEM((kinds, tiles, 8, width), F32)],
        name="smooth_once",
    )(kind, coeff, halo, hold(residual), hold(inverse))


def again_kernel(
    kind, coeff, cols, kinds, coeffs, smoothed, low, high, residual, coupling, inverse, out, work, rest
):
    tiles, _, width = smoothed.shape
    sources = jnp.concatenate(
        [
            smoothed[...].reshape(tiles * 8, width),
            low[...].reshape(low.shape[0] * 8, width),
            high[...].reshape(high.shape[0] * 8, width),
        ],
        axis=0,
    )
    parts = stacked(sources)
    count = sources.shape[0] // 8
    for k in range(coupling.shape[0]):
        work[k] = product_nt(parts, coupling[k]).reshape(count, 8, width)
    for t in range(tiles):
        total = coeff[t] * work[kind[t], t]
        for m in range(cols.shape[0]):
            total = total + coeffs[m, t] * work[kinds[m, t], cols[m, t]]
        rest[t] = residual[:, t * width : (t + 1) * width] - total
    parts = stacked(rest[...].reshape(tiles * 8, width))
    for k in range(inverse.shape[0]):
        work[k, 0:tiles] = product_nt(parts, inverse[k]).reshape(tiles, 8, width)
    for t in range(tiles):
        out[t] = smoothed[t] + DAMPING * (work[kind[t], t] / coeff[t])


def smooth_again(kind, coeff, cols, kinds, coeffs, smoothed, low, high, residual, coupling, inverse):
    tiles, _, width = smoothed.shape
    count = tiles + low.shape[0] + high.shape[0]
    return pl.pallas_call(
        again_kernel,
        out_shape=held((tiles, 8, width)),
        in_specs=[smem_spec] * 5 + [vmem_spec] * 6,
        out_specs=vmem_spec,
        scratch_shapes=[
            VMEM((coupling.shape[0], count, 8, width), F32),
            VMEM((tiles, 8, width), F32),
        ],
        name="smooth_again",
    )(
        kind, coeff, cols, kinds, coeffs,
        hold(smoothed), hold(low), hold(high), hold(residual), hold(coupling), hold(inverse),
    )


def finish_kernel(smoothed, pieces, out):
    tiles, _, width = smoothed.shape
    for t in range(tiles):
        rows = pieces[0, t]
        for q in range(1, pieces.shape[0]):
            rows = rows + pieces[q, t]
        out[:, t * width : (t + 1) * width] = smoothed[t] + rows


def finish(smoothed, pieces):
    tiles, cases, width = smoothed.shape
    return pl.pallas_call(
        finish_kernel,
        out_shape=jax.ShapeDtypeStruct((cases, tiles * width), F32),
        in_specs=[vmem_spec] * 2,
        out_specs=vmem_spec,
        name="finish",
    )(hold(smoothed), hold(pieces))


TEAM = ("section", "core")
HEIGHT = ("far", "near")
TEAMS = ("section", "near", "core")


def body(
    residual,
    coupling_tiles,
    inverse_tiles,
    diag_kind,
    diag_coeff,
    tile_cols,
    tile_kinds,
    tile_coeff,
    halo_rows,
    tile_owner,
    node_slot,
    edge_nodes,
    tangents,
    grad_blocks,
    vec_blocks,
):
    far, team = lax.axis_size("far"), lax.axis_size(TEAM)
    node_tiles = grad_blocks.shape[0]
    tiles = diag_kind.shape[0]
    width = coupling_tiles.shape[1]
    cls = lax.axis_index(TEAM).astype(jnp.int32).reshape(1)
    parity = lax.axis_index("near").astype(jnp.int32).reshape(1)
    own = pack(tile_owner[:, 0], node_slot, residual, tangents, edge_nodes, far * NEAR * CORES)
    gathered = lax.all_gather(own, TEAMS)

    smoothed, rim = smooth(diag_kind, diag_coeff, halo_rows, residual, inverse_tiles)
    slabs = lax.axis_size("slab")
    low = lax.ppermute(rim, "slab", [(i, i + 1) for i in range(slabs - 1)])
    high = lax.ppermute(rim, "slab", [(i + 1, i) for i in range(slabs - 1)])

    sums = node_sums(cls, parity, gathered, tiles, width, far * node_tiles)
    sums = sums.reshape(far, node_tiles * 32, width)
    arrived = lax.all_to_all(sums, "far", split_axis=0, concat_axis=0, tiled=True)

    chosen = class_list(cls, parity, gathered, tiles, width)
    smoothed_twice = smooth_again(
        diag_kind, diag_coeff, tile_cols, tile_kinds, tile_coeff,
        smoothed, low, high, residual, coupling_tiles, inverse_tiles,
    )
    arrived, smoothed_twice, chosen = lax.optimization_barrier((arrived, smoothed_twice, chosen))

    solved = solve(arrived.reshape(far, node_tiles, 32, width), grad_blocks, vec_blocks)
    values = lax.all_gather(solved, HEIGHT, tiled=True)
    corrections = back(chosen, gathered, values, tiles).reshape(team, tiles, 8, width)
    pieces = lax.all_to_all(corrections, TEAM, split_axis=0, concat_axis=0, tiled=True)
    return finish(smoothed_twice, pieces)


def solution(mesh):
    names = ("section", "far", "near", "core", "slab")
    sections, doms, slabs = (mesh.shape[name] for name in ("section", "dom", "slab"))
    shape = (sections, doms // CORES // NEAR, NEAR, CORES, slabs)
    inner = Mesh(mesh.devices.reshape(shape), names)
    rows, cols = P(names), P(None, names)
    placed = (
        cols, P(), P(), rows, rows, cols, cols, cols, rows, rows, rows, cols, cols, rows, rows,
    )
    return jax.shard_map(
        body, mesh=inner, in_specs=placed, out_specs=cols, check_vma=False
    )
```

```python
import functools

import jax
import jax.numpy as jnp
from jax import lax
from jax.experimental import pallas as pl
from jax.experimental.pallas import tpu as pltpu
from jax.sharding import Mesh, PartitionSpec as P

DAMPING = 0.7
CORES = 2
NEAR = 2
GROUP = 8
F32 = jnp.float32
BF16 = jnp.bfloat16
SMEM = pltpu.SMEM
VMEM = pltpu.VMEM

vmem_spec = pl.BlockSpec(memory_space=VMEM)
smem_spec = pl.BlockSpec(memory_space=SMEM)
any_spec = pl.BlockSpec(memory_space=pl.ANY)


def held(shape):
    return pltpu.VMEM(shape, F32)


def hold(x):
    return pltpu.with_memory_space_constraint(x, VMEM)


def split(x):
    high = x.astype(BF16)
    low = (x - high.astype(F32)).astype(BF16)
    return high, low


def dot_nt(a, b):
    return lax.dot_general(a, b, (((1,), (1,)), ((), ())), preferred_element_type=F32)


def product_nt(parts, matrix):
    count = parts.shape[0] // 2
    high, low = split(matrix)
    both = dot_nt(parts, high)
    return both[:count] + both[count:] + dot_nt(parts[:count], low)


def stacked(rows):
    high, low = split(rows)
    return jnp.concatenate([high, low], axis=0)


def parts_of(x, size):
    if size & (size - 1) == 0:
        return lax.shift_right_logical(x, jnp.int32(size.bit_length() - 1)), x & (size - 1)
    return x // size, x % size


FIELDS = 5


def pack_kernel(owner, slot, residual, tangents, ends, out, *, doms):
    tiles = owner.shape[0]
    width = residual.shape[1] // tiles
    lanes = lax.broadcasted_iota(jnp.int32, (1, width), 1)
    owners = jnp.zeros((1, width), jnp.int32)
    slots = jnp.zeros((1, width), jnp.int32)
    for t in range(tiles):
        owners = jnp.where(lanes == t, owner[t], owners)
        slots = jnp.where(lanes == t, slot[t], slots)
    section, dom = parts_of(owners, doms)
    z, core = parts_of(dom, CORES)
    out[:, 0 : tiles * width] = residual[...]
    for t in range(tiles):
        part = slice(t * width, (t + 1) * width)
        for f in range(FIELDS):
            row = tangents[f : f + 1, part] if f < 3 else ends[f - 3 : f - 2, part].astype(F32)
            at = (tiles + (t // 8) * FIELDS + f) * width
            out[t % 8 : t % 8 + 1, at : at + width] = row
    at = (tiles + tiles // 8 * FIELDS) * width
    out[:, at : at + width] = jnp.zeros((8, width), F32)
    out[0:1, at : at + width] = (section * CORES + core).astype(F32)
    out[1:2, at : at + width] = (z * 2 + slots).astype(F32)


def pack(owner, slot, residual, tangents, ends, doms):
    tiles = owner.shape[0]
    width = residual.shape[1] // tiles
    return pl.pallas_call(
        functools.partial(pack_kernel, doms=doms),
        out_shape=held((8, (tiles + tiles // 8 * FIELDS + 1) * width)),
        in_specs=[smem_spec, smem_spec, vmem_spec, vmem_spec, vmem_spec],
        out_specs=vmem_spec,
        name="pack",
    )(owner, slot, residual, tangents, ends)


def tile_reader(gathered, tile, tiles, width):
    device, t = parts_of(tile, tiles)
    block, row = parts_of(t, 8)
    base = tiles + block * FIELDS

    def lanes(at):
        return pl.ds(pl.multiple_of(at * width, width), width)

    return (
        lambda: gathered[device, :, lanes(t)],
        lambda f: pltpu.roll(gathered[device, :, lanes(base + f)], 8 - row, 0)[0:1],
    )


def choose(chosen, gathered, tiles, width, rule):
    count = jnp.int32(0)
    for q in range(gathered.shape[0]):
        block = gathered[q, :, gathered.shape[2] - width :]
        codes = rule(q, block[0:1], block[1:2].astype(jnp.int32))
        for t in range(tiles):
            code = codes[0, t]
            chosen[0, count + 1] = q * tiles + t
            chosen[1, count + 1] = code
            count = count + (code >= 0).astype(jnp.int32)
    chosen[0, 0] = count
    last, place = chosen[0, count], chosen[1, count]
    for extra in range(GROUP):
        chosen[0, count + 1 + extra] = last
        chosen[1, count + 1 + extra] = place
    return count


def sums_kernel(cls, parity, gathered, sums, chosen, *, tiles, width):
    sums[...] = jnp.zeros_like(sums)
    mine, near = cls[0].astype(F32), parity[0]

    def rule(q, classes, places):
        fits = (classes == mine) & (((places >> 1) & (NEAR - 1)) == near)
        return jnp.where(fits, (places >> NEAR) * 2 + (places & 1), -1)

    nodes = lax.broadcasted_iota(jnp.int32, (width, width), 0).astype(F32)
    count = choose(chosen, gathered, tiles, width, rule)

    def step(i, carry):
        for j in range(GROUP):
            at = i * GROUP + j + 1
            tile, local = chosen[0, at], chosen[1, at]
            residual, field = tile_reader(gathered, tile, tiles, width)
            rows = residual() * jnp.where(at <= count, 1.0, 0.0)
            at_a = (nodes == field(3)).astype(F32)
            at_b = (nodes == field(4)).astype(F32)
            plus = (at_a + at_b).astype(BF16)
            minus = (at_b - at_a).astype(BF16)
            vec = jnp.concatenate([(0.5 * field(c)) * rows for c in range(3)], axis=0)
            total_vec = dot_nt(stacked(vec), plus)
            total_grad = dot_nt(stacked(rows), minus)
            sums[local, 0:8, :] += total_grad[:8] + total_grad[8:]
            sums[local, 8:32, :] += total_vec[:24] + total_vec[24:]
        return carry

    lax.fori_loop(0, (count + GROUP - 1) // GROUP, step, 0)


def list_shape(gathered, tiles):
    return (2, gathered.shape[0] * tiles + 1 + GROUP)


def node_sums(cls, parity, gathered, tiles, width, places):
    return pl.pallas_call(
        functools.partial(sums_kernel, tiles=tiles, width=width),
        out_shape=held((places, 32, width)),
        in_specs=[smem_spec, smem_spec, vmem_spec],
        out_specs=vmem_spec,
        scratch_shapes=[SMEM(list_shape(gathered, tiles), jnp.int32)],
        name="node_sums",
    )(cls, parity, hold(gathered))


def list_kernel(cls, parity, gathered, chosen, *, tiles, width):
    mine = cls[0].astype(F32)

    def rule(q, classes, places):
        beside = jnp.where(parity[0] == q // (gathered.shape[0] // NEAR), mine, -1.0)
        return jnp.where(classes == beside, places, -1)

    choose(chosen, gathered, tiles, width, rule)


def class_list(cls, parity, gathered, tiles, width):
    return pl.pallas_call(
        functools.partial(list_kernel, tiles=tiles, width=width),
        out_shape=jax.ShapeDtypeStruct(list_shape(gathered, tiles), jnp.int32),
        in_specs=[smem_spec, smem_spec, vmem_spec],
        out_specs=smem_spec,
        name="class_list",
    )(cls, parity, hold(gathered))


def solve_kernel(arrived, grad, vec, out):
    count = arrived.shape[0]
    for n in range(grad.shape[0]):
        rows = arrived[0, n]
        for z in range(1, count):
            rows = rows + arrived[z, n]
        out[n, 0:8, :] = product_nt(stacked(rows[:8]), grad[n])
        out[n, 8:32, :] = product_nt(stacked(rows[8:]), vec[n])


def solve(arrived, grad, vec):
    return pl.pallas_call(
        solve_kernel,
        out_shape=held(arrived.shape[1:]),
        in_specs=[vmem_spec] * 3,
        out_specs=vmem_spec,
        name="solve",
    )(hold(arrived), hold(grad), hold(vec))


def back_kernel(chosen, gathered, values, out, *, tiles):
    out[...] = jnp.zeros_like(out)
    width = out.shape[2]

    def pick(rows, index):
        return jnp.take_along_axis(rows, index, axis=1)

    def step(i, carry):
        for j in range(GROUP):
            at = i * GROUP + j + 1
            tile, local = chosen[0, at], chosen[1, at]
            _, field = tile_reader(gathered, tile, tiles, width)
            index_a = jnp.broadcast_to(field(3).astype(jnp.int32), (8, width))
            index_b = jnp.broadcast_to(field(4).astype(jnp.int32), (8, width))
            grad = values[local, 0:8, :]
            found = pick(grad, index_b) - pick(grad, index_a)
            for c in range(3):
                rows = values[local, 8 + 8 * c : 16 + 8 * c, :]
                half = 0.5 * field(c)
                found = found + half * (pick(rows, index_a) + pick(rows, index_b))
            _, place = parts_of(tile, out.shape[0])
            out[place] = found
        return carry

    lax.fori_loop(0, (chosen[0, 0] + GROUP - 1) // GROUP, step, 0)


def back(chosen, gathered, values, tiles):
    width = values.shape[2]
    return pl.pallas_call(
        functools.partial(back_kernel, tiles=tiles),
        out_shape=held((gathered.shape[0] // NEAR * tiles, 8, width)),
        in_specs=[smem_spec, vmem_spec, vmem_spec],
        out_specs=vmem_spec,
        name="back",
    )(chosen, hold(gathered), hold(values))


def by_tile(ref, tiles, width):
    return jnp.concatenate([ref[:, t * width : (t + 1) * width] for t in range(tiles)], axis=0)


def smooth_kernel(kind, coeff, halo, residual, inverse, out, rim, work):
    tiles, _, width = out.shape
    parts = stacked(by_tile(residual, tiles, width))
    for k in range(inverse.shape[0]):
        work[k] = product_nt(parts, inverse[k]).reshape(tiles, 8, width)
    for t in range(tiles):
        out[t] = work[kind[t], t] / coeff[t]
    for h in range(rim.shape[0]):
        rim[h] = out[halo[h]]


def smooth(kind, coeff, halo, residual, inverse):
    tiles = kind.shape[0]
    kinds, width, _ = inverse.shape
    return pl.pallas_call(
        smooth_kernel,
        out_shape=(
            held((tiles, 8, width)),
            held((halo.shape[0], 8, width)),
        ),
        in_specs=[smem_spec] * 3 + [vmem_spec] * 2,
        out_specs=(vmem_spec, vmem_spec),
        scratch_shapes=[VMEM((kinds, tiles, 8, width), F32)],
        name="smooth_once",
    )(kind, coeff, halo, hold(residual), hold(inverse))


def again_kernel(
    kind, coeff, cols, kinds, coeffs, smoothed, low, high, residual, coupling, inverse, out, work, rest
):
    tiles, _, width = smoothed.shape
    sources = jnp.concatenate(
        [
            smoothed[...].reshape(tiles * 8, width),
            low[...].reshape(low.shape[0] * 8, width),
            high[...].reshape(high.shape[0] * 8, width),
        ],
        axis=0,
    )
    parts = stacked(sources)
    count = sources.shape[0] // 8
    for k in range(coupling.shape[0]):
        work[k] = product_nt(parts, coupling[k]).reshape(count, 8, width)
    for t in range(tiles):
        total = coeff[t] * work[kind[t], t]
        for m in range(cols.shape[0]):
            total = total + coeffs[m, t] * work[kinds[m, t], cols[m, t]]
        rest[t] = residual[:, t * width : (t + 1) * width] - total
    parts = stacked(rest[...].reshape(tiles * 8, width))
    for k in range(inverse.shape[0]):
        work[k, 0:tiles] = product_nt(parts, inverse[k]).reshape(tiles, 8, width)
    for t in range(tiles):
        out[t] = smoothed[t] + DAMPING * (work[kind[t], t] / coeff[t])


def smooth_again(kind, coeff, cols, kinds, coeffs, smoothed, low, high, residual, coupling, inverse):
    tiles, _, width = smoothed.shape
    count = tiles + low.shape[0] + high.shape[0]
    return pl.pallas_call(
        again_kernel,
        out_shape=held((tiles, 8, width)),
        in_specs=[smem_spec] * 5 + [vmem_spec] * 6,
        out_specs=vmem_spec,
        scratch_shapes=[
            VMEM((coupling.shape[0], count, 8, width), F32),
            VMEM((tiles, 8, width), F32),
        ],
        name="smooth_again",
    )(
        kind, coeff, cols, kinds, coeffs,
        hold(smoothed), hold(low), hold(high), hold(residual), hold(coupling), hold(inverse),
    )


def finish_kernel(smoothed, pieces, out):
    tiles, _, width = smoothed.shape
    for t in range(tiles):
        rows = pieces[0, t]
        for q in range(1, pieces.shape[0]):
            rows = rows + pieces[q, t]
        out[:, t * width : (t + 1) * width] = smoothed[t] + rows


def finish(smoothed, pieces):
    tiles, cases, width = smoothed.shape
    return pl.pallas_call(
        finish_kernel,
        out_shape=jax.ShapeDtypeStruct((cases, tiles * width), F32),
        in_specs=[vmem_spec] * 2,
        out_specs=vmem_spec,
        name="finish",
    )(hold(smoothed), hold(pieces))


TEAM = ("section", "core")
HEIGHT = ("far", "near")
TEAMS = ("near", "section", "core")


def body(
    residual,
    coupling_tiles,
    inverse_tiles,
    diag_kind,
    diag_coeff,
    tile_cols,
    tile_kinds,
    tile_coeff,
    halo_rows,
    tile_owner,
    node_slot,
    edge_nodes,
    tangents,
    grad_blocks,
    vec_blocks,
):
    far, team = lax.axis_size("far"), lax.axis_size(TEAM)
    node_tiles = grad_blocks.shape[0]
    tiles = diag_kind.shape[0]
    width = coupling_tiles.shape[1]
    cls = lax.axis_index(TEAM).astype(jnp.int32).reshape(1)
    parity = lax.axis_index("near").astype(jnp.int32).reshape(1)
    own = pack(tile_owner[:, 0], node_slot, residual, tangents, edge_nodes, far * NEAR * CORES)
    gathered = lax.all_gather(own, TEAMS)

    smoothed, rim = smooth(diag_kind, diag_coeff, halo_rows, residual, inverse_tiles)
    slabs = lax.axis_size("slab")
    low = lax.ppermute(rim, "slab", [(i, i + 1) for i in range(slabs - 1)])
    high = lax.ppermute(rim, "slab", [(i + 1, i) for i in range(slabs - 1)])

    sums = node_sums(cls, parity, gathered, tiles, width, far * node_tiles)
    sums = sums.reshape(far, node_tiles * 32, width)
    arrived = lax.all_to_all(sums, "far", split_axis=0, concat_axis=0, tiled=True)

    chosen = class_list(cls, parity, gathered, tiles, width)
    smoothed_twice = smooth_again(
        diag_kind, diag_coeff, tile_cols, tile_kinds, tile_coeff,
        smoothed, low, high, residual, coupling_tiles, inverse_tiles,
    )
    arrived, smoothed_twice, chosen = lax.optimization_barrier((arrived, smoothed_twice, chosen))

    solved = solve(arrived.reshape(far, node_tiles, 32, width), grad_blocks, vec_blocks)
    values = lax.all_gather(solved, HEIGHT, tiled=True)
    corrections = back(chosen, gathered, values, tiles).reshape(team, tiles, 8, width)
    pieces = lax.all_to_all(corrections, TEAM, split_axis=0, concat_axis=0, tiled=True)
    return finish(smoothed_twice, pieces)


def solution(mesh):
    names = ("section", "far", "near", "core", "slab")
    sections, doms, slabs = (mesh.shape[name] for name in ("section", "dom", "slab"))
    shape = (sections, doms // CORES // NEAR, NEAR, CORES, slabs)
    inner = Mesh(mesh.devices.reshape(shape), names)
    rows, cols = P(names), P(None, names)
    placed = (
        cols, P(), P(), rows, rows, cols, cols, cols, rows, rows, rows, cols, cols, rows, rows,
    )
    return jax.shard_map(
        body, mesh=inner, in_specs=placed, out_specs=cols, check_vma=False
    )
```

```python
import functools

import jax
import jax.numpy as jnp
from jax import lax
from jax.experimental import pallas as pl
from jax.experimental.pallas import tpu as pltpu
from jax.sharding import Mesh, PartitionSpec as P

DAMPING = 0.7
CORES = 2
NEAR = 2
GROUP = 16
F32 = jnp.float32
BF16 = jnp.bfloat16
SMEM = pltpu.SMEM
VMEM = pltpu.VMEM

vmem_spec = pl.BlockSpec(memory_space=VMEM)
smem_spec = pl.BlockSpec(memory_space=SMEM)
any_spec = pl.BlockSpec(memory_space=pl.ANY)


def held(shape):
    return pltpu.VMEM(shape, F32)


def hold(x):
    return pltpu.with_memory_space_constraint(x, VMEM)


def split(x):
    high = x.astype(BF16)
    low = (x - high.astype(F32)).astype(BF16)
    return high, low


def dot_nt(a, b):
    return lax.dot_general(a, b, (((1,), (1,)), ((), ())), preferred_element_type=F32)


def product_nt(parts, matrix):
    count = parts.shape[0] // 2
    high, low = split(matrix)
    both = dot_nt(parts, high)
    return both[:count] + both[count:] + dot_nt(parts[:count], low)


def stacked(rows):
    high, low = split(rows)
    return jnp.concatenate([high, low], axis=0)


def parts_of(x, size):
    if size & (size - 1) == 0:
        return lax.shift_right_logical(x, jnp.int32(size.bit_length() - 1)), x & (size - 1)
    return x // size, x % size


FIELDS = 5


def pack_kernel(owner, slot, residual, tangents, ends, out, *, doms):
    tiles = owner.shape[0]
    width = residual.shape[1] // tiles
    lanes = lax.broadcasted_iota(jnp.int32, (1, width), 1)
    owners = jnp.zeros((1, width), jnp.int32)
    slots = jnp.zeros((1, width), jnp.int32)
    for t in range(tiles):
        owners = jnp.where(lanes == t, owner[t], owners)
        slots = jnp.where(lanes == t, slot[t], slots)
    section, dom = parts_of(owners, doms)
    z, core = parts_of(dom, CORES)
    out[:, 0 : tiles * width] = residual[...]
    for t in range(tiles):
        part = slice(t * width, (t + 1) * width)
        for f in range(FIELDS):
            row = tangents[f : f + 1, part] if f < 3 else ends[f - 3 : f - 2, part].astype(F32)
            at = (tiles + (t // 8) * FIELDS + f) * width
            out[t % 8 : t % 8 + 1, at : at + width] = row
    at = (tiles + tiles // 8 * FIELDS) * width
    out[:, at : at + width] = jnp.zeros((8, width), F32)
    out[0:1, at : at + width] = (section * CORES + core).astype(F32)
    out[1:2, at : at + width] = (z * 2 + slots).astype(F32)


def pack(owner, slot, residual, tangents, ends, doms):
    tiles = owner.shape[0]
    width = residual.shape[1] // tiles
    return pl.pallas_call(
        functools.partial(pack_kernel, doms=doms),
        out_shape=held((8, (tiles + tiles // 8 * FIELDS + 1) * width)),
        in_specs=[smem_spec, smem_spec, vmem_spec, vmem_spec, vmem_spec],
        out_specs=vmem_spec,
        name="pack",
    )(owner, slot, residual, tangents, ends)


def tile_reader(gathered, tile, tiles, width):
    device, t = parts_of(tile, tiles)
    block, row = parts_of(t, 8)
    base = tiles + block * FIELDS

    def lanes(at):
        return pl.ds(pl.multiple_of(at * width, width), width)

    return (
        lambda: gathered[device, :, lanes(t)],
        lambda f: pltpu.roll(gathered[device, :, lanes(base + f)], 8 - row, 0)[0:1],
    )


def choose(chosen, gathered, tiles, width, rule):
    count = jnp.int32(0)
    for q in range(gathered.shape[0]):
        block = gathered[q, :, gathered.shape[2] - width :]
        codes = rule(q, block[0:1], block[1:2].astype(jnp.int32))
        for t in range(tiles):
            code = codes[0, t]
            chosen[0, count + 1] = q * tiles + t
            chosen[1, count + 1] = code
            count = count + (code >= 0).astype(jnp.int32)
    chosen[0, 0] = count
    last, place = chosen[0, count], chosen[1, count]
    for extra in range(GROUP):
        chosen[0, count + 1 + extra] = last
        chosen[1, count + 1 + extra] = place
    return count


def sums_kernel(cls, parity, gathered, sums, chosen, *, tiles, width):
    sums[...] = jnp.zeros_like(sums)
    mine, near = cls[0].astype(F32), parity[0]

    def rule(q, classes, places):
        fits = (classes == mine) & (((places >> 1) & (NEAR - 1)) == near)
        return jnp.where(fits, (places >> NEAR) * 2 + (places & 1), -1)

    nodes = lax.broadcasted_iota(jnp.int32, (width, width), 0).astype(F32)
    count = choose(chosen, gathered, tiles, width, rule)

    def step(i, carry):
        for j in range(GROUP):
            at = i * GROUP + j + 1
            tile, local = chosen[0, at], chosen[1, at]
            residual, field = tile_reader(gathered, tile, tiles, width)
            rows = residual() * jnp.where(at <= count, 1.0, 0.0)
            at_a = (nodes == field(3)).astype(F32)
            at_b = (nodes == field(4)).astype(F32)
            plus = (at_a + at_b).astype(BF16)
            minus = (at_b - at_a).astype(BF16)
            vec = jnp.concatenate([(0.5 * field(c)) * rows for c in range(3)], axis=0)
            total_vec = dot_nt(stacked(vec), plus)
            total_grad = dot_nt(stacked(rows), minus)
            sums[local, 0:8, :] += total_grad[:8] + total_grad[8:]
            sums[local, 8:32, :] += total_vec[:24] + total_vec[24:]
        return carry

    lax.fori_loop(0, (count + GROUP - 1) // GROUP, step, 0)


def list_shape(gathered, tiles):
    return (2, gathered.shape[0] * tiles + 1 + GROUP)


def node_sums(cls, parity, gathered, tiles, width, places):
    return pl.pallas_call(
        functools.partial(sums_kernel, tiles=tiles, width=width),
        out_shape=held((places, 32, width)),
        in_specs=[smem_spec, smem_spec, vmem_spec],
        out_specs=vmem_spec,
        scratch_shapes=[SMEM(list_shape(gathered, tiles), jnp.int32)],
        name="node_sums",
    )(cls, parity, hold(gathered))


def list_kernel(cls, parity, gathered, chosen, *, tiles, width):
    mine = cls[0].astype(F32)

    def rule(q, classes, places):
        beside = jnp.where(parity[0] == q // (gathered.shape[0] // NEAR), mine, -1.0)
        return jnp.where(classes == beside, places, -1)

    choose(chosen, gathered, tiles, width, rule)


def class_list(cls, parity, gathered, tiles, width):
    return pl.pallas_call(
        functools.partial(list_kernel, tiles=tiles, width=width),
        out_shape=jax.ShapeDtypeStruct(list_shape(gathered, tiles), jnp.int32),
        in_specs=[smem_spec, smem_spec, vmem_spec],
        out_specs=smem_spec,
        name="class_list",
    )(cls, parity, hold(gathered))


def solve_kernel(arrived, grad, vec, out):
    count = arrived.shape[0]
    for n in range(grad.shape[0]):
        rows = arrived[0, n]
        for z in range(1, count):
            rows = rows + arrived[z, n]
        out[n, 0:8, :] = product_nt(stacked(rows[:8]), grad[n])
        out[n, 8:32, :] = product_nt(stacked(rows[8:]), vec[n])


def solve(arrived, grad, vec):
    return pl.pallas_call(
        solve_kernel,
        out_shape=held(arrived.shape[1:]),
        in_specs=[vmem_spec] * 3,
        out_specs=vmem_spec,
        name="solve",
    )(hold(arrived), hold(grad), hold(vec))


def back_kernel(chosen, gathered, values, out, *, tiles):
    out[...] = jnp.zeros_like(out)
    width = out.shape[2]

    def pick(rows, index):
        return jnp.take_along_axis(rows, index, axis=1)

    def step(i, carry):
        for j in range(GROUP):
            at = i * GROUP + j + 1
            tile, local = chosen[0, at], chosen[1, at]
            _, field = tile_reader(gathered, tile, tiles, width)
            index_a = jnp.broadcast_to(field(3).astype(jnp.int32), (8, width))
            index_b = jnp.broadcast_to(field(4).astype(jnp.int32), (8, width))
            grad = values[local, 0:8, :]
            found = pick(grad, index_b) - pick(grad, index_a)
            for c in range(3):
                rows = values[local, 8 + 8 * c : 16 + 8 * c, :]
                half = 0.5 * field(c)
                found = found + half * (pick(rows, index_a) + pick(rows, index_b))
            _, place = parts_of(tile, out.shape[0])
            out[place] = found
        return carry

    lax.fori_loop(0, (chosen[0, 0] + GROUP - 1) // GROUP, step, 0)


def back(chosen, gathered, values, tiles):
    width = values.shape[2]
    return pl.pallas_call(
        functools.partial(back_kernel, tiles=tiles),
        out_shape=held((gathered.shape[0] // NEAR * tiles, 8, width)),
        in_specs=[smem_spec, vmem_spec, vmem_spec],
        out_specs=vmem_spec,
        name="back",
    )(chosen, hold(gathered), hold(values))


def by_tile(ref, tiles, width):
    return jnp.concatenate([ref[:, t * width : (t + 1) * width] for t in range(tiles)], axis=0)


def smooth_kernel(kind, coeff, halo, residual, inverse, out, rim, work):
    tiles, _, width = out.shape
    parts = stacked(by_tile(residual, tiles, width))
    for k in range(inverse.shape[0]):
        work[k] = product_nt(parts, inverse[k]).reshape(tiles, 8, width)
    for t in range(tiles):
        out[t] = work[kind[t], t] / coeff[t]
    for h in range(rim.shape[0]):
        rim[h] = out[halo[h]]


def smooth(kind, coeff, halo, residual, inverse):
    tiles = kind.shape[0]
    kinds, width, _ = inverse.shape
    return pl.pallas_call(
        smooth_kernel,
        out_shape=(
            held((tiles, 8, width)),
            held((halo.shape[0], 8, width)),
        ),
        in_specs=[smem_spec] * 3 + [vmem_spec] * 2,
        out_specs=(vmem_spec, vmem_spec),
        scratch_shapes=[VMEM((kinds, tiles, 8, width), F32)],
        name="smooth_once",
    )(kind, coeff, halo, hold(residual), hold(inverse))


def again_kernel(
    kind, coeff, cols, kinds, coeffs, smoothed, low, high, residual, coupling, inverse, out, work, rest
):
    tiles, _, width = smoothed.shape
    sources = jnp.concatenate(
        [
            smoothed[...].reshape(tiles * 8, width),
            low[...].reshape(low.shape[0] * 8, width),
            high[...].reshape(high.shape[0] * 8, width),
        ],
        axis=0,
    )
    parts = stacked(sources)
    count = sources.shape[0] // 8
    for k in range(coupling.shape[0]):
        work[k] = product_nt(parts, coupling[k]).reshape(count, 8, width)
    for t in range(tiles):
        total = coeff[t] * work[kind[t], t]
        for m in range(cols.shape[0]):
            total = total + coeffs[m, t] * work[kinds[m, t], cols[m, t]]
        rest[t] = residual[:, t * width : (t + 1) * width] - total
    parts = stacked(rest[...].reshape(tiles * 8, width))
    for k in range(inverse.shape[0]):
        work[k, 0:tiles] = product_nt(parts, inverse[k]).reshape(tiles, 8, width)
    for t in range(tiles):
        out[t] = smoothed[t] + DAMPING * (work[kind[t], t] / coeff[t])


def smooth_again(kind, coeff, cols, kinds, coeffs, smoothed, low, high, residual, coupling, inverse):
    tiles, _, width = smoothed.shape
    count = tiles + low.shape[0] + high.shape[0]
    return pl.pallas_call(
        again_kernel,
        out_shape=held((tiles, 8, width)),
        in_specs=[smem_spec] * 5 + [vmem_spec] * 6,
        out_specs=vmem_spec,
        scratch_shapes=[
            VMEM((coupling.shape[0], count, 8, width), F32),
            VMEM((tiles, 8, width), F32),
        ],
        name="smooth_again",
    )(
        kind, coeff, cols, kinds, coeffs,
        hold(smoothed), hold(low), hold(high), hold(residual), hold(coupling), hold(inverse),
    )


def finish_kernel(smoothed, pieces, out):
    tiles, _, width = smoothed.shape
    for t in range(tiles):
        rows = pieces[0, t]
        for q in range(1, pieces.shape[0]):
            rows = rows + pieces[q, t]
        out[:, t * width : (t + 1) * width] = smoothed[t] + rows


def finish(smoothed, pieces):
    tiles, cases, width = smoothed.shape
    return pl.pallas_call(
        finish_kernel,
        out_shape=jax.ShapeDtypeStruct((cases, tiles * width), F32),
        in_specs=[vmem_spec] * 2,
        out_specs=vmem_spec,
        name="finish",
    )(hold(smoothed), hold(pieces))


TEAM = ("section", "core")
HEIGHT = ("far", "near")
TEAMS = ("near", "section", "core")


def body(
    residual,
    coupling_tiles,
    inverse_tiles,
    diag_kind,
    diag_coeff,
    tile_cols,
    tile_kinds,
    tile_coeff,
    halo_rows,
    tile_owner,
    node_slot,
    edge_nodes,
    tangents,
    grad_blocks,
    vec_blocks,
):
    far, team = lax.axis_size("far"), lax.axis_size(TEAM)
    node_tiles = grad_blocks.shape[0]
    tiles = diag_kind.shape[0]
    width = coupling_tiles.shape[1]
    cls = lax.axis_index(TEAM).astype(jnp.int32).reshape(1)
    parity = lax.axis_index("near").astype(jnp.int32).reshape(1)
    own = pack(tile_owner[:, 0], node_slot, residual, tangents, edge_nodes, far * NEAR * CORES)
    gathered = lax.all_gather(own, TEAMS)

    smoothed, rim = smooth(diag_kind, diag_coeff, halo_rows, residual, inverse_tiles)
    slabs = lax.axis_size("slab")
    low = lax.ppermute(rim, "slab", [(i, i + 1) for i in range(slabs - 1)])
    high = lax.ppermute(rim, "slab", [(i + 1, i) for i in range(slabs - 1)])

    sums = node_sums(cls, parity, gathered, tiles, width, far * node_tiles)
    sums = sums.reshape(far, node_tiles * 32, width)
    arrived = lax.all_to_all(sums, "far", split_axis=0, concat_axis=0, tiled=True)

    chosen = class_list(cls, parity, gathered, tiles, width)
    smoothed_twice = smooth_again(
        diag_kind, diag_coeff, tile_cols, tile_kinds, tile_coeff,
        smoothed, low, high, residual, coupling_tiles, inverse_tiles,
    )
    arrived, smoothed_twice, chosen = lax.optimization_barrier((arrived, smoothed_twice, chosen))

    solved = solve(arrived.reshape(far, node_tiles, 32, width), grad_blocks, vec_blocks)
    values = lax.all_gather(solved, HEIGHT, tiled=True)
    corrections = back(chosen, gathered, values, tiles).reshape(team, tiles, 8, width)
    pieces = lax.all_to_all(corrections, TEAM, split_axis=0, concat_axis=0, tiled=True)
    return finish(smoothed_twice, pieces)


def solution(mesh):
    names = ("section", "far", "near", "core", "slab")
    sections, doms, slabs = (mesh.shape[name] for name in ("section", "dom", "slab"))
    shape = (sections, doms // CORES // NEAR, NEAR, CORES, slabs)
    inner = Mesh(mesh.devices.reshape(shape), names)
    rows, cols = P(names), P(None, names)
    placed = (
        cols, P(), P(), rows, rows, cols, cols, cols, rows, rows, rows, cols, cols, rows, rows,
    )
    return jax.shard_map(
        body, mesh=inner, in_specs=placed, out_specs=cols, check_vma=False
    )
```

```python
import functools

import jax
import jax.numpy as jnp
from jax import lax
from jax.experimental import pallas as pl
from jax.experimental.pallas import tpu as pltpu
from jax.sharding import Mesh, PartitionSpec as P

DAMPING = 0.7
CORES = 2
NEAR = 2
GROUP = 12
F32 = jnp.float32
BF16 = jnp.bfloat16
SMEM = pltpu.SMEM
VMEM = pltpu.VMEM

vmem_spec = pl.BlockSpec(memory_space=VMEM)
smem_spec = pl.BlockSpec(memory_space=SMEM)
any_spec = pl.BlockSpec(memory_space=pl.ANY)


def held(shape):
    return pltpu.VMEM(shape, F32)


def hold(x):
    return pltpu.with_memory_space_constraint(x, VMEM)


def split(x):
    high = x.astype(BF16)
    low = (x - high.astype(F32)).astype(BF16)
    return high, low


def dot_nt(a, b):
    return lax.dot_general(a, b, (((1,), (1,)), ((), ())), preferred_element_type=F32)


def product_nt(parts, matrix):
    count = parts.shape[0] // 2
    high, low = split(matrix)
    both = dot_nt(parts, high)
    return both[:count] + both[count:] + dot_nt(parts[:count], low)


def stacked(rows):
    high, low = split(rows)
    return jnp.concatenate([high, low], axis=0)


def parts_of(x, size):
    if size & (size - 1) == 0:
        return lax.shift_right_logical(x, jnp.int32(size.bit_length() - 1)), x & (size - 1)
    return x // size, x % size


FIELDS = 5


def pack_kernel(owner, slot, residual, tangents, ends, out, *, doms):
    tiles = owner.shape[0]
    width = residual.shape[1] // tiles
    lanes = lax.broadcasted_iota(jnp.int32, (1, width), 1)
    owners = jnp.zeros((1, width), jnp.int32)
    slots = jnp.zeros((1, width), jnp.int32)
    for t in range(tiles):
        owners = jnp.where(lanes == t, owner[t], owners)
        slots = jnp.where(lanes == t, slot[t], slots)
    section, dom = parts_of(owners, doms)
    z, core = parts_of(dom, CORES)
    out[:, 0 : tiles * width] = residual[...]
    for t in range(tiles):
        part = slice(t * width, (t + 1) * width)
        for f in range(FIELDS):
            row = tangents[f : f + 1, part] if f < 3 else ends[f - 3 : f - 2, part].astype(F32)
            at = (tiles + (t // 8) * FIELDS + f) * width
            out[t % 8 : t % 8 + 1, at : at + width] = row
    at = (tiles + tiles // 8 * FIELDS) * width
    out[:, at : at + width] = jnp.zeros((8, width), F32)
    out[0:1, at : at + width] = (section * CORES + core).astype(F32)
    out[1:2, at : at + width] = (z * 2 + slots).astype(F32)


def pack(owner, slot, residual, tangents, ends, doms):
    tiles = owner.shape[0]
    width = residual.shape[1] // tiles
    return pl.pallas_call(
        functools.partial(pack_kernel, doms=doms),
        out_shape=held((8, (tiles + tiles // 8 * FIELDS + 1) * width)),
        in_specs=[smem_spec, smem_spec, vmem_spec, vmem_spec, vmem_spec],
        out_specs=vmem_spec,
        name="pack",
    )(owner, slot, residual, tangents, ends)


def tile_reader(gathered, tile, tiles, width):
    device, t = parts_of(tile, tiles)
    block, row = parts_of(t, 8)
    base = tiles + block * FIELDS

    def lanes(at):
        return pl.ds(pl.multiple_of(at * width, width), width)

    return (
        lambda: gathered[device, :, lanes(t)],
        lambda f: pltpu.roll(gathered[device, :, lanes(base + f)], 8 - row, 0)[0:1],
    )


def choose(chosen, gathered, tiles, width, rule):
    count = jnp.int32(0)
    for q in range(gathered.shape[0]):
        block = gathered[q, :, gathered.shape[2] - width :]
        codes = rule(q, block[0:1], block[1:2].astype(jnp.int32))
        for t in range(tiles):
            code = codes[0, t]
            chosen[0, count + 1] = q * tiles + t
            chosen[1, count + 1] = code
            count = count + (code >= 0).astype(jnp.int32)
    chosen[0, 0] = count
    last, place = chosen[0, count], chosen[1, count]
    for extra in range(GROUP):
        chosen[0, count + 1 + extra] = last
        chosen[1, count + 1 + extra] = place
    return count


def sums_kernel(cls, parity, gathered, sums, chosen, *, tiles, width):
    sums[...] = jnp.zeros_like(sums)
    mine, near = cls[0].astype(F32), parity[0]

    def rule(q, classes, places):
        fits = (classes == mine) & (((places >> 1) & (NEAR - 1)) == near)
        return jnp.where(fits, (places >> NEAR) * 2 + (places & 1), -1)

    nodes = lax.broadcasted_iota(jnp.int32, (width, width), 0).astype(F32)
    count = choose(chosen, gathered, tiles, width, rule)

    def step(i, carry):
        for j in range(GROUP):
            at = i * GROUP + j + 1
            tile, local = chosen[0, at], chosen[1, at]
            residual, field = tile_reader(gathered, tile, tiles, width)
            rows = residual() * jnp.where(at <= count, 1.0, 0.0)
            at_a = (nodes == field(3)).astype(F32)
            at_b = (nodes == field(4)).astype(F32)
            plus = (at_a + at_b).astype(BF16)
            minus = (at_b - at_a).astype(BF16)
            vec = jnp.concatenate([(0.5 * field(c)) * rows for c in range(3)], axis=0)
            total_vec = dot_nt(stacked(vec), plus)
            total_grad = dot_nt(stacked(rows), minus)
            sums[local, 0:8, :] += total_grad[:8] + total_grad[8:]
            sums[local, 8:32, :] += total_vec[:24] + total_vec[24:]
        return carry

    lax.fori_loop(0, (count + GROUP - 1) // GROUP, step, 0)


def list_shape(gathered, tiles):
    return (2, gathered.shape[0] * tiles + 1 + GROUP)


def node_sums(cls, parity, gathered, tiles, width, places):
    return pl.pallas_call(
        functools.partial(sums_kernel, tiles=tiles, width=width),
        out_shape=held((places, 32, width)),
        in_specs=[smem_spec, smem_spec, vmem_spec],
        out_specs=vmem_spec,
        scratch_shapes=[SMEM(list_shape(gathered, tiles), jnp.int32)],
        name="node_sums",
    )(cls, parity, hold(gathered))


def list_kernel(cls, parity, gathered, chosen, *, tiles, width):
    mine = cls[0].astype(F32)

    def rule(q, classes, places):
        beside = jnp.where(parity[0] == q // (gathered.shape[0] // NEAR), mine, -1.0)
        return jnp.where(classes == beside, places, -1)

    choose(chosen, gathered, tiles, width, rule)


def class_list(cls, parity, gathered, tiles, width):
    return pl.pallas_call(
        functools.partial(list_kernel, tiles=tiles, width=width),
        out_shape=jax.ShapeDtypeStruct(list_shape(gathered, tiles), jnp.int32),
        in_specs=[smem_spec, smem_spec, vmem_spec],
        out_specs=smem_spec,
        name="class_list",
    )(cls, parity, hold(gathered))


def solve_kernel(arrived, grad, vec, out):
    count = arrived.shape[0]
    for n in range(grad.shape[0]):
        rows = arrived[0, n]
        for z in range(1, count):
            rows = rows + arrived[z, n]
        out[n, 0:8, :] = product_nt(stacked(rows[:8]), grad[n])
        out[n, 8:32, :] = product_nt(stacked(rows[8:]), vec[n])


def solve(arrived, grad, vec):
    return pl.pallas_call(
        solve_kernel,
        out_shape=held(arrived.shape[1:]),
        in_specs=[vmem_spec] * 3,
        out_specs=vmem_spec,
        name="solve",
    )(hold(arrived), hold(grad), hold(vec))


def back_kernel(chosen, gathered, values, out, *, tiles):
    out[...] = jnp.zeros_like(out)
    width = out.shape[2]

    def pick(rows, index):
        return jnp.take_along_axis(rows, index, axis=1)

    def step(i, carry):
        for j in range(GROUP):
            at = i * GROUP + j + 1
            tile, local = chosen[0, at], chosen[1, at]
            _, field = tile_reader(gathered, tile, tiles, width)
            index_a = jnp.broadcast_to(field(3).astype(jnp.int32), (8, width))
            index_b = jnp.broadcast_to(field(4).astype(jnp.int32), (8, width))
            grad = values[local, 0:8, :]
            found = pick(grad, index_b) - pick(grad, index_a)
            for c in range(3):
                rows = values[local, 8 + 8 * c : 16 + 8 * c, :]
                half = 0.5 * field(c)
                found = found + half * (pick(rows, index_a) + pick(rows, index_b))
            _, place = parts_of(tile, out.shape[0])
            out[place] = found
        return carry

    lax.fori_loop(0, (chosen[0, 0] + GROUP - 1) // GROUP, step, 0)


def back(chosen, gathered, values, tiles):
    width = values.shape[2]
    return pl.pallas_call(
        functools.partial(back_kernel, tiles=tiles),
        out_shape=held((gathered.shape[0] // NEAR * tiles, 8, width)),
        in_specs=[smem_spec, vmem_spec, vmem_spec],
        out_specs=vmem_spec,
        name="back",
    )(chosen, hold(gathered), hold(values))


def by_tile(ref, tiles, width):
    return jnp.concatenate([ref[:, t * width : (t + 1) * width] for t in range(tiles)], axis=0)


def smooth_kernel(kind, coeff, halo, residual, inverse, out, rim, work):
    tiles, _, width = out.shape
    parts = stacked(by_tile(residual, tiles, width))
    for k in range(inverse.shape[0]):
        work[k] = product_nt(parts, inverse[k]).reshape(tiles, 8, width)
    for t in range(tiles):
        out[t] = work[kind[t], t] / coeff[t]
    for h in range(rim.shape[0]):
        rim[h] = out[halo[h]]


def smooth(kind, coeff, halo, residual, inverse):
    tiles = kind.shape[0]
    kinds, width, _ = inverse.shape
    return pl.pallas_call(
        smooth_kernel,
        out_shape=(
            held((tiles, 8, width)),
            held((halo.shape[0], 8, width)),
        ),
        in_specs=[smem_spec] * 3 + [vmem_spec] * 2,
        out_specs=(vmem_spec, vmem_spec),
        scratch_shapes=[VMEM((kinds, tiles, 8, width), F32)],
        name="smooth_once",
    )(kind, coeff, halo, hold(residual), hold(inverse))


def again_kernel(
    kind, coeff, cols, kinds, coeffs, smoothed, low, high, residual, coupling, inverse, out, work, rest
):
    tiles, _, width = smoothed.shape
    sources = jnp.concatenate(
        [
            smoothed[...].reshape(tiles * 8, width),
            low[...].reshape(low.shape[0] * 8, width),
            high[...].reshape(high.shape[0] * 8, width),
        ],
        axis=0,
    )
    parts = stacked(sources)
    count = sources.shape[0] // 8
    for k in range(coupling.shape[0]):
        work[k] = product_nt(parts, coupling[k]).reshape(count, 8, width)
    for t in range(tiles):
        total = coeff[t] * work[kind[t], t]
        for m in range(cols.shape[0]):
            total = total + coeffs[m, t] * work[kinds[m, t], cols[m, t]]
        rest[t] = residual[:, t * width : (t + 1) * width] - total
    parts = stacked(rest[...].reshape(tiles * 8, width))
    for k in range(inverse.shape[0]):
        work[k, 0:tiles] = product_nt(parts, inverse[k]).reshape(tiles, 8, width)
    for t in range(tiles):
        out[t] = smoothed[t] + DAMPING * (work[kind[t], t] / coeff[t])


def smooth_again(kind, coeff, cols, kinds, coeffs, smoothed, low, high, residual, coupling, inverse):
    tiles, _, width = smoothed.shape
    count = tiles + low.shape[0] + high.shape[0]
    return pl.pallas_call(
        again_kernel,
        out_shape=held((tiles, 8, width)),
        in_specs=[smem_spec] * 5 + [vmem_spec] * 6,
        out_specs=vmem_spec,
        scratch_shapes=[
            VMEM((coupling.shape[0], count, 8, width), F32),
            VMEM((tiles, 8, width), F32),
        ],
        name="smooth_again",
    )(
        kind, coeff, cols, kinds, coeffs,
        hold(smoothed), hold(low), hold(high), hold(residual), hold(coupling), hold(inverse),
    )


def finish_kernel(smoothed, pieces, out):
    tiles, _, width = smoothed.shape
    for t in range(tiles):
        rows = pieces[0, t]
        for q in range(1, pieces.shape[0]):
            rows = rows + pieces[q, t]
        out[:, t * width : (t + 1) * width] = smoothed[t] + rows


def finish(smoothed, pieces):
    tiles, cases, width = smoothed.shape
    return pl.pallas_call(
        finish_kernel,
        out_shape=jax.ShapeDtypeStruct((cases, tiles * width), F32),
        in_specs=[vmem_spec] * 2,
        out_specs=vmem_spec,
        name="finish",
    )(hold(smoothed), hold(pieces))


TEAM = ("section", "core")
HEIGHT = ("far", "near")
TEAMS = ("near", "section", "core")


def body(
    residual,
    coupling_tiles,
    inverse_tiles,
    diag_kind,
    diag_coeff,
    tile_cols,
    tile_kinds,
    tile_coeff,
    halo_rows,
    tile_owner,
    node_slot,
    edge_nodes,
    tangents,
    grad_blocks,
    vec_blocks,
):
    far, team = lax.axis_size("far"), lax.axis_size(TEAM)
    node_tiles = grad_blocks.shape[0]
    tiles = diag_kind.shape[0]
    width = coupling_tiles.shape[1]
    cls = lax.axis_index(TEAM).astype(jnp.int32).reshape(1)
    parity = lax.axis_index("near").astype(jnp.int32).reshape(1)
    own = pack(tile_owner[:, 0], node_slot, residual, tangents, edge_nodes, far * NEAR * CORES)
    gathered = lax.all_gather(own, TEAMS)

    smoothed, rim = smooth(diag_kind, diag_coeff, halo_rows, residual, inverse_tiles)
    slabs = lax.axis_size("slab")
    low = lax.ppermute(rim, "slab", [(i, i + 1) for i in range(slabs - 1)])
    high = lax.ppermute(rim, "slab", [(i + 1, i) for i in range(slabs - 1)])

    sums = node_sums(cls, parity, gathered, tiles, width, far * node_tiles)
    sums = sums.reshape(far, node_tiles * 32, width)
    arrived = lax.all_to_all(sums, "far", split_axis=0, concat_axis=0, tiled=True)

    chosen = class_list(cls, parity, gathered, tiles, width)
    smoothed_twice = smooth_again(
        diag_kind, diag_coeff, tile_cols, tile_kinds, tile_coeff,
        smoothed, low, high, residual, coupling_tiles, inverse_tiles,
    )
    arrived, smoothed_twice, chosen = lax.optimization_barrier((arrived, smoothed_twice, chosen))

    solved = solve(arrived.reshape(far, node_tiles, 32, width), grad_blocks, vec_blocks)
    values = lax.all_gather(solved, HEIGHT, tiled=True)
    corrections = back(chosen, gathered, values, tiles).reshape(team, tiles, 8, width)
    pieces = lax.all_to_all(corrections, TEAM, split_axis=0, concat_axis=0, tiled=True)
    return finish(smoothed_twice, pieces)


def solution(mesh):
    names = ("section", "far", "near", "core", "slab")
    sections, doms, slabs = (mesh.shape[name] for name in ("section", "dom", "slab"))
    shape = (sections, doms // CORES // NEAR, NEAR, CORES, slabs)
    inner = Mesh(mesh.devices.reshape(shape), names)
    rows, cols = P(names), P(None, names)
    placed = (
        cols, P(), P(), rows, rows, cols, cols, cols, rows, rows, rows, cols, cols, rows, rows,
    )
    return jax.shard_map(
        body, mesh=inner, in_specs=placed, out_specs=cols, check_vma=False
    )
```
